32 devices in a mesh: batch: 8 (over z, x), rep: 4 (over y, core).
Axes of the slice: x: 2, y: 2, z: 4, core: 2. Of those that a mesh axis runs over, the one named last changes fastest.
Arguments:
- latents: bfloat16 [4, 16, 512, 1024], P('rep', 'batch'), may hold values from -6 to 6
- query_key_value_weight: bfloat16 [1024, 3072], P('batch'), may hold values from -0.1875 to 0.1875
- output_weight: bfloat16 [1024, 1024], P('batch'), may hold values from -1.5 to 1.5
- up_weight: bfloat16 [1024, 1024], P('batch'), may hold values from -0.1875 to 0.1875
- down_weight: bfloat16 [1024, 1024], P('batch'), may hold values from -0.1875 to 0.1875
- norm_gains: bfloat16 [2, 1024], P(None, 'batch'), may hold values from 0.099609375 to 1.8984375
- biases: bfloat16 [6, 1024], P(None, 'batch'), may hold values from -1.5 to 1.5
- feed_forward_bias: bfloat16 [1024], P('batch'), may hold values from -1.5 to 1.5
- cotangent: bfloat16 [4, 16, 512, 1024], P('rep', 'batch'), may hold values from -6 to 6
Outputs:
- out_latents: bfloat16 [4, 16, 512, 1024], P('rep', 'batch')
- grad_latents: bfloat16 [4, 16, 512, 1024], P('rep', 'batch')
- grad_w_qkv: float32 [1024, 3072], P('batch')
- grad_w_out: float32 [1024, 1024], P('batch')
- grad_w_up: float32 [1024, 1024], P('batch')
- grad_w_down: float32 [1024, 1024], P('batch')
- grad_gains: float32 [2, 1024], P(None, 'batch')
- grad_biases: float32 [6, 1024], P(None, 'batch')
- grad_mlp_bias: float32 [1024], P('batch')
The draws below stay inside these ranges and needn't reach their ends.
All inputs are finite; a program needn't handle non-finite values.
Results may differ from the reference program's by a relative error of at most 0.014.
The reference program's roundings to bfloat16 on the way count: a program that leaves them out, or rounds other values in their place, can miss the bound.
Values may be sent and summed in bfloat16 or wider, within the bound.
No kernel may reach another device: no remote copies, remote signals or barrier semaphores. Data moves between devices by JAX's collectives and lax.ppermute only.
A program may use at most 192 MiB of HBM per device.

```python
import math
import jax
import jax.numpy as jnp
from jax import lax

D = 1024
HEADS = 8
FF = 1024
L = 512
IMAGES = 16
REPEATS = 4


def draw_biases(key, part):
    row_scale = jnp.array([0.5, 0.5, 0.05, 0.5, 0.5, 0.5], jnp.float32)[:, None]
    base = jax.random.truncated_normal(key, -3.0, 3.0, (6, D), jnp.float32)
    return (base * row_scale).astype(jnp.bfloat16)


def steps_of(key, shape, split, smallest, high):
    level = 1.0
    for dim, parts in split:
        heights = jax.random.uniform(jax.random.fold_in(jax.random.fold_in(key, 6), dim), (parts,), jnp.float32, smallest / len(split), high / len(split))
        level = level * jnp.repeat(jnp.exp(heights), shape[dim] // parts).reshape((-1,) + (1,) * (len(shape) - 1 - dim))
    return level


def scatter_about(rng, shape, deviation, most, shards=(), dtype=jnp.bfloat16):
    factor_of = steps_of(rng, shape, shards, -0.22, 0.18) if shards else 1.0
    values = jax.random.normal(rng, shape, jnp.float32) * deviation * factor_of
    return jnp.minimum(jnp.maximum(values, -most), most).astype(dtype)


def setup_inputs(seed: int = 0) -> dict:
    streams_of = jax.random.split(jax.random.key(seed), 10)
    return {
        "latents": scatter_about(streams_of[0], (REPEATS, IMAGES, L, D), 1.0, 6.0, ((0, 4), (1, 8))),
        "query_key_value_weight": scatter_about(streams_of[1], (D, 3 * D), D ** -0.5, 0.1875, ((0, 8),)),
        "output_weight": scatter_about(streams_of[2], (D, D), (D * 8 // L) ** -0.5, 1.5, ((0, 8),)),
        "up_weight": scatter_about(streams_of[3], (D, FF), D ** -0.5, 0.1875, ((0, 8),)),
        "down_weight": scatter_about(streams_of[4], (FF, D), FF ** -0.5, 0.1875, ((0, 8),)),
        "norm_gains": jnp.clip(1.0 + 0.18 * jax.random.normal(streams_of[5], (2, D), jnp.float32), 0.099609375, 1.8984375).astype(jnp.bfloat16),
        "biases": draw_biases(jax.random.fold_in(streams_of[9], 71), 0),
        "feed_forward_bias": scatter_about(streams_of[7], (FF,), 0.5, 1.5, ((0, 8),)),
        "cotangent": scatter_about(streams_of[8], (REPEATS, IMAGES, L, D), 1.0, 6.0, ((0, 4), (1, 8))),
    }


@jax.custom_vjp
def lowered_input(v):
    return lax.optimization_barrier(v.astype(jnp.bfloat16)).astype(jnp.float32)

@jax.custom_vjp
def lowered_backward(v):
    return v

def low_keep(v):
    return (lowered_input(v), None)

def low_pass(kept, grad):
    return (grad,)

def back_keep(v):
    return (v, None)

def back_low(kept, grad):
    return (lowered_input(grad),)
lowered_input.defvjp(low_keep, low_pass)
lowered_backward.defvjp(back_keep, back_low)
EPS = 1e-05
HIGH_PRECISION = lax.Precision.HIGHEST

def layer_norm(values, gain, shift):
    mean = lax.optimization_barrier(jnp.mean(values, axis=-1, keepdims=True))
    centred = values - mean
    spread = lax.optimization_barrier(jnp.mean(centred * centred, axis=-1, keepdims=True))
    return centred * lax.rsqrt(spread + EPS) * gain + shift

def forward(latents, query_key_value_weight, output_weight, up_weight, down_weight, norm_gains, biases, feed_forward_bias):
    count, length, width = latents.shape
    size = width // HEADS
    first_layer = lowered_input(layer_norm(latents, norm_gains[0], biases[0]))
    column_offset = jnp.concatenate([biases[1], jnp.zeros_like(biases[1]), biases[2]])
    packed_rows = lowered_backward(lowered_input(jnp.einsum('gxy,yw->gxw', first_layer, query_key_value_weight, precision=HIGH_PRECISION) + column_offset))
    query = packed_rows[..., :width].reshape(count, length, HEADS, size)
    keys = packed_rows[..., width:2 * width].reshape(count, length, HEADS, size)
    values = packed_rows[..., 2 * width:].reshape(count, length, HEADS, size)
    scores = lowered_backward(jnp.einsum('sqhd,skhd->shqk', query, keys, precision=HIGH_PRECISION) * size ** (-0.5))
    probs = lowered_input(jax.nn.softmax(scores, axis=-1))
    joined = jnp.einsum('shqk,skhd->sqhd', probs, values, precision=HIGH_PRECISION).reshape(count, length, width)
    mixed_heads = lowered_backward(lowered_input(joined))
    middle_state = latents + lowered_backward(jnp.einsum('gxy,yw->gxw', mixed_heads, output_weight, precision=HIGH_PRECISION) + biases[3])
    second_layer = lowered_input(layer_norm(middle_state, norm_gains[1], biases[4]))
    hidden_units = lowered_backward(jnp.einsum('uob,bw->uow', second_layer, up_weight, precision=HIGH_PRECISION) + feed_forward_bias)
    active_state = lowered_input(jax.nn.gelu(hidden_units))
    return middle_state + lowered_backward(jnp.einsum('rnx,xk->rnk', active_state, down_weight, precision=HIGH_PRECISION) + biases[5])

def reference(latents, query_key_value_weight, output_weight, up_weight, down_weight, norm_gains, biases, feed_forward_bias, cotangent):
    count = REPEATS * IMAGES
    group = math.gcd(count, max(1, 4096 // L))
    blocks = latents.reshape(count // group, group, L, D)
    cot_blocks = cotangent.reshape(count // group, group, L, D)
    params = tuple((a.astype(jnp.float32) for a in (query_key_value_weight, output_weight, up_weight, down_weight, norm_gains, biases, feed_forward_bias)))
    zeros = tuple((jnp.zeros(a.shape, jnp.float32) for a in params))

    def step(totals, pair):
        block, block_cotangent = pair
        result, pull = jax.vjp(forward, block.astype(jnp.float32), *params)
        grads = pull(block_cotangent.astype(jnp.float32))
        totals = tuple((t + g for t, g in zip(totals, grads[1:])))
        return (totals, (result.astype(jnp.bfloat16), grads[0].astype(jnp.bfloat16)))
    totals, (results, backs) = lax.scan(step, zeros, (blocks, cot_blocks))
    out_latents = results.reshape(REPEATS, IMAGES, L, D)
    grad_latents = backs.reshape(REPEATS, IMAGES, L, D)
    return (out_latents, grad_latents, totals[0], totals[1], totals[2], totals[3], totals[4], totals[5], totals[6])
```

```python
import jax
import jax.numpy as jnp
from jax import lax
from jax.sharding import PartitionSpec as P

HEADS = 8
EPS = 1e-05
AXES = ("batch", "rep")
BF = jnp.bfloat16
F32 = jnp.float32


def layer_norm(values, gain, shift):
    mean = jnp.mean(values, axis=-1, keepdims=True)
    centred = values - mean
    spread = jnp.mean(centred * centred, axis=-1, keepdims=True)
    return centred * lax.rsqrt(spread + EPS) * gain + shift


def permutation(move, nb, nr):
    pairs = []
    for b in range(nb):
        for r in range(nr):
            tb, tr = move(b, r)
            pairs.append((b * nr + r, tb * nr + tr))
    return pairs


class Links:
    def __init__(self, nb, nr):
        def swap(kb, kr):
            return permutation(lambda b, r: (b ^ kb, r ^ kr), nb, nr)

        self.core = swap(0, 1)
        self.rep = [swap(0, 1), swap(0, 2), swap(0, 3)]
        self.z = [swap(2, 0), swap(4, 0), swap(6, 0)]
        self.y_or_x = permutation(lambda b, r: (b, r ^ 2) if r % 2 == 0 else (b ^ 1, r), nb, nr)
        self.x_or_y = permutation(lambda b, r: (b ^ 1, r) if r % 2 == 0 else (b, r ^ 2), nb, nr)
        batch, rep = lax.axis_index("batch"), lax.axis_index("rep")
        self.xi, self.zi = batch % 2, batch // 2
        self.ci, self.yi = rep % 2, rep // 2


def move(value, pairs):
    return lax.ppermute(value, AXES, pairs)


def flip_if(bit, value, axis):
    return jnp.where(bit == 1, jnp.flip(value, axis), value)


def gather_rows(local, links):
    rows, n = local.shape
    quarter = lax.dynamic_index_in_dim(
        local.reshape(4, rows // 4, n), links.ci * 2 + links.yi, 0, keepdims=False
    )
    own = jnp.stack([quarter] + [move(quarter, p) for p in links.z])
    first = move(own, links.y_or_x)
    second = move(own, links.x_or_y)
    third = move(first, links.x_or_y)
    halves = []
    here = [own, first, second, third]
    there = [move(part, links.core) for part in here]
    for parts, core in ((here, links.ci), (there, 1 - links.ci)):
        a, f, s, t = parts
        dx = jnp.where(core == 1, f, s)
        dy = jnp.where(core == 1, s, f)
        halves.append(jnp.stack([jnp.stack([a, dy]), jnp.stack([dx, t])]))
    whole = jnp.stack(halves)
    whole = flip_if(links.ci, whole, 0)
    whole = flip_if(links.xi, whole, 1)
    whole = flip_if(links.yi, whole, 2)
    whole = flip_if(links.zi % 2, whole.reshape(2, 2, 2, 2, 2, rows // 4, n), 4)
    whole = flip_if(links.zi // 2, whole, 3)
    whole = whole.transpose(3, 4, 1, 0, 2, 5, 6)
    return whole.reshape(8 * rows, n)


def reduce_rows(partial, links):
    total, n = partial.shape
    rows, q = total // 8, n // 4
    view = partial.reshape(4, 2, rows, 2, 2, q)
    view = view.transpose(3, 1, 4, 0, 2, 5)
    keep = lax.dynamic_index_in_dim(view, links.ci, 0, keepdims=False)
    send = lax.dynamic_index_in_dim(view, 1 - links.ci, 0, keepdims=False).astype(BF)
    held = keep + move(send, links.core).astype(F32)
    held = jnp.where(links.ci == 0, held, held.transpose(1, 0, 2, 3, 4))
    mine = jnp.where(links.ci == 0, links.xi, links.yi)
    keep = lax.dynamic_index_in_dim(held, mine, 0, keepdims=False)
    send = lax.dynamic_index_in_dim(held, 1 - mine, 0, keepdims=False).astype(BF)
    held = keep + move(send, links.x_or_y).astype(F32)
    mine = jnp.where(links.ci == 0, links.yi, links.xi)
    keep = lax.dynamic_index_in_dim(held, mine, 0, keepdims=False)
    send = lax.dynamic_index_in_dim(held, 1 - mine, 0, keepdims=False).astype(BF)
    held = keep + move(send, links.y_or_x).astype(F32)
    out = lax.dynamic_index_in_dim(held, links.zi, 0, keepdims=False)
    for k, pairs in enumerate(links.z):
        send = lax.dynamic_index_in_dim(held, links.zi ^ (k + 1), 0, keepdims=False).astype(BF)
        out = out + move(send, pairs).astype(F32)
    out = out.astype(BF)
    by_core, by_y, by_both = [move(out, p) for p in links.rep]
    grid = jnp.stack([jnp.stack([out, by_y]), jnp.stack([by_core, by_both])])
    grid = flip_if(links.yi, flip_if(links.ci, grid, 0), 1)
    return grid.transpose(2, 0, 1, 3).reshape(rows, n).astype(F32)


def heads_of(packed):
    images, length, width = packed.shape
    size = width // 3 // HEADS
    view = packed.reshape(images, length, 3, HEADS, size)
    return view[:, :, 0], view[:, :, 1], view[:, :, 2], size ** (-0.5)


def per_device(latents, w_qkv, w_out, w_up, w_down, gains, biases, ff_bias, cotangent, *, nb, nr):
    reps, images, length, width = latents.shape
    x = latents.reshape(-1, width).astype(F32)
    cot = cotangent.reshape(-1, width)
    count = reps * images
    small = jnp.concatenate([gains, biases, ff_bias[None]], axis=0)
    native = nb != 8 or nr != 4
    if native:
        small = lax.all_gather(small, "batch", axis=1, tiled=True)
        w_qkv, w_out, w_up, w_down = (
            lax.all_gather(w, "batch", axis=0, tiled=True) for w in (w_qkv, w_out, w_up, w_down)
        )
    else:
        links = Links(nb, nr)
        small = lax.all_gather(small, "batch", axis=1, tiled=True)
        w_qkv = gather_rows(w_qkv, links)
        rest = gather_rows(jnp.concatenate([w_out, w_up, w_down], axis=1), links)
        w_out, w_up, w_down = rest[:, :width], rest[:, width : -width], rest[:, -width:]
    small = small.astype(F32)
    g1, g2 = small[0], small[1]
    b1, bq, bv, bo, b2, bd, bu = (small[i] for i in range(2, 9))

    def dot(a, b, dims):
        return lax.dot_general(a, b, (dims, ((), ())), preferred_element_type=F32)

    NN, NT, TN = ((1,), (0,)), ((1,), (1,)), ((0,), (0,))
    first, pull_one = jax.vjp(layer_norm, x, g1, b1)
    first = first.astype(BF)
    packed = dot(first, w_qkv, NN) + jnp.concatenate([bq, jnp.zeros_like(bq), bv])
    packed = packed.astype(BF).reshape(count, length, 3 * width)
    q, k, v, scale = heads_of(packed)
    scores = jnp.einsum("iqhd,ikhd->ihqk", q, k, preferred_element_type=F32) * scale
    top = jnp.max(scores, axis=-1, keepdims=True)
    raised = jnp.exp(scores - top)
    p = raised / jnp.sum(raised, axis=-1, keepdims=True)
    probs = p.astype(BF)
    mixed = jnp.einsum("ihqk,ikhd->iqhd", probs, v, preferred_element_type=F32)
    mixed = mixed.astype(BF).reshape(-1, width)
    middle = x + dot(mixed, w_out, NN) + bo
    second, pull_two = jax.vjp(layer_norm, middle, g2, b2)
    second = second.astype(BF)
    hidden = dot(second, w_up, NN) + bu
    active, pull_gelu = jax.vjp(jax.nn.gelu, hidden)
    active = active.astype(BF)
    out = (middle + dot(active, w_down, NN) + bd).astype(BF)
    gw_down = dot(active, cot, TN)
    gb_down = jnp.sum(cot.astype(F32), axis=0)
    g_hidden = pull_gelu(dot(cot, w_down, NT))[0].astype(BF)
    gw_up = dot(second, g_hidden, TN)
    gb_up = jnp.sum(g_hidden.astype(F32), axis=0)
    g_mid, gg2, gb2 = pull_two(dot(g_hidden, w_up, NT))
    g_middle = cot.astype(F32) + g_mid
    g_attn = g_middle.astype(BF)
    gw_out = dot(mixed, g_attn, TN)
    gb_out = jnp.sum(g_attn.astype(F32), axis=0)
    g_mixed = dot(g_attn, w_out, NT).astype(BF).reshape(count, length, HEADS, -1)
    g_v = jnp.einsum("ihqk,iqhd->ikhd", probs, g_mixed, preferred_element_type=F32)
    g_p = jnp.einsum("iqhd,ikhd->ihqk", g_mixed, v, preferred_element_type=F32)
    g_s = (p * (g_p - jnp.sum(g_p * p, axis=-1, keepdims=True))).astype(BF)
    g_q = jnp.einsum("ihqk,ikhd->iqhd", g_s, k, preferred_element_type=F32) * scale
    g_k = jnp.einsum("ihqk,iqhd->ikhd", g_s, q, preferred_element_type=F32) * scale
    g_packed = jnp.stack([g_q, g_k, g_v], axis=2).astype(BF).reshape(-1, 3 * width)
    gw_qkv = dot(first, g_packed, TN)
    gb_packed = jnp.sum(g_packed.astype(F32), axis=0)
    g_in, gg1, gb1 = pull_one(dot(g_packed, w_qkv, NT))
    g_lat = (g_middle + g_in).astype(BF)
    zero = jnp.zeros_like(gb_up)
    smalls = jnp.stack(
        [gg1, gg2, gb1, gb_packed[:width], gb_packed[2 * width :], gb_out, gb2, gb_down, gb_up]
        + [zero] * 7
    )
    smalls = lax.psum(smalls, AXES)
    smalls = lax.dynamic_slice_in_dim(smalls, lax.axis_index("batch") * (width // nb), width // nb, 1)
    if native:

        def reduced(g):
            g = lax.psum_scatter(g, "batch", scatter_dimension=0, tiled=True)
            return lax.psum(g.astype(BF), "rep").astype(F32)

        gw_qkv, gw_out, gw_up, gw_down = (reduced(g) for g in (gw_qkv, gw_out, gw_up, gw_down))
    else:
        rest = reduce_rows(jnp.concatenate([gw_out, gw_up, gw_down], axis=1), links)
        gw_qkv = reduce_rows(gw_qkv, links)
        gw_out, gw_up, gw_down = rest[:, :width], rest[:, width : -width], rest[:, -width:]
    return (
        out.reshape(latents.shape),
        g_lat.reshape(latents.shape),
        gw_qkv,
        gw_out,
        gw_up,
        gw_down,
        smalls[:2],
        smalls[2:8],
        smalls[8],
    )


def solution(mesh):
    nb, nr = mesh.shape["batch"], mesh.shape["rep"]

    def body(*args):
        return per_device(*args, nb=nb, nr=nr)

    rows = P("batch", None)
    cols = P(None, "batch")
    data = P("rep", "batch", None, None)
    return jax.shard_map(
        body,
        mesh=mesh,
        in_specs=(data, rows, rows, rows, rows, cols, cols, P("batch"), data),
        out_specs=(data, data, rows, rows, rows, rows, cols, cols, P("batch")),
        check_vma=False,
    )
```

```python
import functools

import jax
import jax.numpy as jnp
from jax import lax
from jax.experimental import pallas as pl
from jax.experimental.pallas import tpu as pltpu
from jax.sharding import PartitionSpec as P

HEADS = 8
SIZE = 128
GROUP = 4
EPS = 1e-05
AXES = ("batch", "rep")
BF = jnp.bfloat16
F32 = jnp.float32
NN, NT, TN = ((1,), (0,)), ((1,), (1,)), ((0,), (0,))
SCALE = SIZE ** (-0.5)
GELU = 0.7978845608028654
CUBIC = 0.044715
VMEM_LIMIT = 56 << 20
G1, G2, B1, BQ, BV, BO, B2, BD, BU = range(9)
CORE, YPOS, XPOS, ZPOS, THEIRS, OURS = range(6)


def dot(a, b, dims=NN):
    return lax.dot_general(a, b, (dims, ((), ())), preferred_element_type=F32)


def params(*semantics):
    return pltpu.CompilerParams(vmem_limit_bytes=VMEM_LIMIT)


def cost(flops, nbytes, trans=0):
    return pl.CostEstimate(flops=int(flops), bytes_accessed=int(nbytes), transcendentals=int(trans))


def full(array):
    rank = array.ndim
    return pl.BlockSpec(array.shape, lambda *_: (0,) * rank)


def column_sum(values):
    return jnp.sum(values.astype(F32), axis=0, keepdims=True)


def permutation(target, nb, nr):
    pairs = []
    for b in range(nb):
        for r in range(nr):
            tb, tr = target(b, r)
            pairs.append((b * nr + r, tb * nr + tr))
    return pairs


class Links:
    def __init__(self, nb, nr):
        def swap(kb, kr):
            return permutation(lambda b, r: (b ^ kb, r ^ kr), nb, nr)

        self.core = swap(0, 1)
        self.rep = [swap(0, 1), swap(0, 2), swap(0, 3)]
        self.x = swap(1, 0)
        self.y = swap(0, 2)
        self.z = [swap(2, 0), swap(4, 0), swap(6, 0)]
        self.y_or_x = permutation(lambda b, r: (b, r ^ 2) if r % 2 == 0 else (b ^ 1, r), nb, nr)
        self.x_or_y = permutation(lambda b, r: (b ^ 1, r) if r % 2 == 0 else (b, r ^ 2), nb, nr)
        batch, rep = lax.axis_index("batch"), lax.axis_index("rep")
        self.xi, self.zi = batch % 2, batch // 2
        self.ci, self.yi = rep % 2, rep // 2


def move(value, pairs):
    return lax.ppermute(value, AXES, pairs)


def flip_if(bit, value, axis):
    return jnp.where(bit == 1, jnp.flip(value, axis), value)


def pick(value, axis, index):
    return lax.dynamic_index_in_dim(value, index, axis, keepdims=False)


def gather_parts(quarter, links):
    own = jnp.stack([quarter] + [move(quarter, p) for p in links.z])
    first = move(own, links.y_or_x)
    second = move(own, links.x_or_y)
    third = move(first, links.x_or_y)
    here = [own, first, second, third]
    return here + [move(part, links.core) for part in here]


def reduce_piece(send, keep, links):
    mine_f = jnp.where(links.ci == 0, links.xi, links.yi)
    mine_s = jnp.where(links.ci == 0, links.yi, links.xi)
    parts = [keep, move(send, links.core)]

    def total(terms):
        return functools.reduce(jnp.add, [t.astype(F32) for t in terms])

    out = total([pick(p, 1, 1 - mine_f) for p in parts]).astype(BF)
    parts = [pick(p, 1, mine_f) for p in parts] + [move(out, links.x_or_y)]
    out = total([pick(p, 1, 1 - mine_s) for p in parts]).astype(BF)
    parts = [pick(p, 1, mine_s) for p in parts] + [move(out, links.y_or_x)]
    got = []
    for k, pairs in enumerate(links.z):
        out = total([pick(p, 1, links.zi ^ (k + 1)) for p in parts]).astype(BF)
        got.append(move(out, pairs))
    out = total([pick(p, 1, links.zi) for p in parts] + got).astype(BF)
    by_core, by_y, by_both = [move(out, p) for p in links.rep]
    grid = jnp.stack([jnp.stack([out, by_y]), jnp.stack([by_core, by_both])])
    return flip_if(links.yi, flip_if(links.ci, grid, 0), 1)


def reduce_small(values, links):
    for pairs in (links.core, links.y, links.x):
        values = values + move(values, pairs)
    rows, width = values.shape
    values = values.reshape(rows, 4, 2, width // 8)
    values = pick(values, 2, links.xi).transpose(1, 0, 2)
    out = pick(values, 0, links.zi)
    for k, pairs in enumerate(links.z):
        out = out + move(pick(values, 0, links.zi ^ (k + 1)), pairs)
    return out


def assemble(meta, parts, whole):
    core, y, x, z = meta[CORE], meta[YPOS], meta[XPOS], meta[ZPOS]
    rows = parts[0].shape[1]
    for i, part in enumerate(parts):
        source = core if i < 4 else 1 - core
        dx = (0, source, 1 - source, 1)[i % 4]
        dy = (0, 1 - source, source, 1)[i % 4]
        for dz in range(4):
            block = (((z ^ dz) * 2 + (x ^ dx)) * 2 + source) * 2 + (y ^ dy)
            whole[pl.ds(pl.multiple_of(block * rows, rows), rows), :] = part[dz]


def first_norm_kernel(meta, x_ref, own_ref, other_ref, first_ref, small_ref):
    @pl.when(pl.program_id(0) == 0)
    def _():
        x, z = meta[XPOS], meta[ZPOS]
        for dx, ref in enumerate((own_ref, other_ref)):
            for dz in range(4):
                block = (z ^ dz) * 2 + (x ^ dx)
                small_ref[:, pl.ds(pl.multiple_of(block * 128, 128), 128)] = ref[dz].astype(F32)

    x = x_ref[...].astype(F32)
    centred = x - jnp.mean(x, axis=-1, keepdims=True)
    scale = lax.rsqrt(jnp.mean(centred * centred, axis=-1, keepdims=True) + EPS)
    first = centred * scale * small_ref[G1 : G1 + 1, :] + small_ref[B1 : B1 + 1, :]
    first_ref[...] = first.astype(BF)


def first_norm(meta, x, own, other):
    rows, width = x.shape
    block = pl.BlockSpec((rows // 4, width), lambda i, m: (i, 0))
    return pl.pallas_call(
        first_norm_kernel,
        out_shape=(
            jax.ShapeDtypeStruct((rows, width), BF),
            jax.ShapeDtypeStruct((16, width), F32),
        ),
        grid_spec=pltpu.PrefetchScalarGridSpec(
            num_scalar_prefetch=1,
            grid=(4,),
            in_specs=[block, full(own), full(other)],
            out_specs=[block, pl.BlockSpec((16, width), lambda i, m: (0, 0))],
        ),
        compiler_params=params(),
        cost_estimate=cost(rows * width * 20, rows * width * 4),
        name="first_norm",
    )(meta, x, own, other)


def attention_forward_kernel(meta, first_ref, small_ref, *refs, images, base, count):
    parts, (packed_ref, probs_ref, mixed_ref, *rest) = refs[:count], refs[count:]
    head = pl.program_id(0)
    if count > 1:
        weight_ref = rest[0]

        @pl.when(head == 0)
        def _():
            assemble(meta, parts, weight_ref)

    else:
        weight_ref = parts[0]
    weight = weight_ref[:, pl.ds(pl.multiple_of(head * 384, 384), 384)]
    columns = pl.ds(pl.multiple_of((base + head) * SIZE, SIZE), SIZE)
    bias_q, bias_v = small_ref[BQ : BQ + 1, columns], small_ref[BV : BV + 1, columns]
    bias = jnp.concatenate([bias_q, jnp.zeros_like(bias_q), bias_v], axis=1)
    packed = (dot(first_ref[...], weight) + bias).astype(BF)
    packed_ref[...] = packed
    length = packed.shape[0] // images
    for i in range(images):
        rows = slice(i * length, (i + 1) * length)
        q, k, v = packed[rows, :SIZE], packed[rows, SIZE : 2 * SIZE], packed[rows, 2 * SIZE :]
        scores = dot(q, k, NT) * SCALE
        raised = jnp.exp(scores - jnp.max(scores, axis=-1, keepdims=True))
        probs = (raised * (1.0 / jnp.sum(raised, axis=-1, keepdims=True))).astype(BF)
        probs_ref[0, i] = probs
        mixed_ref[rows, :] = dot(probs, v).astype(BF)


def attention_forward(meta, first, small, parts, base, images):
    rows, width = first.shape
    length, n = rows // images, GROUP * 3 * SIZE
    many = len(parts) > 1
    out_shape = [
        jax.ShapeDtypeStruct((rows, n), BF),
        jax.ShapeDtypeStruct((GROUP, images, length, length), BF),
        jax.ShapeDtypeStruct((rows, GROUP * SIZE), BF),
    ]
    out_specs = [
        pl.BlockSpec((rows, 3 * SIZE), lambda h, m: (0, h)),
        pl.BlockSpec((1, images, length, length), lambda h, m: (h, 0, 0, 0)),
        pl.BlockSpec((rows, SIZE), lambda h, m: (0, h)),
    ]
    if many:
        out_shape.append(jax.ShapeDtypeStruct((width, n), BF))
        out_specs.append(pl.BlockSpec((width, n), lambda h, m: (0, 0)))
    outs = pl.pallas_call(
        functools.partial(attention_forward_kernel, images=images, base=base, count=len(parts)),
        out_shape=out_shape,
        grid_spec=pltpu.PrefetchScalarGridSpec(
            num_scalar_prefetch=1,
            grid=(GROUP,),
            in_specs=[full(first), full(small)] + [full(p) for p in parts],
            out_specs=out_specs,
        ),
        compiler_params=params(),
        cost_estimate=cost(
            2 * rows * width * n * 2 + 8 * rows * length * SIZE * GROUP,
            2 * (rows * width + width * n * 2 + rows * n + GROUP * rows * length),
            GROUP * rows * length,
        ),
        name="attention_forward",
    )(meta, first, small, *parts)
    packed, probs, mixed = outs[:3]
    return packed, probs, mixed, (outs[3] if many else parts[0])


def feed_forward_kernel(meta, x_ref, cot_ref, small_ref, *refs, mixed_count, count):
    mixed_refs, parts = refs[:mixed_count], refs[mixed_count : mixed_count + count]
    refs = refs[mixed_count + count :]
    out_ref, left_ref, right_ref, grad_mixed_ref, sums_ref = refs[:5]
    step = pl.program_id(0)
    if count > 1:
        whole = refs[5]

        @pl.when(step == 0)
        def _():
            assemble(meta, parts, whole)

    else:
        whole = parts[0]

    @pl.when(step == 0)
    def _():
        sums_ref[...] = jnp.zeros_like(sums_ref)

    d = x_ref.shape[1]

    def row(r):
        return small_ref[r : r + 1, :]

    w_out, w_up, w_down = whole[:, :d], whole[:, d : 2 * d], whole[:, 2 * d :]
    mixed = jnp.concatenate([r[...] for r in mixed_refs], axis=1)
    left_ref[0] = mixed
    middle = x_ref[...].astype(F32) + dot(mixed, w_out) + row(BO)
    centred = middle - jnp.mean(middle, axis=-1, keepdims=True)
    scale = lax.rsqrt(jnp.mean(centred * centred, axis=-1, keepdims=True) + EPS)
    normed = centred * scale
    second = (normed * row(G2) + row(B2)).astype(BF)
    left_ref[1] = second
    v = dot(second, w_up) + row(BU)
    square = v * v
    tanh = jnp.tanh(GELU * v * (1.0 + CUBIC * square))
    half = 0.5 * (1.0 + tanh)
    active = (v * half).astype(BF)
    left_ref[2] = active
    slope = half + (0.5 * v) * (1.0 - tanh * tanh) * (GELU * (1.0 + (3 * CUBIC) * square))
    out_ref[...] = (middle + dot(active, w_down) + row(BD)).astype(BF)
    cot = cot_ref[...]
    right_ref[2] = cot
    grad_hidden = (slope * dot(cot, w_down, NT)).astype(BF)
    right_ref[1] = grad_hidden
    grad_second = dot(grad_hidden, w_up, NT)
    inner = grad_second * row(G2)
    mean_one = jnp.mean(inner, axis=-1, keepdims=True)
    mean_two = jnp.mean(inner * normed, axis=-1, keepdims=True)
    grad_middle = cot.astype(F32) + scale * (inner - mean_one - normed * mean_two)
    grad_attn = grad_middle.astype(BF)
    right_ref[0] = grad_attn
    grad_mixed_ref[...] = dot(grad_attn, w_out, NT).astype(BF)
    sums_ref[0:1, :] += column_sum(grad_second * normed)
    sums_ref[1:2, :] += column_sum(grad_second)
    sums_ref[2:3, :] += column_sum(grad_attn)
    sums_ref[3:4, :] += column_sum(grad_hidden)
    sums_ref[4:5, :] += column_sum(cot)


def feed_forward(meta, x, cot, small, mixed, parts):
    rows, width = x.shape
    tm = min(512, rows)
    many = len(parts) > 1
    block = pl.BlockSpec((tm, width), lambda i, m: (i, 0))
    three = pl.BlockSpec((3, tm, width), lambda i, m: (0, i, 0))
    one = jax.ShapeDtypeStruct((rows, width), BF)
    stack = jax.ShapeDtypeStruct((3, rows, width), BF)
    return pl.pallas_call(
        functools.partial(feed_forward_kernel, mixed_count=len(mixed), count=len(parts)),
        out_shape=(one, stack, stack, one, jax.ShapeDtypeStruct((8, width), F32)),
        grid_spec=pltpu.PrefetchScalarGridSpec(
            num_scalar_prefetch=1,
            grid=(rows // tm,),
            in_specs=[block, block, full(small)]
            + [pl.BlockSpec((tm, a.shape[1]), lambda i, m: (i, 0)) for a in mixed]
            + [full(p) for p in parts],
            out_specs=[block, three, three, block, pl.BlockSpec((8, width), lambda i, m: (0, 0))],
            scratch_shapes=[pltpu.VMEM((width, 3 * width), BF)] if many else [],
        ),
        compiler_params=params(),
        cost_estimate=cost(12 * rows * width * width * 1.8, 2 * 17 * rows * width, rows * width),
        name="feed_forward",
    )(meta, x, cot, small, *mixed, *parts)


def store_piece(owner, piece_ref, values, y, columns):
    rows = values.shape[0] // 8
    for z in range(4):
        for x in range(2):
            first = jnp.where(owner == 0, x, y)
            second = jnp.where(owner == 0, y, x)
            start = (z * 2 + x) * rows
            piece_ref[0, first, second, z] = values[start : start + rows, columns].astype(BF)


def weight_grad_kernel(meta, left_ref, right_ref, piece_ref, *, half):
    values = dot(left_ref[0], right_ref[0], TN)
    q = values.shape[1] // 2
    for y in range(2):
        store_piece(meta[half], piece_ref, values, y, slice(y * q, (y + 1) * q))


def weight_grad(meta, left, right, half):
    m, rows, width = left.shape
    return pl.pallas_call(
        functools.partial(weight_grad_kernel, half=half),
        out_shape=jax.ShapeDtypeStruct((m, 2, 2, 4, width // 8, width // 4), BF),
        grid_spec=pltpu.PrefetchScalarGridSpec(
            num_scalar_prefetch=1,
            grid=(m,),
            in_specs=[
                pl.BlockSpec((1, rows, width), lambda i, s: (i, 0, 0)),
                pl.BlockSpec((1, rows, width // 2), lambda i, s: (i, 0, s[half])),
            ],
            out_specs=pl.BlockSpec(
                (1, 2, 2, 4, width // 8, width // 4), lambda i, s: (i, 0, 0, 0, 0, 0)
            ),
        ),
        compiler_params=params(),
        cost_estimate=cost(2 * m * rows * width * width // 2 * 2, 2 * m * rows * width * 2),
        name="weight_grad",
    )(meta, left, right)


def attention_backward_kernel(
    meta, first_ref, packed_ref, probs_ref, grad_ref, mixed_ref, grad_packed_ref, piece_ref, *, half, images
):
    packed, grad, mixed = packed_ref[...], grad_ref[...], mixed_ref[...]
    length = packed.shape[0] // images
    for i in range(images):
        rows = slice(i * length, (i + 1) * length)
        q, k, v = packed[rows, :SIZE], packed[rows, SIZE : 2 * SIZE], packed[rows, 2 * SIZE :]
        grad_mixed = grad[rows]
        inner = jnp.sum(
            grad_mixed.astype(F32) * mixed[rows].astype(F32), axis=-1, keepdims=True
        )
        probs = probs_ref[0, i]
        grad_packed_ref[rows, 2 * SIZE :] = dot(probs, grad_mixed, TN).astype(BF)
        grad_probs = dot(grad_mixed, v, NT)
        grad_scores = (probs.astype(F32) * (grad_probs - inner)).astype(BF)
        grad_packed_ref[rows, :SIZE] = (dot(grad_scores, k) * SCALE).astype(BF)
        grad_packed_ref[rows, SIZE : 2 * SIZE] = (dot(grad_scores, q, TN) * SCALE).astype(BF)
    values = dot(first_ref[...], grad_packed_ref[...], TN)
    store_piece(meta[half], piece_ref, values, pl.program_id(0), slice(None))


def attention_backward(meta, first, packed, probs, grad_mixed, mixed, base, half, images):
    rows, width = first.shape
    length, n = rows // images, 3 * SIZE
    pair = GROUP // 2
    return pl.pallas_call(
        functools.partial(attention_backward_kernel, half=half, images=images),
        out_shape=(
            jax.ShapeDtypeStruct((rows, pair * n), BF),
            jax.ShapeDtypeStruct((1, 2, 2, 4, width // 8, n), BF),
        ),
        grid_spec=pltpu.PrefetchScalarGridSpec(
            num_scalar_prefetch=1,
            grid=(pair,),
            in_specs=[
                full(first),
                pl.BlockSpec((rows, n), lambda j, m: (0, m[half] * pair + j)),
                pl.BlockSpec(
                    (1, images, length, length), lambda j, m: (m[half] * pair + j, 0, 0, 0)
                ),
                pl.BlockSpec((rows, SIZE), lambda j, m: (0, base + m[half] * pair + j)),
                pl.BlockSpec((rows, SIZE), lambda j, m: (0, m[half] * pair + j)),
            ],
            out_specs=[
                pl.BlockSpec((rows, n), lambda j, m: (0, j)),
                pl.BlockSpec((1, 2, 2, 4, width // 8, n), lambda j, m: (0, 0, 0, 0, 0, 0)),
            ],
        ),
        compiler_params=params(),
        cost_estimate=cost(
            pair * (2 * rows * width * n * 2 + 16 * rows * length * SIZE),
            2 * (rows * width + pair * (rows * length + 3 * rows * n)),
        ),
        name="attention_backward",
    )(meta, first, packed, probs, grad_mixed, mixed)


def input_grad_kernel(meta, x_ref, grad_ref, small_ref, *refs, groups):
    pieces, weights = refs[: 2 * groups], refs[2 * groups : 3 * groups]
    out_ref, sums_ref, packed_sums_ref = refs[3 * groups :]
    step = pl.program_id(0)

    @pl.when(step == 0)
    def _():
        sums_ref[...] = jnp.zeros_like(sums_ref)
        packed_sums_ref[...] = jnp.zeros_like(packed_sums_ref)

    total = None
    n = pieces[0].shape[1]
    for g in range(groups):
        for j, which in enumerate((THEIRS, OURS)):
            piece = pieces[2 * g + j][...]
            start = pl.multiple_of(meta[which] * n, n)
            term = dot(piece, weights[g][:, pl.ds(start, n)], NT)
            total = term if total is None else total + term
            where = pl.ds(pl.multiple_of(start + g * 2 * n, n), n)
            packed_sums_ref[0:1, where] += column_sum(piece)
    x = x_ref[...].astype(F32)
    centred = x - jnp.mean(x, axis=-1, keepdims=True)
    scale = lax.rsqrt(jnp.mean(centred * centred, axis=-1, keepdims=True) + EPS)
    normed = centred * scale
    inner = total * small_ref[G1 : G1 + 1, :]
    mean_one = jnp.mean(inner, axis=-1, keepdims=True)
    mean_two = jnp.mean(inner * normed, axis=-1, keepdims=True)
    grad = grad_ref[0].astype(F32) + scale * (inner - mean_one - normed * mean_two)
    out_ref[...] = grad.astype(BF)
    sums_ref[0:1, :] += column_sum(total * normed)
    sums_ref[1:2, :] += column_sum(total)


def input_grad(meta, x, right, small, pieces, weights):
    rows, width = x.shape
    tm = min(512, rows)
    groups = len(weights)
    block = pl.BlockSpec((tm, width), lambda i, m: (i, 0))
    return pl.pallas_call(
        functools.partial(input_grad_kernel, groups=groups),
        out_shape=(
            jax.ShapeDtypeStruct((rows, width), BF),
            jax.ShapeDtypeStruct((8, width), F32),
            jax.ShapeDtypeStruct((8, 3 * width), F32),
        ),
        grid_spec=pltpu.PrefetchScalarGridSpec(
            num_scalar_prefetch=1,
            grid=(rows // tm,),
            in_specs=[block, pl.BlockSpec((1, tm, width), lambda i, m: (0, i, 0)), full(small)]
            + [pl.BlockSpec((tm, p.shape[1]), lambda i, m: (i, 0)) for p in pieces]
            + [full(w) for w in weights],
            out_specs=[
                block,
                pl.BlockSpec((8, width), lambda i, m: (0, 0)),
                pl.BlockSpec((8, 3 * width), lambda i, m: (0, 0)),
            ],
        ),
        compiler_params=params(),
        cost_estimate=cost(2 * rows * width * width * 3 * 1.5, 2 * 9 * rows * width),
        name="input_grad",
    )(meta, x, right, small, *pieces, *weights)


def by_head(weight, base):
    rows = weight.shape[0]
    view = weight.reshape(rows, 3, HEADS, SIZE)[:, :, base : base + GROUP]
    return view.transpose(0, 2, 1, 3).reshape(rows, GROUP * 3 * SIZE)


def per_device(latents, w_qkv, w_out, w_up, w_down, gains, biases, ff_bias, cotangent, *, nb, nr):
    reps, images, length, width = latents.shape
    x = latents.reshape(-1, width)
    cot = cotangent.reshape(-1, width)
    count = reps * images
    bases = range(0, HEADS, GROUP)
    native = nb != 8 or nr != 4
    small = jnp.concatenate([gains, biases, ff_bias[None]], axis=0)
    small = jnp.pad(small, ((0, 16 - small.shape[0]), (0, 0)))
    if native:
        links = None
        zero = jnp.zeros((), jnp.int32)
        meta = jnp.stack([zero, zero, zero, zero, zero + 1, zero])

        def whole(w):
            return [lax.all_gather(w, "batch", axis=0, tiled=True)]

        table = lax.all_gather(small, "batch", axis=1, tiled=True)
        table = table.reshape(16, 4, 2, width // 8).transpose(2, 1, 0, 3)
        own, other = table[0], table[1]
        chunks = [whole(by_head(w_qkv, base)) for base in bases]
        rest = whole(jnp.concatenate([w_out, w_up, w_down], axis=1))
    else:
        links = Links(nb, nr)
        meta = jnp.stack([links.ci, links.yi, links.xi, links.zi, 1 - links.ci, links.ci])
        meta = meta.astype(jnp.int32)

        def quarter(w):
            rows = w.shape[0] // 4
            return lax.dynamic_slice_in_dim(w, (links.ci * 2 + links.yi) * rows, rows, 0)

        w_qkv = quarter(w_qkv)
        chunks = [by_head(w_qkv, base) for base in bases]
        extra = jnp.pad(small, ((0, w_qkv.shape[0] - 16), (0, 0)))
        chunks[0] = jnp.concatenate([chunks[0], extra], axis=1)
        chunks = [gather_parts(chunk, links) for chunk in chunks]
        rest = jnp.concatenate([quarter(w) for w in (w_out, w_up, w_down)], axis=1)
        rest = gather_parts(rest, links)
        n = GROUP * 3 * SIZE
        tables = [part[:, :16, n:] for part in chunks[0][:3]]
        own, other = tables[0], jnp.where(links.ci == 1, tables[1], tables[2])
        chunks[0] = [part[:, :, :n] for part in chunks[0]]

    first, small = first_norm(meta, x, own, other)
    packed, probs, mixed, weights = [], [], [], []
    for base, parts in zip(bases, chunks):
        a, b, c, d = attention_forward(meta, first, small, parts, base, count)
        packed.append(a)
        probs.append(b)
        mixed.append(c)
        weights.append(d)
    out, left, right, grad_mixed, sums = feed_forward(meta, x, cot, small, mixed, rest)
    rest_send = weight_grad(meta, left, right, THEIRS)
    rest_keep = weight_grad(meta, left, right, OURS)
    pieces, grads = [], []
    for g, base in enumerate(bases):
        pair = []
        for half in (THEIRS, OURS):
            grad_packed, piece = attention_backward(
                meta, first, packed[g], probs[g], grad_mixed, mixed[g], base, half, count
            )
            pieces.append(grad_packed)
            pair.append(piece)
        grads.append(pair)
    grad_x, sums_one, sums_packed = input_grad(meta, x, right, small, pieces, weights)
    sums_packed = sums_packed[0].reshape(HEADS, 3, SIZE)
    sums_q, sums_v = sums_packed[:, 0].reshape(width), sums_packed[:, 2].reshape(width)
    smalls = jnp.stack(
        [sums_one[0], sums[0], sums_one[1], sums_q, sums_v, sums[2], sums[1], sums[4], sums[3]]
    )
    if native:
        smalls = lax.psum_scatter(smalls, "batch", scatter_dimension=1, tiled=True)
        smalls = lax.psum(smalls, "rep")

        def reduced(send, keep):
            both = jnp.stack([keep, jnp.swapaxes(send, 1, 2)])
            m, rows, q = both.shape[1], both.shape[5], both.shape[6]
            both = both.transpose(4, 2, 5, 1, 0, 3, 6).reshape(8 * rows, m * 4 * q)
            both = lax.psum_scatter(both, "batch", scatter_dimension=0, tiled=True)
            both = lax.psum(both.astype(BF), "rep")
            return both.reshape(-1, m, 2, 2, q).transpose(2, 3, 1, 0, 4)

    else:
        smalls = reduce_small(jnp.pad(smalls, ((0, 7), (0, 0))), links)

        def reduced(send, keep):
            return reduce_piece(send, keep, links)

    rest = reduced(rest_send, rest_keep)
    rows = rest.shape[3]
    rest = rest.transpose(2, 3, 0, 1, 4).reshape(3, rows, width).astype(F32)
    heads = [reduced(send, keep)[:, :, 0] for send, keep in grads]
    heads = jnp.stack(heads)
    heads = heads.reshape(HEADS, rows, 3, SIZE).transpose(1, 2, 0, 3).reshape(rows, 3 * width)
    return (
        out.reshape(latents.shape),
        grad_x.reshape(latents.shape),
        heads.astype(F32),
        rest[0],
        rest[1],
        rest[2],
        smalls[:2],
        smalls[2:8],
        smalls[8],
    )


def solution(mesh):
    nb, nr = mesh.shape["batch"], mesh.shape["rep"]

    def body(*args):
        return per_device(*args, nb=nb, nr=nr)

    rows = P("batch", None)
    cols = P(None, "batch")
    data = P("rep", "batch", None, None)
    return jax.shard_map(
        body,
        mesh=mesh,
        in_specs=(data, rows, rows, rows, rows, cols, cols, P("batch"), data),
        out_specs=(data, data, rows, rows, rows, rows, cols, cols, P("batch")),
        check_vma=False,
    )
```

```python
import functools

import jax
import jax.numpy as jnp
from jax import lax
from jax.experimental import pallas as pl
from jax.experimental.pallas import tpu as pltpu
from jax.sharding import PartitionSpec as P

HEADS = 8
SIZE = 128
GROUP = 4
EPS = 1e-05
AXES = ("batch", "rep")
BF = jnp.bfloat16
F32 = jnp.float32
NN, NT, TN = ((1,), (0,)), ((1,), (1,)), ((0,), (0,))
SCALE = SIZE ** (-0.5)
GELU = 0.7978845608028654
CUBIC = 0.044715
VMEM_LIMIT = 56 << 20
G1, G2, B1, BQ, BV, BO, B2, BD, BU = range(9)
CORE, YPOS, XPOS, ZPOS, THEIRS, OURS = range(6)


def dot(a, b, dims=NN):
    return lax.dot_general(a, b, (dims, ((), ())), preferred_element_type=F32)


def params(*semantics):
    return pltpu.CompilerParams(vmem_limit_bytes=VMEM_LIMIT)


def cost(flops, nbytes, trans=0):
    return pl.CostEstimate(flops=int(flops), bytes_accessed=int(nbytes), transcendentals=int(trans))


def full(array):
    rank = array.ndim
    return pl.BlockSpec(array.shape, lambda *_: (0,) * rank)


def column_sum(values):
    return jnp.sum(values.astype(F32), axis=0, keepdims=True)


def permutation(target, nb, nr):
    pairs = []
    for b in range(nb):
        for r in range(nr):
            tb, tr = target(b, r)
            pairs.append((b * nr + r, tb * nr + tr))
    return pairs


class Links:
    def __init__(self, nb, nr):
        def swap(kb, kr):
            return permutation(lambda b, r: (b ^ kb, r ^ kr), nb, nr)

        self.core = swap(0, 1)
        self.rep = [swap(0, 1), swap(0, 2), swap(0, 3)]
        self.x = swap(1, 0)
        self.y = swap(0, 2)
        self.z = [swap(2, 0), swap(4, 0), swap(6, 0)]
        self.y_or_x = permutation(lambda b, r: (b, r ^ 2) if r % 2 == 0 else (b ^ 1, r), nb, nr)
        self.x_or_y = permutation(lambda b, r: (b ^ 1, r) if r % 2 == 0 else (b, r ^ 2), nb, nr)
        batch, rep = lax.axis_index("batch"), lax.axis_index("rep")
        self.xi, self.zi = batch % 2, batch // 2
        self.ci, self.yi = rep % 2, rep // 2


def move(value, pairs):
    return lax.ppermute(value, AXES, pairs)


def flip_if(bit, value, axis):
    return jnp.where(bit == 1, jnp.flip(value, axis), value)


def pick(value, axis, index):
    return lax.dynamic_index_in_dim(value, index, axis, keepdims=False)


def after(value, *others):
    return lax.optimization_barrier((value, *others))[0]


def gather_chunks(quarters, links):
    chunks = []
    along, across = (), ()
    for quarter in quarters:
        quarter = after(quarter, *along)
        along = [move(quarter, p) for p in links.z]
        own = after(jnp.stack([quarter] + along), *across)
        first = move(own, links.y_or_x)
        second = move(own, links.x_or_y)
        across = (first, second)
        third = move(first, links.x_or_y)
        here = [own, first, second, third]
        chunks.append(here + [move(part, links.core) for part in here])
    return chunks


def total(terms):
    return functools.reduce(jnp.add, [t.astype(F32) for t in terms])


class Reduction:
    def __init__(self, send, links):
        self.links = links
        self.mine_f = jnp.where(links.ci == 0, links.xi, links.yi)
        self.mine_s = jnp.where(links.ci == 0, links.yi, links.xi)
        self.got = move(send, links.core)

    def swap_first(self, keep):
        parts = [keep, self.got]
        out = total([pick(p, 1, 1 - self.mine_f) for p in parts]).astype(BF)
        self.parts = [pick(p, 1, self.mine_f) for p in parts] + [move(out, self.links.x_or_y)]
        return out

    def swap_second(self):
        out = total([pick(p, 1, 1 - self.mine_s) for p in self.parts]).astype(BF)
        self.parts = [pick(p, 1, self.mine_s) for p in self.parts]
        self.parts.append(move(out, self.links.y_or_x))
        return out

    def along(self):
        zi = self.links.zi
        outs = [total([pick(p, 1, zi ^ k) for p in self.parts]).astype(BF) for k in (1, 2, 3)]
        self.got = [move(out, pairs) for out, pairs in zip(outs, self.links.z)]
        return outs[-1]

    def share(self):
        out = total([pick(p, 1, self.links.zi) for p in self.parts] + self.got).astype(BF)
        self.quarters = [out] + [move(out, p) for p in self.links.rep]
        return out


def reduce_small(values, links):
    for pairs in (links.core, links.y, links.x):
        values = values + move(values, pairs)
    rows, width = values.shape
    values = values.reshape(rows, 4, 2, width // 8)
    values = pick(values, 2, links.xi).transpose(1, 0, 2)
    out = pick(values, 0, links.zi)
    for k, pairs in enumerate(links.z):
        out = out + move(pick(values, 0, links.zi ^ (k + 1)), pairs)
    return out


def assemble(meta, parts, whole):
    core, y, x, z = meta[CORE], meta[YPOS], meta[XPOS], meta[ZPOS]
    rows = parts[0].shape[1]
    for i, part in enumerate(parts):
        source = core if i < 4 else 1 - core
        dx = (0, source, 1 - source, 1)[i % 4]
        dy = (0, 1 - source, source, 1)[i % 4]
        for dz in range(4):
            block = (((z ^ dz) * 2 + (x ^ dx)) * 2 + source) * 2 + (y ^ dy)
            whole[pl.ds(pl.multiple_of(block * rows, rows), rows), :] = part[dz]


def first_norm_kernel(meta, x_ref, own_ref, one_ref, two_ref, first_ref, small_ref):
    @pl.when(pl.program_id(0) == 0)
    def _():
        x, z = meta[XPOS], meta[ZPOS]
        for dz in range(4):
            other = jnp.where(meta[CORE] == 1, one_ref[dz].astype(F32), two_ref[dz].astype(F32))
            for dx, values in enumerate((own_ref[dz].astype(F32), other)):
                block = (z ^ dz) * 2 + (x ^ dx)
                small_ref[:, pl.ds(pl.multiple_of(block * 128, 128), 128)] = values

    x = x_ref[...].astype(F32)
    centred = x - jnp.mean(x, axis=-1, keepdims=True)
    scale = lax.rsqrt(jnp.mean(centred * centred, axis=-1, keepdims=True) + EPS)
    first = centred * scale * small_ref[G1 : G1 + 1, :] + small_ref[B1 : B1 + 1, :]
    first_ref[...] = first.astype(BF)


def first_norm(meta, x, tables):
    rows, width = x.shape
    table = pl.BlockSpec((4, 16, 128), lambda i, m: (0, 0, tables[0].shape[2] // 128 - 1))
    block = pl.BlockSpec((rows // 4, width), lambda i, m: (i, 0))
    return pl.pallas_call(
        first_norm_kernel,
        out_shape=(
            jax.ShapeDtypeStruct((rows, width), BF),
            jax.ShapeDtypeStruct((16, width), F32),
        ),
        grid_spec=pltpu.PrefetchScalarGridSpec(
            num_scalar_prefetch=1,
            grid=(4,),
            in_specs=[block, table, table, table],
            out_specs=[block, pl.BlockSpec((16, width), lambda i, m: (0, 0))],
        ),
        compiler_params=params(),
        cost_estimate=cost(rows * width * 20, rows * width * 4),
        name="first_norm",
    )(meta, x, *tables)


def attention_forward_kernel(meta, first_ref, small_ref, *refs, images, base, count):
    parts, (packed_ref, probs_ref, mixed_ref, *rest) = refs[:count], refs[count:]
    head = pl.program_id(0)
    if count > 1:
        weight_ref = rest[0]

        @pl.when(head == 0)
        def _():
            assemble(meta, parts, weight_ref)

    else:
        weight_ref = parts[0]
    weight = weight_ref[:, pl.ds(pl.multiple_of(head * 384, 384), 384)]
    columns = pl.ds(pl.multiple_of((base + head) * SIZE, SIZE), SIZE)
    bias_q, bias_v = small_ref[BQ : BQ + 1, columns], small_ref[BV : BV + 1, columns]
    bias = jnp.concatenate([bias_q, jnp.zeros_like(bias_q), bias_v], axis=1)
    packed = (dot(first_ref[...], weight) + bias).astype(BF)
    packed_ref[...] = packed
    length = packed.shape[0] // images
    for i in range(images):
        rows = slice(i * length, (i + 1) * length)
        q, k, v = packed[rows, :SIZE], packed[rows, SIZE : 2 * SIZE], packed[rows, 2 * SIZE :]
        scores = dot(q, k, NT) * SCALE
        raised = jnp.exp(scores - jnp.max(scores, axis=-1, keepdims=True))
        probs = (raised * (1.0 / jnp.sum(raised, axis=-1, keepdims=True))).astype(BF)
        probs_ref[0, i] = probs
        mixed_ref[rows, :] = dot(probs, v).astype(BF)


def attention_forward(meta, first, small, parts, base, images):
    rows, width = first.shape
    length, n = rows // images, GROUP * 3 * SIZE
    many = len(parts) > 1
    out_shape = [
        jax.ShapeDtypeStruct((rows, n), BF),
        jax.ShapeDtypeStruct((GROUP, images, length, length), BF),
        jax.ShapeDtypeStruct((rows, GROUP * SIZE), BF),
    ]
    out_specs = [
        pl.BlockSpec((rows, 3 * SIZE), lambda h, m: (0, h)),
        pl.BlockSpec((1, images, length, length), lambda h, m: (h, 0, 0, 0)),
        pl.BlockSpec((rows, SIZE), lambda h, m: (0, h)),
    ]
    if many:
        out_shape.append(jax.ShapeDtypeStruct((width, n), BF))
        out_specs.append(pl.BlockSpec((width, n), lambda h, m: (0, 0)))
    outs = pl.pallas_call(
        functools.partial(attention_forward_kernel, images=images, base=base, count=len(parts)),
        out_shape=out_shape,
        grid_spec=pltpu.PrefetchScalarGridSpec(
            num_scalar_prefetch=1,
            grid=(GROUP,),
            in_specs=[full(first), full(small)]
            + [pl.BlockSpec((*p.shape[:-1], n), lambda *_, r=p.ndim: (0,) * r) for p in parts],
            out_specs=out_specs,
        ),
        compiler_params=params(),
        cost_estimate=cost(
            2 * rows * width * n * 2 + 8 * rows * length * SIZE * GROUP,
            2 * (rows * width + width * n * 2 + rows * n + GROUP * rows * length),
            GROUP * rows * length,
        ),
        name="attention_forward",
    )(meta, first, small, *parts)
    packed, probs, mixed = outs[:3]
    return packed, probs, mixed, (outs[3] if many else parts[0])


def feed_forward_kernel(meta, x_ref, cot_ref, small_ref, *refs, mixed_count, count):
    mixed_refs, parts = refs[:mixed_count], refs[mixed_count : mixed_count + count]
    refs = refs[mixed_count + count :]
    out_ref, left_ref, right_ref, grad_mixed_ref, sums_ref = refs[:5]
    step = pl.program_id(0)
    if count > 1:
        whole = refs[5]

        @pl.when(step == 0)
        def _():
            assemble(meta, parts, whole)

    else:
        whole = parts[0]

    @pl.when(step == 0)
    def _():
        sums_ref[...] = jnp.zeros_like(sums_ref)

    d = x_ref.shape[1]

    def row(r):
        return small_ref[r : r + 1, :]

    w_out, w_up, w_down = whole[:, :d], whole[:, d : 2 * d], whole[:, 2 * d :]
    mixed = jnp.concatenate([r[...] for r in mixed_refs], axis=1)
    left_ref[0] = mixed
    middle = x_ref[...].astype(F32) + dot(mixed, w_out) + row(BO)
    centred = middle - jnp.mean(middle, axis=-1, keepdims=True)
    scale = lax.rsqrt(jnp.mean(centred * centred, axis=-1, keepdims=True) + EPS)
    normed = centred * scale
    second = (normed * row(G2) + row(B2)).astype(BF)
    left_ref[1] = second
    v = dot(second, w_up) + row(BU)
    square = v * v
    tanh = jnp.tanh(GELU * v * (1.0 + CUBIC * square))
    half = 0.5 * (1.0 + tanh)
    active = (v * half).astype(BF)
    left_ref[2] = active
    slope = half + (0.5 * v) * (1.0 - tanh * tanh) * (GELU * (1.0 + (3 * CUBIC) * square))
    out_ref[...] = (middle + dot(active, w_down) + row(BD)).astype(BF)
    cot = cot_ref[...]
    right_ref[2] = cot
    grad_hidden = (slope * dot(cot, w_down, NT)).astype(BF)
    right_ref[1] = grad_hidden
    grad_second = dot(grad_hidden, w_up, NT)
    inner = grad_second * row(G2)
    mean_one = jnp.mean(inner, axis=-1, keepdims=True)
    mean_two = jnp.mean(inner * normed, axis=-1, keepdims=True)
    grad_middle = cot.astype(F32) + scale * (inner - mean_one - normed * mean_two)
    grad_attn = grad_middle.astype(BF)
    right_ref[0] = grad_attn
    grad_mixed_ref[...] = dot(grad_attn, w_out, NT).astype(BF)
    sums_ref[0:1, :] += column_sum(grad_second * normed)
    sums_ref[1:2, :] += column_sum(grad_second)
    sums_ref[2:3, :] += column_sum(grad_attn)
    sums_ref[3:4, :] += column_sum(grad_hidden)
    sums_ref[4:5, :] += column_sum(cot)


def feed_forward(meta, x, cot, small, mixed, parts):
    rows, width = x.shape
    tm = min(512, rows)
    many = len(parts) > 1
    block = pl.BlockSpec((tm, width), lambda i, m: (i, 0))
    three = pl.BlockSpec((3, tm, width), lambda i, m: (0, i, 0))
    one = jax.ShapeDtypeStruct((rows, width), BF)
    stack = jax.ShapeDtypeStruct((3, rows, width), BF)
    return pl.pallas_call(
        functools.partial(feed_forward_kernel, mixed_count=len(mixed), count=len(parts)),
        out_shape=(one, stack, stack, one, jax.ShapeDtypeStruct((8, width), F32)),
        grid_spec=pltpu.PrefetchScalarGridSpec(
            num_scalar_prefetch=1,
            grid=(rows // tm,),
            in_specs=[block, block, full(small)]
            + [pl.BlockSpec((tm, a.shape[1]), lambda i, m: (i, 0)) for a in mixed]
            + [full(p) for p in parts],
            out_specs=[block, three, three, block, pl.BlockSpec((8, width), lambda i, m: (0, 0))],
            scratch_shapes=[pltpu.VMEM((width, 3 * width), BF)] if many else [],
        ),
        compiler_params=params(),
        cost_estimate=cost(12 * rows * width * width * 1.8, 2 * 17 * rows * width, rows * width),
        name="feed_forward",
    )(meta, x, cot, small, *mixed, *parts)


def store_piece(owner, piece_ref, values, y, columns):
    rows = values.shape[0] // 8
    for z in range(4):
        for x in range(2):
            first = jnp.where(owner == 0, x, y)
            second = jnp.where(owner == 0, y, x)
            start = (z * 2 + x) * rows
            piece_ref[0, first, second, z] = values[start : start + rows, columns].astype(BF)


def weight_grad_kernel(meta, left_ref, right_ref, piece_ref, *, half):
    values = dot(left_ref[0], right_ref[0], TN)
    q = values.shape[1] // 2
    for y in range(2):
        store_piece(meta[half], piece_ref, values, y, slice(y * q, (y + 1) * q))


def weight_grad(meta, left, right, half):
    m, rows, width = left.shape
    return pl.pallas_call(
        functools.partial(weight_grad_kernel, half=half),
        out_shape=jax.ShapeDtypeStruct((m, 2, 2, 4, width // 8, width // 4), BF),
        grid_spec=pltpu.PrefetchScalarGridSpec(
            num_scalar_prefetch=1,
            grid=(m,),
            in_specs=[
                pl.BlockSpec((1, rows, width), lambda i, s: (i, 0, 0)),
                pl.BlockSpec((1, rows, width // 2), lambda i, s: (i, 0, s[half])),
            ],
            out_specs=pl.BlockSpec(
                (1, 2, 2, 4, width // 8, width // 4), lambda i, s: (i, 0, 0, 0, 0, 0)
            ),
        ),
        compiler_params=params(),
        cost_estimate=cost(2 * m * rows * width * width // 2 * 2, 2 * m * rows * width * 2),
        name="weight_grad",
    )(meta, left, right)


def attention_backward_kernel(
    meta, first_ref, packed_ref, probs_ref, grad_ref, mixed_ref, grad_packed_ref, piece_ref, *, half, images
):
    packed, grad, mixed = packed_ref[...], grad_ref[...], mixed_ref[...]
    length = packed.shape[0] // images
    for i in range(images):
        rows = slice(i * length, (i + 1) * length)
        q, k, v = packed[rows, :SIZE], packed[rows, SIZE : 2 * SIZE], packed[rows, 2 * SIZE :]
        grad_mixed = grad[rows]
        inner = jnp.sum(
            grad_mixed.astype(F32) * mixed[rows].astype(F32), axis=-1, keepdims=True
        )
        probs = probs_ref[0, i]
        grad_packed_ref[rows, 2 * SIZE :] = dot(probs, grad_mixed, TN).astype(BF)
        grad_probs = dot(grad_mixed, v, NT)
        grad_scores = (probs.astype(F32) * (grad_probs - inner)).astype(BF)
        grad_packed_ref[rows, :SIZE] = (dot(grad_scores, k) * SCALE).astype(BF)
        grad_packed_ref[rows, SIZE : 2 * SIZE] = (dot(grad_scores, q, TN) * SCALE).astype(BF)
    values = dot(first_ref[...], grad_packed_ref[...], TN)
    store_piece(meta[half], piece_ref, values, pl.program_id(0), slice(None))


def attention_backward(meta, first, packed, probs, grad_mixed, mixed, base, half, images):
    rows, width = first.shape
    length, n = rows // images, 3 * SIZE
    pair = GROUP // 2
    return pl.pallas_call(
        functools.partial(attention_backward_kernel, half=half, images=images),
        out_shape=(
            jax.ShapeDtypeStruct((rows, pair * n), BF),
            jax.ShapeDtypeStruct((1, 2, 2, 4, width // 8, n), BF),
        ),
        grid_spec=pltpu.PrefetchScalarGridSpec(
            num_scalar_prefetch=1,
            grid=(pair,),
            in_specs=[
                full(first),
                pl.BlockSpec((rows, n), lambda j, m: (0, m[half] * pair + j)),
                pl.BlockSpec(
                    (1, images, length, length), lambda j, m: (m[half] * pair + j, 0, 0, 0)
                ),
                pl.BlockSpec((rows, SIZE), lambda j, m: (0, base + m[half] * pair + j)),
                pl.BlockSpec((rows, SIZE), lambda j, m: (0, m[half] * pair + j)),
            ],
            out_specs=[
                pl.BlockSpec((rows, n), lambda j, m: (0, j)),
                pl.BlockSpec((1, 2, 2, 4, width // 8, n), lambda j, m: (0, 0, 0, 0, 0, 0)),
            ],
        ),
        compiler_params=params(),
        cost_estimate=cost(
            pair * (2 * rows * width * n * 2 + 16 * rows * length * SIZE),
            2 * (rows * width + pair * (rows * length + 3 * rows * n)),
        ),
        name="attention_backward",
    )(meta, first, packed, probs, grad_mixed, mixed)


def input_grad_kernel(meta, x_ref, grad_ref, small_ref, *refs, groups):
    pieces, weights = refs[: 2 * groups], refs[2 * groups : 3 * groups]
    out_ref, sums_ref, packed_sums_ref = refs[3 * groups :]
    step = pl.program_id(0)

    @pl.when(step == 0)
    def _():
        sums_ref[...] = jnp.zeros_like(sums_ref)
        packed_sums_ref[...] = jnp.zeros_like(packed_sums_ref)

    total = None
    n = pieces[0].shape[1]
    for g in range(groups):
        for j, which in enumerate((THEIRS, OURS)):
            piece = pieces[2 * g + j][...]
            start = pl.multiple_of(meta[which] * n, n)
            term = dot(piece, weights[g][:, pl.ds(start, n)], NT)
            total = term if total is None else total + term
            where = pl.ds(pl.multiple_of(start + g * 2 * n, n), n)
            packed_sums_ref[0:1, where] += column_sum(piece)
    x = x_ref[...].astype(F32)
    centred = x - jnp.mean(x, axis=-1, keepdims=True)
    scale = lax.rsqrt(jnp.mean(centred * centred, axis=-1, keepdims=True) + EPS)
    normed = centred * scale
    inner = total * small_ref[G1 : G1 + 1, :]
    mean_one = jnp.mean(inner, axis=-1, keepdims=True)
    mean_two = jnp.mean(inner * normed, axis=-1, keepdims=True)
    grad = grad_ref[0].astype(F32) + scale * (inner - mean_one - normed * mean_two)
    out_ref[...] = grad.astype(BF)
    sums_ref[0:1, :] += column_sum(total * normed)
    sums_ref[1:2, :] += column_sum(total)


def input_grad(meta, x, right, small, pieces, weights):
    rows, width = x.shape
    tm = min(512, rows)
    groups = len(weights)
    block = pl.BlockSpec((tm, width), lambda i, m: (i, 0))
    return pl.pallas_call(
        functools.partial(input_grad_kernel, groups=groups),
        out_shape=(
            jax.ShapeDtypeStruct((rows, width), BF),
            jax.ShapeDtypeStruct((8, width), F32),
            jax.ShapeDtypeStruct((8, 3 * width), F32),
        ),
        grid_spec=pltpu.PrefetchScalarGridSpec(
            num_scalar_prefetch=1,
            grid=(rows // tm,),
            in_specs=[block, pl.BlockSpec((1, tm, width), lambda i, m: (0, i, 0)), full(small)]
            + [pl.BlockSpec((tm, p.shape[1]), lambda i, m: (i, 0)) for p in pieces]
            + [full(w) for w in weights],
            out_specs=[
                block,
                pl.BlockSpec((8, width), lambda i, m: (0, 0)),
                pl.BlockSpec((8, 3 * width), lambda i, m: (0, 0)),
            ],
        ),
        compiler_params=params(),
        cost_estimate=cost(2 * rows * width * width * 3 * 1.5, 2 * 9 * rows * width),
        name="input_grad",
    )(meta, x, right, small, *pieces, *weights)


def quarter_of(meta, i):
    return (meta[CORE] ^ (i % 2)) * 2 + (meta[YPOS] ^ (i // 2))


def finish_rest_kernel(meta, *refs):
    parts, outs = refs[:4], refs[4:]
    q = parts[0].shape[2]
    for i, part in enumerate(parts):
        start = pl.multiple_of(quarter_of(meta, i) * q, q)
        for m, out in enumerate(outs):
            out[:, pl.ds(start, q)] = part[m].astype(F32)


def finish_rest(meta, quarters):
    m, rows, q = quarters[0].shape
    one = jax.ShapeDtypeStruct((rows, 4 * q), F32)
    return pl.pallas_call(
        finish_rest_kernel,
        out_shape=(one,) * m,
        grid_spec=pltpu.PrefetchScalarGridSpec(
            num_scalar_prefetch=1,
            grid=(1,),
            in_specs=[full(p) for p in quarters],
            out_specs=[pl.BlockSpec((rows, 4 * q), lambda i, s: (0, 0))] * m,
        ),
        compiler_params=params(),
        cost_estimate=cost(m * rows * q * 4, m * rows * q * 24),
        name="finish_rest",
    )(meta, *quarters)


def finish_heads_kernel(meta, *refs):
    out = refs[-1]
    width = out.shape[1] // 3
    for g in range((len(refs) - 1) // 4):
        for i in range(4):
            part = refs[4 * g + i]
            head = g * GROUP + quarter_of(meta, i)
            for j in range(3):
                start = pl.multiple_of(j * width + head * SIZE, SIZE)
                out[:, pl.ds(start, SIZE)] = part[0, :, j * SIZE : (j + 1) * SIZE].astype(F32)


def finish_heads(meta, groups):
    quarters = [q for group in groups for q in group]
    rows, n = quarters[0].shape[1], sum(q.shape[2] for q in quarters)
    return pl.pallas_call(
        finish_heads_kernel,
        out_shape=jax.ShapeDtypeStruct((rows, n), F32),
        grid_spec=pltpu.PrefetchScalarGridSpec(
            num_scalar_prefetch=1,
            grid=(1,),
            in_specs=[full(p) for p in quarters],
            out_specs=pl.BlockSpec((rows, n), lambda i, s: (0, 0)),
        ),
        compiler_params=params(),
        cost_estimate=cost(rows * n, rows * n * 6),
        name="finish_heads",
    )(meta, *quarters)


def by_head(weight, base):
    rows = weight.shape[0]
    view = weight.reshape(rows, 3, HEADS, SIZE)[:, :, base : base + GROUP]
    return view.transpose(0, 2, 1, 3).reshape(rows, GROUP * 3 * SIZE)


def per_device(latents, w_qkv, w_out, w_up, w_down, gains, biases, ff_bias, cotangent, *, nb, nr):
    reps, images, length, width = latents.shape
    x = latents.reshape(-1, width)
    cot = cotangent.reshape(-1, width)
    count = reps * images
    bases = range(0, HEADS, GROUP)
    native = nb != 8 or nr != 4
    small = jnp.concatenate([gains, biases, ff_bias[None]], axis=0)
    small = jnp.pad(small, ((0, 16 - small.shape[0]), (0, 0)))
    if native:
        links = None
        zero = jnp.zeros((), jnp.int32)
        meta = jnp.stack([zero, zero, zero, zero, zero + 1, zero])

        def whole(w):
            return [lax.all_gather(w, "batch", axis=0, tiled=True)]

        table = lax.all_gather(small, "batch", axis=1, tiled=True)
        table = table.reshape(16, 4, 2, width // 8).transpose(2, 1, 0, 3)
        tables = [table[0], table[1], table[1]]
        chunks = [whole(by_head(w_qkv, base)) for base in bases]
        rest = whole(jnp.concatenate([w_out, w_up, w_down], axis=1))
    else:
        links = Links(nb, nr)
        meta = jnp.stack([links.ci, links.yi, links.xi, links.zi, 1 - links.ci, links.ci])
        meta = meta.astype(jnp.int32)

        def quarter(w):
            rows = w.shape[0] // 4
            return lax.dynamic_slice_in_dim(w, (links.ci * 2 + links.yi) * rows, rows, 0)

        w_qkv = quarter(w_qkv)
        chunks = [by_head(w_qkv, base) for base in bases]
        extra = jnp.pad(small, ((0, w_qkv.shape[0] - 16), (0, 0)))
        chunks[0] = jnp.concatenate([chunks[0], extra], axis=1)
        rest = jnp.concatenate([quarter(w) for w in (w_out, w_up, w_down)], axis=1)
        *chunks, rest = gather_chunks(chunks + [rest], links)
        tables = chunks[0][:3]

    first, small = first_norm(meta, x, tables)
    packed, probs, mixed, weights = [], [], [], []
    for base, parts in zip(bases, chunks):
        a, b, c, d = attention_forward(meta, first, small, parts, base, count)
        packed.append(a)
        probs.append(b)
        mixed.append(c)
        weights.append(d)
    out, left, right, grad_mixed, sums = feed_forward(meta, x, cot, small, mixed, rest)

    def backward(g, half, gate):
        return attention_backward(
            meta, first, packed[g], probs[g], after(grad_mixed, *gate), mixed[g], bases[g], half, count
        )

    def collect(sums_one, sums_packed):
        sums_packed = sums_packed[0].reshape(HEADS, 3, SIZE)
        sums_q, sums_v = sums_packed[:, 0].reshape(width), sums_packed[:, 2].reshape(width)
        rows = [sums_one[0], sums[0], sums_one[1], sums_q, sums_v, sums[2], sums[1], sums[4], sums[3]]
        return jnp.stack(rows)

    def result(grad_x, grads, smalls):
        return (
            out.reshape(latents.shape),
            grad_x.reshape(latents.shape),
            *grads,
            smalls[:2],
            smalls[2:8],
            smalls[8],
        )

    if native:
        rest = [weight_grad(meta, left, right, half) for half in (THEIRS, OURS)]
        halves = [[backward(g, half, ()) for half in (THEIRS, OURS)] for g in range(len(bases))]
        pieces = [half[0] for pair in halves for half in pair]
        grad_x, sums_one, sums_packed = input_grad(meta, x, right, small, pieces, weights)
        smalls = lax.psum_scatter(
            collect(sums_one, sums_packed), "batch", scatter_dimension=1, tiled=True
        )
        smalls = lax.psum(smalls, "rep")

        def reduced(send, keep):
            both = jnp.stack([keep, jnp.swapaxes(send, 1, 2)])
            m, rows, q = both.shape[1], both.shape[5], both.shape[6]
            both = both.transpose(4, 2, 5, 1, 0, 3, 6).reshape(8 * rows, m * 4 * q)
            both = lax.psum_scatter(both, "batch", scatter_dimension=0, tiled=True)
            both = lax.psum(both.astype(BF), "rep").astype(F32)
            return both.reshape(-1, m, 4, q)

        rest = reduced(*rest)
        rows = rest.shape[0]
        heads = [reduced(pair[0][1], pair[1][1])[:, 0] for pair in halves]
        heads = jnp.concatenate(heads, axis=1).reshape(rows, HEADS, 3, SIZE)
        heads = heads.transpose(0, 2, 1, 3).reshape(rows, 3 * width)
        rest = [rest[:, i].reshape(rows, width) for i in range(3)]
        return result(grad_x, [heads, *rest], smalls)

    send = weight_grad(meta, left, right, THEIRS)
    one = Reduction(send, links)
    keep = weight_grad(meta, left, after(right, send), OURS)
    gate = one.swap_first(keep)
    packed_1, send = backward(0, THEIRS, [gate])
    two = Reduction(send, links)
    packed_2, keep = backward(0, OURS, [send])
    gate_1 = two.swap_first(keep)
    gate_2 = one.swap_second()
    packed_3, send = backward(1, THEIRS, [gate_1, gate_2])
    three = Reduction(send, links)
    packed_4, keep = backward(1, OURS, [send])
    gate_1 = three.swap_first(keep)
    gate_2 = two.swap_second()
    gate_3 = one.along()
    pieces = [packed_1, packed_2, packed_3, after(packed_4, gate_1, gate_2, gate_3)]
    grad_x, sums_one, sums_packed = input_grad(meta, x, right, small, pieces, weights)
    three.swap_second()
    one.share()
    two.along()
    smalls = reduce_small(jnp.pad(collect(sums_one, sums_packed), ((0, 7), (0, 0))), links)
    two.share()
    three.along()
    three.share()
    rest = finish_rest(meta, one.quarters)
    heads = finish_heads(meta, [two.quarters, three.quarters])
    return result(grad_x, [heads, *rest], smalls)


def solution(mesh):
    nb, nr = mesh.shape["batch"], mesh.shape["rep"]

    def body(*args):
        return per_device(*args, nb=nb, nr=nr)

    rows = P("batch", None)
    cols = P(None, "batch")
    data = P("rep", "batch", None, None)
    return jax.shard_map(
        body,
        mesh=mesh,
        in_specs=(data, rows, rows, rows, rows, cols, cols, P("batch"), data),
        out_specs=(data, data, rows, rows, rows, rows, cols, cols, P("batch")),
        check_vma=False,
    )
```

```python
import functools

import jax
import jax.numpy as jnp
from jax import lax
from jax.experimental import pallas as pl
from jax.experimental.pallas import tpu as pltpu
from jax.sharding import PartitionSpec as P

HEADS = 8
SIZE = 128
GROUP = 4
EPS = 1e-05
AXES = ("batch", "rep")
BF = jnp.bfloat16
F32 = jnp.float32
NN, NT, TN = ((1,), (0,)), ((1,), (1,)), ((0,), (0,))
SCALE = SIZE ** (-0.5)
LOG2E = 1.4426950408889634
GELU = 0.7978845608028654
CUBIC = 0.044715
G1, G2, B1, BQ, BV, BO, B2, BD, BU = range(9)
CORE, YPOS, XPOS, ZPOS, THEIRS, OURS, MINE_F, MINE_S = range(8)


def dot(a, b, dims=NN):
    return lax.dot_general(a, b, (dims, ((), ())), preferred_element_type=F32)


HBM, VMEM = pltpu.HBM, pltpu.VMEM
ANY = pl.BlockSpec(memory_space=pl.ANY)


def call(kernel, meta, operands, outs, limit, estimate, name, scratch=(), grid=(1,)):
    shapes = [shape for shape, _ in outs]
    return pl.pallas_call(
        kernel,
        out_shape=shapes,
        grid_spec=pltpu.PrefetchScalarGridSpec(
            num_scalar_prefetch=1,
            grid=grid,
            in_specs=[spec or full(a) for a, spec in operands],
            out_specs=[spec or full(a) for a, spec in outs],
            scratch_shapes=scratch,
        ),
        compiler_params=pltpu.CompilerParams(vmem_limit_bytes=limit << 20),
        cost_estimate=estimate,
        name=name,
    )(meta, *[a for a, _ in operands])


def hbm(array):
    return pltpu.with_memory_space_constraint(array, HBM)


def shaped(dtype, *shape):
    return jax.ShapeDtypeStruct(shape, dtype)


def span(index, size):
    return pl.ds(pl.multiple_of(index * size, size), size)


def cost(flops, nbytes, trans=0):
    return pl.CostEstimate(flops=1, bytes_accessed=1, transcendentals=0)


def full(array):
    rank = len(array.shape)
    return pl.BlockSpec(array.shape, lambda *_: (0,) * rank)


def column_sum(values):
    return jnp.sum(values.astype(F32), axis=0, keepdims=True)


def permutation(target, nb, nr):
    pairs = []
    for b in range(nb):
        for r in range(nr):
            tb, tr = target(b, r)
            pairs.append((b * nr + r, tb * nr + tr))
    return pairs


class Links:
    def __init__(self, nb, nr):
        def swap(kb, kr):
            return permutation(lambda b, r: (b ^ kb, r ^ kr), nb, nr)

        self.core = swap(0, 1)
        self.rep = [swap(0, 1), swap(0, 2), swap(0, 3)]
        self.x = swap(1, 0)
        self.y = swap(0, 2)
        self.z = [swap(2, 0), swap(4, 0), swap(6, 0)]
        self.y_or_x = permutation(lambda b, r: (b, r ^ 2) if r % 2 == 0 else (b ^ 1, r), nb, nr)
        self.x_or_y = permutation(lambda b, r: (b ^ 1, r) if r % 2 == 0 else (b, r ^ 2), nb, nr)
        batch, rep = lax.axis_index("batch"), lax.axis_index("rep")
        self.xi, self.zi = batch % 2, batch // 2
        self.ci, self.yi = rep % 2, rep // 2


def move(value, pairs):
    return lax.ppermute(value, AXES, pairs)


def flip_if(bit, value, axis):
    return jnp.where(bit == 1, jnp.flip(value, axis), value)


def pick(value, axis, index):
    return lax.dynamic_index_in_dim(value, index, axis, keepdims=False)


def after(value, *others):
    return lax.optimization_barrier((value, *others))[0]


def gather_chunks(quarters, links, norm):
    chunks = []
    along, across = (), ()
    late = None
    for quarter in quarters:
        quarter = after(quarter, *along)
        along = [move(quarter, p) for p in links.z]
        own = after(jnp.stack([quarter] + along), *across)
        first = move(own, links.y_or_x)
        both = own if late is None else jnp.concatenate([late, own], axis=2)
        both = move(both, links.x_or_y)
        if late is not None:
            chunks[-1].append((both, 0))
        chunks.append([(own, 0), (first, 0), (both, 0 if late is None else late.shape[2])])
        across = (both,) if len(chunks) > 1 else (both, *norm([own, first, both]))
        late = first
    chunks[-1].append((move(late, links.x_or_y), 0))
    return chunks


class CoreSwap:
    def __init__(self, links):
        self.pairs, self.moved = links.core, {}

    def __call__(self, chunk, *gates):
        for part, _ in chunk:
            if id(part) not in self.moved:
                self.moved[id(part)] = move(after(part, *gates), self.pairs)
        return chunk + [(self.moved[id(part)], start) for part, start in chunk]


class Piece:
    def __init__(self, keep, other, odd):
        self.terms, self.t = [keep, other], keep.shape[3]
        self.odd = odd
        self.late = []

    def mine(self, meta):
        both = meta[MINE_F], meta[MINE_S]
        return both[::-1] if self.odd else both


class Step:
    def __init__(self):
        self.arrays, self.views, self.jobs, self.outs = [], [], [], []

    def load(self, array, shape, view):
        self.views.append((self.place(array), shape, view))
        return len(self.views) - 1

    def place(self, array):
        for i, known in enumerate(self.arrays):
            if known is array:
                return i
        self.arrays.append(array)
        return len(self.arrays) - 1

    def out(self, shape, dtype):
        self.outs.append((shaped(dtype, *shape), None))
        return len(self.outs) - 1

    def swap(self, firsts=(), seconds=()):
        at = 0
        out = len(self.outs)
        for piece in seconds:
            self.second(piece, out, at)
            piece.next, at = at, at + 4 * piece.t
        for piece in firsts:
            self.first(piece, out, at)
            piece.next, at = at, at + 8 * piece.t
        self.out((at, 128, 128), BF)

    def first(self, piece, out, at):
        def view(ref, meta):
            return ref.at[1 - piece.mine(meta)[0]]

        loads = [self.load(a, a.shape[1:], view) for a in piece.terms]
        n = 8 * piece.t

        def job(meta, got, outs):
            values = sum(got[i][...].astype(F32) for i in loads)
            outs[out][at : at + n] = values.astype(BF).reshape(n, 128, 128)

        self.jobs.append(job)

    def second(self, piece, out, at):
        n = 4 * piece.t
        ((late, start),) = piece.late

        def view(ref, meta):
            f, s = piece.mine(meta)
            return ref.at[f, 1 - s]

        def late_view(ref, meta):
            return ref.at[pl.ds(start + (1 - piece.mine(meta)[1]) * n, n)]

        loads = [self.load(a, a.shape[2:], view) for a in piece.terms]
        loads.append(self.load(late, (n, 128, 128), late_view))

        def job(meta, got, outs):
            values = sum(got[i][...].reshape(n, 128, 128).astype(F32) for i in loads)
            outs[out][at : at + n] = values.astype(BF)

        self.jobs.append(job)

    def along(self, piece, sums=()):
        t = piece.t
        (one, start_one), (two, start_two) = piece.late

        def view(ref, meta):
            f, s = piece.mine(meta)
            return ref.at[f, s]

        def view_one(ref, meta):
            return ref.at[pl.ds(start_one + piece.mine(meta)[1] * 4 * t, 4 * t)]

        def view_two(ref, meta):
            return ref.at[pl.ds(start_two, 4 * t)]

        loads = [self.load(a, a.shape[2:], view) for a in piece.terms]
        late = [self.load(one, (4 * t, 128, 128), view_one)]
        late.append(self.load(two, (4 * t, 128, 128), view_two))
        extra = [
            (self.load(a, a.shape, lambda ref, meta: ref), row, scale, shift)
            for a, row, scale, shift in sums
        ]
        out = len(self.outs)
        for k in range(4):
            self.out((t + bool(sums), 128, 128), BF if k else F32)

        def job(meta, got, outs):
            for k in range(4):
                z = meta[ZPOS] ^ k
                dtype = BF if k else F32
                values = sum(got[i][z].astype(F32) for i in loads)
                values += sum(got[i][pl.ds(z * t, t)].astype(F32) for i in late)
                outs[out + k][:t] = values.astype(dtype)
                if extra:
                    outs[out + k][t] = jnp.zeros((128, 128), dtype)
                    for x in range(2):
                        rows = [
                            got[i][row : row + 1, span((z * 2 + x) * scale + shift, 128)]
                            for i, row, scale, shift in extra
                        ]
                        rows += [jnp.zeros((16 - len(rows), 128), F32)]
                        rows = jnp.concatenate(rows, axis=0).astype(dtype)
                        outs[out + k][t, 16 * x : 16 * x + 16] = rows

        self.jobs.append(job)

    def share(self, groups):
        loads = [
            [self.load(a, a.shape, lambda ref, meta: ref) for a in arrays] for arrays in groups
        ]
        sizes = [arrays[0].shape[0] for arrays in groups]
        out = self.out((sum(sizes), 128, 128), BF)

        def job(meta, got, outs):
            at = 0
            for slots, size in zip(loads, sizes):
                outs[out][at : at + size] = sum(got[i][...].astype(F32) for i in slots).astype(BF)
                at += size

        self.jobs.append(job)

    def small(self, arrays):
        tile = arrays[0].shape[0] - 1
        loads = [self.load(a, (128, 128), lambda ref, meta: ref.at[tile]) for a in arrays]
        out = self.out((16, 128), F32)
        self.out((16, 128), F32)

        def job(meta, got, outs):
            for k in range(2):
                rows = span(meta[XPOS] if k else 1 - meta[XPOS], 16)
                outs[out + k][...] = sum(got[i][rows, :].astype(F32) for i in loads)

        self.jobs.append(job)

    def run(self, meta, name):
        count, total = len(self.arrays), len(self.outs)

        def kernel(meta, *refs):
            outs, got, sems = refs[count : count + total], refs[count + total : -1], refs[-1]
            copies = [
                pltpu.make_async_copy(view(refs[i], meta), got[j], sems.at[j])
                for j, (i, _, view) in enumerate(self.views)
            ]
            for copy in copies:
                copy.start()
            for copy in copies:
                copy.wait()
            for job in self.jobs:
                job(meta, got, outs)

        return call(
            kernel,
            meta,
            [(a, ANY) for a in self.arrays],
            self.outs,
            12,
            cost(1, 1),
            name,
            [pltpu.VMEM(shape, self.arrays[i].dtype) for i, shape, _ in self.views]
            + [pltpu.SemaphoreType.DMA((len(self.views),))],
        )


def fetch(meta, parts, starts, whole, columns, sem, skip=0):
    first, n = columns
    if len(parts) == 1:
        source = parts[0].at[:, pl.ds(skip + first, n)]
        pltpu.make_async_copy(source, whole.at[:, pl.ds(first, n)], sem).start()
        return
    core, y, x, z = meta[CORE], meta[YPOS], meta[XPOS], meta[ZPOS]
    for i, (part, start) in enumerate(zip(parts, starts)):
        source = core if i < 4 else 1 - core
        dx = (0, source, 1 - source, 1)[i % 4]
        dy = (0, 1 - source, source, 1)[i % 4]
        for dz in range(4):
            block = (((z ^ dz) * 2 + (x ^ dx)) * 2 + source) * 2 + (y ^ dy)
            pltpu.make_async_copy(
                part.at[dz, :, pl.ds(start + skip + first, n)],
                whole.at[span(block, part.shape[1]), pl.ds(first, n)],
                sem,
            ).start()


def fetched(whole, columns, sem):
    first, n = columns
    here = whole.at[:, pl.ds(first, n)]
    pltpu.make_async_copy(here, here, sem).wait()


def normed_rows(values):
    centred = values - jnp.mean(values, axis=-1, keepdims=True)
    scale = lax.rsqrt(jnp.mean(centred * centred, axis=-1, keepdims=True) + EPS)
    return centred * scale, scale


def norm_back(grad, normed, scale):
    mean_one = jnp.mean(grad, axis=-1, keepdims=True)
    mean_two = jnp.mean(grad * normed, axis=-1, keepdims=True)
    return scale * (grad - mean_one - normed * mean_two)


def first_norm(meta, x, tables):
    rows, width = x.shape
    tm = 256
    last = tables[0].shape[2] - 128

    def kernel(meta, x_ref, own_ref, one_ref, two_ref, first_ref, small_ref):
        x, z = meta[XPOS], meta[ZPOS]
        for dz in range(4):
            own, one, two = (r[dz, :16, last:].astype(F32) for r in (own_ref, one_ref, two_ref))
            for dx, values in enumerate((own, jnp.where(meta[CORE] == 1, one, two))):
                small_ref[:, span((z ^ dz) * 2 + (x ^ dx), 128)] = values

        @pl.loop(0, rows // tm)
        def _(i):
            normed, _ = normed_rows(x_ref[span(i, tm), :].astype(F32))
            first = normed * small_ref[G1 : G1 + 1, :] + small_ref[B1 : B1 + 1, :]
            first_ref[span(i, tm), :] = first.astype(BF)

    return call(
        kernel,
        meta,
        [(a, None) for a in (x, *tables)],
        [(VMEM((rows, width), BF), None), (shaped(F32, 16, width), None)],
        16,
        cost(rows * width * 20, rows * width * 4),
        "first_norm",
    )


def attention_forward(meta, first, small, parts, base, images):
    rows, width = first.shape
    length, n = rows // images, 3 * SIZE
    parts, starts = zip(*parts)
    count = len(parts)
    columns = (0, GROUP * n)

    def kernel(meta, first_ref, small_ref, *refs):
        parts, refs = refs[:count], refs[count:]
        packed_ref, probs_ref, mixed_ref, weight_out, weight_ref, sems = refs
        head = pl.program_id(0)
        keep = pltpu.make_async_copy(weight_ref, weight_out, sems.at[1])

        @pl.when(head == 0)
        def _():
            fetch(meta, parts, starts, weight_ref, columns, sems.at[0])
            fetched(weight_ref, columns, sems.at[0])
            keep.start()

        here = span(base + head, SIZE)
        bias_q, bias_v = small_ref[BQ : BQ + 1, here], small_ref[BV : BV + 1, here]
        bias = jnp.concatenate([bias_q, jnp.zeros_like(bias_q), bias_v], axis=1)
        packed = (dot(first_ref[...], weight_ref[:, span(head, n)]) + bias).astype(BF)
        packed_ref[...] = packed
        for i in range(images):
            part = packed[i * length : (i + 1) * length]
            q, k, v = part[:, :SIZE], part[:, SIZE : 2 * SIZE], part[:, 2 * SIZE :]
            scores = dot(q, k, NT)
            top = jnp.max(scores, axis=-1, keepdims=True)
            raised = jnp.exp2((scores - top) * (SCALE * LOG2E))
            probs = raised * (1.0 / jnp.sum(raised, axis=-1, keepdims=True))
            probs = probs.astype(BF)
            probs_ref[0, i] = probs
            mixed_ref[i * length : (i + 1) * length, span(head, SIZE)] = dot(probs, v).astype(BF)

        @pl.when(head == GROUP - 1)
        def _():
            keep.wait()

    return call(
        kernel,
        meta,
        [(first, None), (small, None)] + [(p, ANY) for p in parts],
        [
            (HBM((rows, GROUP * n), BF), pl.BlockSpec((rows, n), lambda h, m: (0, h))),
            (
                HBM((GROUP, images, length, length), BF),
                pl.BlockSpec((1, images, length, length), lambda h, m: (h, 0, 0, 0)),
            ),
            (VMEM((rows, GROUP * SIZE), BF), None),
            (HBM((width, GROUP * n), BF), ANY),
        ],
        20,
        cost(
            2 * rows * width * GROUP * n * 2 + 8 * rows * length * SIZE * GROUP,
            2 * (rows * width + width * n * GROUP * 2 + rows * n * GROUP + GROUP * rows * length),
            GROUP * rows * length,
        ),
        "attention_forward",
        [pltpu.VMEM((width, GROUP * n), BF), pltpu.SemaphoreType.DMA((2,))],
        (GROUP,),
    )


def store_piece(owner, odd, piece_ref, at, values, y):
    rows = values.shape[0] // 8
    for z in range(4):
        for x in range(2):
            plain = owner == (1 if odd else 0)
            first = jnp.where(plain, x, y)
            second = jnp.where(plain, y, x)
            start = (z * 2 + x) * rows
            for j in range(values.shape[1] // 128):
                part = values[start : start + rows, j * 128 : (j + 1) * 128]
                piece_ref[first, second, z, at + j] = part.astype(BF)


def blocks(rows):
    size = min(256, rows)

    def over(body):
        pl.loop(0, rows // size)(lambda i: body(span(i, size)))

    return over


def feed_forward_first(meta, x, small, mixed, parts):
    rows, width = x.shape
    parts, starts = zip(*parts)
    count = len(parts)

    def kernel(meta, x_ref, small_ref, *refs):
        mixed_refs, parts = refs[: len(mixed)], refs[len(mixed) : len(mixed) + count]
        middle_ref, second_ref, active_ref, slope_ref, whole, sems = refs[len(mixed) + count :]
        for j in range(2):
            fetch(meta, parts, starts, whole, (j * width, width), sems.at[j])

        def row(r):
            return small_ref[r : r + 1, :]

        fetched(whole, (0, width), sems.at[0])
        fetched(whole, (width, width), sems.at[1])

        @blocks(rows)
        def _(here):
            values = jnp.concatenate([r[here, :] for r in mixed_refs], axis=1)
            middle = x_ref[here, :].astype(F32) + dot(values, whole[:, :width]) + row(BO)
            middle_ref[here, :] = middle
            normed, _ = normed_rows(middle)
            second = (normed * row(G2) + row(B2)).astype(BF)
            second_ref[here, :] = second
            v = dot(second, whole[:, width:]) + row(BU)
            square = v * v
            tanh = jnp.tanh(GELU * v * (1.0 + CUBIC * square))
            half = 0.5 * (1.0 + tanh)
            active_ref[here, :] = (v * half).astype(BF)
            slope = (0.5 * v) * (1.0 - tanh * tanh) * (GELU * (1.0 + (3 * CUBIC) * square))
            slope_ref[here, :] = (half + slope).astype(BF)

    return call(
        kernel,
        meta,
        [(x, None), (small, None)] + [(a, None) for a in mixed] + [(p, ANY) for p in parts],
        [
            (VMEM((rows, width), F32), None),
            (VMEM((rows, width), BF), None),
            (VMEM((rows, width), BF), None),
            (VMEM((rows, width), BF), None),
        ],
        24,
        cost(4 * rows * width * width, 2 * 9 * rows * width, rows * width),
        "feed_forward_first",
        [pltpu.VMEM((width, 2 * width), BF), pltpu.SemaphoreType.DMA((2,))],
    )


def store_grads(meta, pieces, m, left, right_ref, odd):
    q = right_ref.shape[1] // 4

    @pl.loop(0, 4)
    def _(j):
        core, y = j // 2, j % 2
        values = dot(left, right_ref[:, span(j, q)], TN).astype(BF)
        for piece_ref, half in zip(pieces, (THEIRS, OURS)):

            @pl.when(core == meta[half])
            def _(piece_ref=piece_ref):
                store_piece(core, odd, piece_ref, 2 * m, values, y)


def feed_forward_second(meta, cot, small, middle, second, active, slope, parts):
    rows, width = cot.shape
    parts, starts = zip(*parts)
    count = len(parts)

    def kernel(meta, cot_ref, small_ref, middle_ref, second_ref, active_ref, slope_ref, *refs):
        parts, refs = refs[:count], refs[count:]
        out_ref, hidden_ref, *pieces, sums_ref, whole, out, sems = refs
        fetch(meta, parts, starts, whole, (0, width), sems.at[0])
        store_grads(meta, pieces, 0, active_ref[...], cot_ref, False)
        fetched(whole, (0, width), sems.at[0])

        @blocks(rows)
        def _(here):
            grad = dot(cot_ref[here, :], whole[...], NT)
            hidden_ref[here, :] = (slope_ref[here, :].astype(F32) * grad).astype(BF)

        @blocks(rows)
        def _(here):
            values = middle_ref[here, :] + dot(active_ref[here, :], whole[...])
            out[here, :] = (values + small_ref[BD : BD + 1, :]).astype(BF)

        write = pltpu.make_async_copy(out, out_ref, sems.at[1])
        write.start()
        store_grads(meta, pieces, 1, second_ref[...], hidden_ref, False)
        sums_ref[...] = jnp.zeros_like(sums_ref)
        sums_ref[0:1, :] = column_sum(hidden_ref[...])
        sums_ref[1:2, :] = column_sum(cot_ref[...])
        write.wait()

    piece = VMEM((2, 2, 4, 4, width // 8, 128), BF)
    return call(
        kernel,
        meta,
        [(a, None) for a in (cot, small, middle, second, active, slope)]
        + [(p, ANY) for p in parts],
        [
            (HBM((rows, width), BF), ANY),
            (VMEM((rows, width), BF), None),
            (piece, None),
            (piece, None),
            (shaped(F32, 8, width), None),
        ],
        24,
        cost(8 * rows * width * width, 2 * 12 * rows * width),
        "feed_forward_second",
        [
            pltpu.VMEM((width, width), BF),
            pltpu.VMEM((rows, width), BF),
            pltpu.SemaphoreType.DMA((2,)),
        ],
    )


def feed_forward_third(meta, cot, small, middle, mixed, hidden, parts):
    rows, width = cot.shape
    parts, starts = zip(*parts)
    count = len(parts)

    def kernel(meta, cot_ref, small_ref, middle_ref, hidden_ref, *refs):
        mixed_refs, parts = refs[: len(mixed)], refs[len(mixed) : len(mixed) + count]
        attn_ref, *pieces, sums_ref, whole, sem = refs[len(mixed) + count :]
        fetch(meta, parts, starts, whole, (0, width), sem, width)
        fetched(whole, (0, width), sem)
        sums_ref[...] = jnp.zeros_like(sums_ref)

        @blocks(rows)
        def _(here):
            grad_second = dot(hidden_ref[here, :], whole[...], NT)
            normed, scale = normed_rows(middle_ref[here, :])
            back = norm_back(grad_second * small_ref[G2 : G2 + 1, :], normed, scale)
            grad_attn = (cot_ref[here, :].astype(F32) + back).astype(BF)
            attn_ref[here, :] = grad_attn
            sums_ref[0:1, :] += column_sum(grad_second * normed)
            sums_ref[1:2, :] += column_sum(grad_second)
            sums_ref[2:3, :] += column_sum(grad_attn)

        values = jnp.concatenate([r[...] for r in mixed_refs], axis=1)
        store_grads(meta, pieces, 0, values, attn_ref, True)

    piece = VMEM((2, 2, 4, 2, width // 8, 128), BF)
    return call(
        kernel,
        meta,
        [(a, None) for a in (cot, small, middle, hidden, *mixed)] + [(p, ANY) for p in parts],
        [(VMEM((rows, width), BF), None), (piece, None), (piece, None), (shaped(F32, 8, width), None)],
        20,
        cost(4 * rows * width * width, 2 * 12 * rows * width),
        "feed_forward_third",
        [pltpu.VMEM((width, width), BF), pltpu.SemaphoreType.DMA],
    )


def mixed_grad(meta, grad_attn, parts):
    rows, width = grad_attn.shape
    parts, starts = zip(*parts)
    count = len(parts)

    def kernel(meta, attn_ref, *refs):
        parts, (grad_ref, attn_out, whole, sems) = refs[:count], refs[count:]
        write = pltpu.make_async_copy(attn_ref, attn_out, sems.at[1])
        write.start()
        fetch(meta, parts, starts, whole, (0, width), sems.at[0])
        fetched(whole, (0, width), sems.at[0])

        @blocks(rows)
        def _(here):
            grad_ref[here, :] = dot(attn_ref[here, :], whole[...], NT).astype(BF)

        write.wait()

    return call(
        kernel,
        meta,
        [(grad_attn, None)] + [(p, ANY) for p in parts],
        [(VMEM((rows, width), BF), None), (HBM((rows, width), BF), ANY)],
        16,
        cost(2 * rows * width * width, 2 * 4 * rows * width),
        "mixed_grad",
        [pltpu.VMEM((width, width), BF), pltpu.SemaphoreType.DMA((2,))],
    )


def attention_backward(meta, first, packed, probs, grad_mixed, mixed, base, half, images, odd):
    rows, width = first.shape
    length, n = rows // images, 3 * SIZE
    pair = GROUP // 2

    def kernel(
        meta, first_ref, packed_ref, probs_ref, grad_ref, mixed_ref, grad_packed_ref, piece_ref
    ):
        j = pl.program_id(0)
        head = meta[half] * pair + j

        @pl.loop(0, images)
        def _(i):
            here = span(i, length)
            packed = packed_ref[here, :]
            q, k, v = packed[:, :SIZE], packed[:, SIZE : 2 * SIZE], packed[:, 2 * SIZE :]
            grad = grad_ref[here, span(base + head, SIZE)]
            mixed = mixed_ref[here, span(head, SIZE)]
            inner = jnp.sum(grad.astype(F32) * mixed.astype(F32), axis=-1, keepdims=True)
            probs = probs_ref[0, i]
            grad_v = dot(probs, grad, TN)
            grad_scores = (probs.astype(F32) * (dot(grad, v, NT) - inner)).astype(BF)
            grad_q = dot(grad_scores, k) * SCALE
            grad_k = dot(grad_scores, q, TN) * SCALE
            grad_packed_ref[here, :] = jnp.concatenate(
                [grad_q.astype(BF), grad_k.astype(BF), grad_v.astype(BF)], axis=1
            )

        values = dot(first_ref[...], grad_packed_ref[...], TN)
        store_piece(meta[half], odd, piece_ref, 0, values, j)

    return call(
        kernel,
        meta,
        [
            (first, None),
            (hbm(packed), pl.BlockSpec((rows, n), lambda j, m: (0, m[half] * pair + j))),
            (
                hbm(probs),
                pl.BlockSpec(
                    (1, images, length, length), lambda j, m: (m[half] * pair + j, 0, 0, 0)
                ),
            ),
            (grad_mixed, None),
            (mixed, None),
        ],
        [
            (HBM((rows, pair * n), BF), pl.BlockSpec((rows, n), lambda j, m: (0, j))),
            (VMEM((2, 2, 4, 3, width // 8, SIZE), BF), None),
        ],
        20,
        cost(
            pair * (2 * rows * width * n * 1.5 + 10 * rows * length * SIZE * 1.5),
            2 * (rows * width + pair * (rows * length + 3 * rows * n)),
        ),
        "attention_backward",
        grid=(pair,),
    )


def input_grad(meta, x, grad_attn, small, pieces, weights):
    rows, width = x.shape
    tm = min(256, rows)
    groups = len(weights)
    n = pieces[0].shape[1]

    def kernel(meta, x_ref, grad_ref, small_ref, *refs):
        pieces, weights = refs[: 2 * groups], refs[2 * groups : 3 * groups]
        out_ref, sums_ref, packed_sums_ref = refs[3 * groups :]

        @pl.when(pl.program_id(0) == 0)
        def _():
            sums_ref[...] = jnp.zeros_like(sums_ref)
            packed_sums_ref[...] = jnp.zeros_like(packed_sums_ref)

        grad = None
        for g in range(groups):
            for j, which in enumerate((THEIRS, OURS)):
                piece = pieces[2 * g + j][...]
                term = dot(piece, weights[g][:, span(meta[which], n)], NT)
                grad = term if grad is None else grad + term
                packed_sums_ref[0:1, span(2 * g + meta[which], n)] += column_sum(piece)
        normed, scale = normed_rows(x_ref[...].astype(F32))
        back = norm_back(grad * small_ref[G1 : G1 + 1, :], normed, scale)
        out_ref[...] = (grad_ref[...].astype(F32) + back).astype(BF)
        sums_ref[0:1, :] += column_sum(grad * normed)
        sums_ref[1:2, :] += column_sum(grad)

    block = pl.BlockSpec((tm, width), lambda i, m: (i, 0))
    return call(
        kernel,
        meta,
        [(hbm(x), block), (hbm(grad_attn), block), (small, None)]
        + [(hbm(p), pl.BlockSpec((tm, n), lambda i, m: (i, 0))) for p in pieces]
        + [(w, None) for w in weights],
        [
            (HBM((rows, width), BF), block),
            (shaped(F32, 8, width), None),
            (shaped(F32, 8, 3 * width), None),
        ],
        24,
        cost(6 * rows * width * width * 1.3, 2 * 9 * rows * width),
        "input_grad",
        grid=(rows // tm,),
    )


def quarter_of(meta, i):
    return (meta[CORE] ^ (i % 2)) * 2 + (meta[YPOS] ^ (i // 2))


def finish(meta, groups, places, widths, name):
    quarters = [q for group in groups for q in group]
    rows = quarters[0].shape[1]

    def kernel(meta, *refs):
        outs = refs[len(quarters) :]
        for g, place in enumerate(places):
            for i in range(4):
                part = refs[4 * g + i]
                for j in range(min(part.shape[0], len(widths) * widths[0] // 128 // 4 // len(groups))):
                    which, column = place(quarter_of(meta, i), j)
                    outs[which][:, span(column, 128)] = part[j].astype(F32)

    outs = [(shaped(F32, rows, n), None) for n in widths]
    return call(kernel, meta, [(a, None) for a in quarters], outs, 8, cost(1, 1), name)


def by_head(weight, base):
    rows = weight.shape[0]
    view = weight.reshape(rows, 3, HEADS, SIZE)[:, :, base : base + GROUP]
    return view.transpose(0, 2, 1, 3).reshape(rows, GROUP * 3 * SIZE)


def per_device(latents, w_qkv, w_out, w_up, w_down, gains, biases, ff_bias, cotangent, *, nb, nr):
    reps, images, length, width = latents.shape
    x = latents.reshape(-1, width)
    cot = cotangent.reshape(-1, width)
    count = reps * images
    bases = range(0, HEADS, GROUP)
    native = nb != 8 or nr != 4
    small = jnp.concatenate([gains, biases, ff_bias[None]], axis=0)
    small = jnp.pad(small, ((0, 16 - small.shape[0]), (0, 0)))
    if native:
        links = None
        zero = jnp.zeros((), jnp.int32)
        meta = jnp.stack([zero, zero, zero, zero, zero + 1, zero, zero, zero])

        def whole(w):
            return [(lax.all_gather(w, "batch", axis=0, tiled=True), 0)]

        table = lax.all_gather(small, "batch", axis=1, tiled=True)
        table = table.reshape(16, 4, 2, width // 8).transpose(2, 1, 0, 3)
        first, small = first_norm(meta, x, [table[0], table[1], table[1]])
        chunks = [whole(by_head(w_qkv, base)) for base in bases]
        chunks += [whole(jnp.concatenate([w_out, w_up], axis=1)), whole(w_down)]
    else:
        links = Links(nb, nr)
        mine_f = jnp.where(links.ci == 0, links.xi, links.yi)
        mine_s = jnp.where(links.ci == 0, links.yi, links.xi)
        meta = [links.ci, links.yi, links.xi, links.zi, 1 - links.ci, links.ci, mine_f, mine_s]
        meta = jnp.stack(meta).astype(jnp.int32)

        def quarter(w):
            rows = w.shape[0] // 4
            return lax.dynamic_slice_in_dim(w, (links.ci * 2 + links.yi) * rows, rows, 0)

        w_qkv = quarter(w_qkv)
        chunks = [by_head(w_qkv, base) for base in bases]
        extra = jnp.pad(small, ((0, w_qkv.shape[0] - 16), (0, 0)))
        chunks[0] = jnp.concatenate([chunks[0], extra], axis=1)
        chunks += [jnp.concatenate([quarter(w_out), quarter(w_up)], axis=1), quarter(w_down)]
        kept = []

        def norm(tables):
            kept.extend(first_norm(meta, x, tables))
            return kept

        chunks = gather_chunks(chunks, links, norm)
        first, small = kept
        other = CoreSwap(links)

    packed, probs, mixed, weights = [], [], [], []
    for base, parts in zip(bases, chunks):
        parts = parts if native else other(parts, *mixed)
        a, b, c, d = attention_forward(meta, first, small, parts, base, count)
        packed.append(a)
        probs.append(b)
        mixed.append(c)
        weights.append(d)
    outer, inner = chunks[len(bases) :]
    outer = outer if native else other(outer, mixed[0])
    middle, second, active, slope = feed_forward_first(meta, x, small, mixed, outer)
    inner = inner if native else other(inner, mixed[1])
    out, hidden, send, keep, sums_two = feed_forward_second(
        meta, cot, small, middle, second, active, slope, inner
    )
    grad_attn, send_out, keep_out, sums_three = feed_forward_third(
        meta, cot, small, middle, mixed, hidden, outer
    )

    def backward(meta, g, half):
        return attention_backward(
            meta, first, packed[g], probs[g], grad_mixed, mixed[g], bases[g], half, count, g == 1
        )

    def collect(sums_one, sums_packed):
        sums_packed = sums_packed[0].reshape(HEADS, 3, SIZE)
        sums_q, sums_v = sums_packed[:, 0].reshape(width), sums_packed[:, 2].reshape(width)
        out, two, three = sums_three[2], sums_two, sums_three
        rows = [sums_one[0], three[0], sums_one[1], sums_q, sums_v, out, three[1], two[1], two[0]]
        return jnp.stack(rows)

    def sums_of(sums_one, sums_packed):
        two, three, one, packed = sums_two, sums_three, sums_one, sums_packed
        plain = [(one, 0), (three, 0), (one, 1), None, None, (three, 2), (three, 1), (two, 1), (two, 0)]
        sums = [entry and (*entry, 1, 0) for entry in plain]
        sums[3], sums[4] = (packed, 0, 3, 0), (packed, 0, 3, 2)
        return sums

    def result(grad_x, grads, smalls):
        return (
            out.reshape(latents.shape),
            grad_x.reshape(latents.shape),
            *grads,
            smalls[:2],
            smalls[2:8],
            smalls[8],
        )

    if native:
        grad_mixed, grad_attn = mixed_grad(meta, grad_attn, outer)
        halves = [[backward(meta, g, half) for half in (THEIRS, OURS)] for g in range(len(bases))]
        pieces = [half[0] for pair in halves for half in pair]
        grad_x, sums_one, sums_packed = input_grad(meta, x, grad_attn, small, pieces, weights)
        smalls = lax.psum_scatter(
            collect(sums_one, sums_packed), "batch", scatter_dimension=1, tiled=True
        )
        smalls = lax.psum(smalls, "rep")

        def reduced(send, keep, odd):
            keep, send = (jnp.swapaxes(keep, 0, 1), send) if odd else (keep, jnp.swapaxes(send, 0, 1))
            both = jnp.stack([keep, send])
            t = both.shape[4]
            both = both.transpose(3, 1, 5, 0, 2, 4, 6).reshape(width, t * 4 * 128)
            both = lax.psum_scatter(both, "batch", scatter_dimension=0, tiled=True)
            both = lax.psum(both.astype(BF), "rep").astype(F32)
            return both.reshape(-1, 4, t, 128)

        rest = [reduced(send_out, keep_out, True), reduced(send, keep, False)]
        rows = rest[0].shape[0]
        rest = [rest[0], rest[1][:, :, 2:], rest[1][:, :, :2]]
        rest = [g.reshape(rows, width) for g in rest]
        heads = [reduced(pair[0][1], pair[1][1], g == 1) for g, pair in enumerate(halves)]
        heads = jnp.concatenate(heads, axis=1).transpose(0, 2, 1, 3).reshape(rows, 3 * width)
        return result(grad_x, [heads, *rest], smalls)

    def to_core(value):
        return move(value, links.core)

    def along(arrays):
        return [arrays[0]] + [move(a, p) for a, p in zip(arrays[1:], links.z)]

    def share(value):
        return [value] + [move(value, p) for p in links.rep]

    both = Piece(keep, to_core(send), False)
    step = Step()
    step.swap(firsts=[both])
    (sent,) = step.run(after(meta, keep_out), "step_0")
    both.late.append((move(sent, links.x_or_y), 0))
    grad_mixed, grad_attn = mixed_grad(after(meta, sent), grad_attn, outer)
    packed_1, send_1 = backward(after(meta, sent), 0, THEIRS)

    outs = Piece(keep_out, to_core(send_out), True)
    step = Step()
    step.swap(firsts=[outs], seconds=[both])
    (sent,) = step.run(after(meta, send_1), "step_1")
    moved = move(sent, links.y_or_x)
    for piece in (outs, both):
        piece.late.append((moved, piece.next))
    packed_2, keep_1 = backward(after(meta, sent), 0, OURS)
    packed_3, send_2 = backward(after(meta, sent, keep_1), 1, THEIRS)

    one = Piece(keep_1, to_core(send_1), False)
    step = Step()
    step.swap(firsts=[one], seconds=[outs])
    step.along(both)
    sent, *z_both = step.run(after(meta, send_2), "step_2")
    moved = move(sent, links.x_or_y)
    for piece in (one, outs):
        piece.late.append((moved, piece.next))
    z_both = along(z_both)
    packed_4, keep_2 = backward(after(meta, sent), 1, OURS)

    two = Piece(keep_2, to_core(send_2), True)
    step = Step()
    step.swap(firsts=[two], seconds=[one])
    step.along(outs)
    sent, *z_outs = step.run(after(meta, keep_2, *z_both[1:]), "step_3")
    moved = move(sent, links.y_or_x)
    for piece in (two, one):
        piece.late.append((moved, piece.next))
    z_outs = along(z_outs)
    pieces = [packed_1, packed_2, packed_3, packed_4]
    grad_x, sums_one, sums_packed = input_grad(
        after(meta, sent), x, grad_attn, small, pieces, weights
    )

    step = Step()
    step.swap(seconds=[two])
    step.along(one, sums_of(sums_one, sums_packed))
    step.share([z_both, z_outs])
    sent, *z_one, r_rest = step.run(after(meta, grad_x), "step_4")
    two.late.append((move(sent, links.x_or_y), 0))
    z_one, r_rest = along(z_one), share(r_rest)

    step = Step()
    step.along(two)
    step.share([z_one])
    *z_two, r_one = step.run(meta, "step_5")
    z_two, r_one = along(z_two), share(r_one)

    step = Step()
    step.share([z_two])
    step.small(r_one)
    r_two, other, smalls = step.run(meta, "step_6")
    smalls = smalls + move(other, links.x)
    rest = finish(
        after(meta, r_two),
        [r_rest],
        [lambda q, j: (2 - j // 2, q * 2 + j % 2)],
        [width] * 3,
        "finish_rest",
    )
    (heads,) = finish(
        meta,
        [r_one, share(r_two)],
        [lambda q, j: (0, j * HEADS + q), lambda q, j: (0, j * HEADS + GROUP + q)],
        [3 * width],
        "finish_heads",
    )
    return result(grad_x, [heads, *rest], smalls)


def solution(mesh):
    nb, nr = mesh.shape["batch"], mesh.shape["rep"]

    def body(*args):
        return per_device(*args, nb=nb, nr=nr)

    rows = P("batch", None)
    cols = P(None, "batch")
    data = P("rep", "batch", None, None)
    return jax.shard_map(
        body,
        mesh=mesh,
        in_specs=(data, rows, rows, rows, rows, cols, cols, P("batch"), data),
        out_specs=(data, data, rows, rows, rows, rows, cols, cols, P("batch")),
        check_vma=False,
    )
```

```python
import functools

import jax
import jax.numpy as jnp
from jax import lax
from jax.experimental import pallas as pl
from jax.experimental.pallas import tpu as pltpu
from jax.sharding import PartitionSpec as P

HEADS = 8
SIZE = 128
GROUP = 4
EPS = 1e-05
AXES = ("batch", "rep")
BF = jnp.bfloat16
F32 = jnp.float32
NN, NT, TN = ((1,), (0,)), ((1,), (1,)), ((0,), (0,))
SCALE = SIZE ** (-0.5)
LOG2E = 1.4426950408889634
GELU = 0.7978845608028654
CUBIC = 0.044715
G1, G2, B1, BQ, BV, BO, B2, BD, BU = range(9)
CORE, YPOS, XPOS, ZPOS, THEIRS, OURS, MINE_F, MINE_S = range(8)


def dot(a, b, dims=NN):
    return lax.dot_general(a, b, (dims, ((), ())), preferred_element_type=F32)


HBM, VMEM = pltpu.HBM, pltpu.VMEM
ANY = pl.BlockSpec(memory_space=pl.ANY)


def call(kernel, meta, operands, outs, limit, estimate, name, scratch=(), grid=(1,)):
    shapes = [shape for shape, _ in outs]
    return pl.pallas_call(
        kernel,
        out_shape=shapes,
        grid_spec=pltpu.PrefetchScalarGridSpec(
            num_scalar_prefetch=1,
            grid=grid,
            in_specs=[spec or full(a) for a, spec in operands],
            out_specs=[spec or full(a) for a, spec in outs],
            scratch_shapes=scratch,
        ),
        compiler_params=pltpu.CompilerParams(vmem_limit_bytes=limit << 20),
        cost_estimate=estimate,
        name=name,
    )(meta, *[a for a, _ in operands])


def hbm(array):
    return pltpu.with_memory_space_constraint(array, HBM)


def shaped(dtype, *shape):
    return jax.ShapeDtypeStruct(shape, dtype)


def span(index, size):
    return pl.ds(pl.multiple_of(index * size, size), size)


def cost(flops, nbytes, trans=0):
    return pl.CostEstimate(flops=1, bytes_accessed=1, transcendentals=0)


def full(array):
    rank = len(array.shape)
    return pl.BlockSpec(array.shape, lambda *_: (0,) * rank)


def column_sum(values):
    return jnp.sum(values.astype(F32), axis=0, keepdims=True)


def permutation(target, nb, nr):
    pairs = []
    for b in range(nb):
        for r in range(nr):
            tb, tr = target(b, r)
            pairs.append((b * nr + r, tb * nr + tr))
    return pairs


class Links:
    def __init__(self, nb, nr):
        def swap(kb, kr):
            return permutation(lambda b, r: (b ^ kb, r ^ kr), nb, nr)

        self.core = swap(0, 1)
        self.rep = [swap(0, 1), swap(0, 2), swap(0, 3)]
        self.x = swap(1, 0)
        self.y = swap(0, 2)
        self.z = [swap(2, 0), swap(4, 0), swap(6, 0)]
        self.y_or_x = permutation(lambda b, r: (b, r ^ 2) if r % 2 == 0 else (b ^ 1, r), nb, nr)
        self.x_or_y = permutation(lambda b, r: (b ^ 1, r) if r % 2 == 0 else (b, r ^ 2), nb, nr)
        batch, rep = lax.axis_index("batch"), lax.axis_index("rep")
        self.xi, self.zi = batch % 2, batch // 2
        self.ci, self.yi = rep % 2, rep // 2


def move(value, pairs):
    return lax.ppermute(value, AXES, pairs)


def flip_if(bit, value, axis):
    return jnp.where(bit == 1, jnp.flip(value, axis), value)


def pick(value, axis, index):
    return lax.dynamic_index_in_dim(value, index, axis, keepdims=False)


def after(value, *others):
    return lax.optimization_barrier((value, *others))[0]


def gather_chunks(quarters, links, visit):
    chunks = []
    along, across = (), ()
    late = None
    for i, quarter in enumerate(quarters):
        quarter = after(quarter, *along)
        along = [move(quarter, p) for p in links.z]
        own = jnp.stack([after(quarter, *across)] + along)
        first = move(own, links.y_or_x)
        both = own if late is None else jnp.concatenate([late, own], axis=2)
        both = move(both, links.x_or_y)
        if late is not None:
            chunks[-1].append((both, 0))
        chunks.append([(own, 0), (first, 0), (both, 0 if late is None else late.shape[2])])
        late = first
        across = (both, *visit(i, chunks))
    chunks[-1].append((move(after(late, *across[1:]), links.x_or_y), 0))
    return chunks


class CoreSwap:
    def __init__(self, links):
        self.pairs, self.moved = links.core, {}

    def __call__(self, chunk, *gates):
        for part, _ in chunk:
            if id(part) not in self.moved:
                self.moved[id(part)] = move(after(part, *gates), self.pairs)
        return chunk + [(self.moved[id(part)], start) for part, start in chunk]

    def early(self, chunk, count, *gates):
        moved = self(chunk[:count], *gates)
        return [part for part, _ in moved[count:]]


class Piece:
    def __init__(self, keep, other, odd):
        self.terms, self.t = [keep, other], keep.shape[3]
        self.odd = odd
        self.late = []

    def mine(self, meta):
        both = meta[MINE_F], meta[MINE_S]
        return both[::-1] if self.odd else both


class Step:
    def __init__(self):
        self.arrays, self.views, self.jobs, self.outs = [], [], [], []

    def load(self, array, shape, view):
        self.views.append((self.place(array), shape, view))
        return len(self.views) - 1

    def place(self, array):
        for i, known in enumerate(self.arrays):
            if known is array:
                return i
        self.arrays.append(array)
        return len(self.arrays) - 1

    def out(self, shape, dtype):
        self.outs.append((shaped(dtype, *shape), None))
        return len(self.outs) - 1

    def swap(self, firsts=(), seconds=()):
        at = 0
        out = len(self.outs)
        for piece in seconds:
            self.second(piece, out, at)
            piece.next, at = at, at + 4 * piece.t
        for piece in firsts:
            self.first(piece, out, at)
            piece.next, at = at, at + 8 * piece.t
        self.out((at, 128, 128), BF)

    def first(self, piece, out, at):
        def view(ref, meta):
            return ref.at[1 - piece.mine(meta)[0]]

        loads = [self.load(a, a.shape[1:], view) for a in piece.terms]
        n = 8 * piece.t

        def job(meta, got, outs):
            values = sum(got[i][...].astype(F32) for i in loads)
            outs[out][at : at + n] = values.astype(BF).reshape(n, 128, 128)

        self.jobs.append((job, len(self.views)))

    def second(self, piece, out, at):
        n = 4 * piece.t
        ((late, start),) = piece.late

        def view(ref, meta):
            f, s = piece.mine(meta)
            return ref.at[f, 1 - s]

        def late_view(ref, meta):
            return ref.at[pl.ds(start + (1 - piece.mine(meta)[1]) * n, n)]

        loads = [self.load(a, a.shape[2:], view) for a in piece.terms]
        loads.append(self.load(late, (n, 128, 128), late_view))

        def job(meta, got, outs):
            values = sum(got[i][...].reshape(n, 128, 128).astype(F32) for i in loads)
            outs[out][at : at + n] = values.astype(BF)

        self.jobs.append((job, len(self.views)))

    def along(self, piece, sums=()):
        t = piece.t
        (one, start_one), (two, start_two) = piece.late

        def view(ref, meta):
            f, s = piece.mine(meta)
            return ref.at[f, s]

        def view_one(ref, meta):
            return ref.at[pl.ds(start_one + piece.mine(meta)[1] * 4 * t, 4 * t)]

        def view_two(ref, meta):
            return ref.at[pl.ds(start_two, 4 * t)]

        loads = [self.load(a, a.shape[2:], view) for a in piece.terms]
        late = [self.load(one, (4 * t, 128, 128), view_one)]
        late.append(self.load(two, (4 * t, 128, 128), view_two))
        extra = [
            (self.load(a, a.shape, lambda ref, meta: ref), row, scale, shift)
            for a, row, scale, shift in sums
        ]
        out = len(self.outs)
        for k in range(4):
            self.out((t + bool(sums), 128, 128), BF if k else F32)

        def job(meta, got, outs):
            for k in range(4):
                z = meta[ZPOS] ^ k
                dtype = BF if k else F32
                values = sum(got[i][z].astype(F32) for i in loads)
                values += sum(got[i][pl.ds(z * t, t)].astype(F32) for i in late)
                outs[out + k][:t] = values.astype(dtype)
                if extra:
                    outs[out + k][t] = jnp.zeros((128, 128), dtype)
                    for x in range(2):
                        rows = [
                            got[i][row : row + 1, span((z * 2 + x) * scale + shift, 128)]
                            for i, row, scale, shift in extra
                        ]
                        rows += [jnp.zeros((16 - len(rows), 128), F32)]
                        rows = jnp.concatenate(rows, axis=0).astype(dtype)
                        outs[out + k][t, 16 * x : 16 * x + 16] = rows

        self.jobs.append((job, len(self.views)))

    def share(self, groups):
        loads = [
            [self.load(a, a.shape, lambda ref, meta: ref) for a in arrays] for arrays in groups
        ]
        sizes = [arrays[0].shape[0] for arrays in groups]
        out = self.out((sum(sizes), 128, 128), BF)

        def job(meta, got, outs):
            at = 0
            for slots, size in zip(loads, sizes):
                outs[out][at : at + size] = sum(got[i][...].astype(F32) for i in slots).astype(BF)
                at += size

        self.jobs.append((job, len(self.views)))

    def small(self, arrays):
        tile = arrays[0].shape[0] - 1
        loads = [self.load(a, (128, 128), lambda ref, meta: ref.at[tile]) for a in arrays]
        out = self.out((16, 128), F32)
        self.out((16, 128), F32)

        def job(meta, got, outs):
            for k in range(2):
                rows = span(meta[XPOS] if k else 1 - meta[XPOS], 16)
                outs[out + k][...] = sum(got[i][rows, :].astype(F32) for i in loads)

        self.jobs.append((job, len(self.views)))

    def run(self, meta, name):
        count, total = len(self.arrays), len(self.outs)

        def kernel(meta, *refs):
            outs, got, sems = refs[count : count + total], refs[count + total : -1], refs[-1]
            copies = [
                pltpu.make_async_copy(view(refs[i], meta), got[j], sems.at[j])
                for j, (i, _, view) in enumerate(self.views)
            ]
            for copy in copies:
                copy.start()
            ready = 0
            for job, last in self.jobs:
                for copy in copies[ready:last]:
                    copy.wait()
                ready = last
                job(meta, got, outs)

        return call(
            kernel,
            meta,
            [(a, ANY) for a in self.arrays],
            self.outs,
            12,
            cost(1, 1),
            name,
            [pltpu.VMEM(shape, self.arrays[i].dtype) for i, shape, _ in self.views]
            + [pltpu.SemaphoreType.DMA((len(self.views),))],
        )


def fetch(meta, parts, starts, whole, columns, sem, skip=0):
    first, n = columns
    if len(parts) == 1:
        source = parts[0].at[:, pl.ds(skip + first, n)]
        pltpu.make_async_copy(source, whole.at[:, pl.ds(first, n)], sem).start()
        return
    core, y, x, z = meta[CORE], meta[YPOS], meta[XPOS], meta[ZPOS]
    for i, (part, start) in enumerate(zip(parts, starts)):
        source = core if i < 4 else 1 - core
        dx = (0, source, 1 - source, 1)[i % 4]
        dy = (0, 1 - source, source, 1)[i % 4]
        for dz in range(4):
            block = (((z ^ dz) * 2 + (x ^ dx)) * 2 + source) * 2 + (y ^ dy)
            pltpu.make_async_copy(
                part.at[dz, :, pl.ds(start + skip + first, n)],
                whole.at[span(block, part.shape[1]), pl.ds(first, n)],
                sem,
            ).start()


def fetched(whole, columns, sem):
    first, n = columns
    here = whole.at[:, pl.ds(first, n)]
    pltpu.make_async_copy(here, here, sem).wait()


def normed_rows(values):
    centred = values - jnp.mean(values, axis=-1, keepdims=True)
    scale = lax.rsqrt(jnp.mean(centred * centred, axis=-1, keepdims=True) + EPS)
    return centred * scale, scale


def norm_back(grad, normed, scale):
    mean_one = jnp.mean(grad, axis=-1, keepdims=True)
    mean_two = jnp.mean(grad * normed, axis=-1, keepdims=True)
    return scale * (grad - mean_one - normed * mean_two)


def first_norm(meta, x, tables):
    rows, width = x.shape
    tm = 256
    last = tables[0].shape[2] - 128

    def kernel(meta, x_ref, own_ref, one_ref, two_ref, first_ref, small_ref):
        x, z = meta[XPOS], meta[ZPOS]
        for dz in range(4):
            own, one, two = (r[dz, :16, last:].astype(F32) for r in (own_ref, one_ref, two_ref))
            for dx, values in enumerate((own, jnp.where(meta[CORE] == 1, one, two))):
                small_ref[:, span((z ^ dz) * 2 + (x ^ dx), 128)] = values

        @pl.loop(0, rows // tm)
        def _(i):
            normed, _ = normed_rows(x_ref[span(i, tm), :].astype(F32))
            first = normed * small_ref[G1 : G1 + 1, :] + small_ref[B1 : B1 + 1, :]
            first_ref[span(i, tm), :] = first.astype(BF)

    return call(
        kernel,
        meta,
        [(a, None) for a in (x, *tables)],
        [(VMEM((rows, width), BF), None), (shaped(F32, 16, width), None)],
        16,
        cost(rows * width * 20, rows * width * 4),
        "first_norm",
    )


def attention_forward(meta, first, small, parts, base, images):
    rows, width = first.shape
    length, n = rows // images, 3 * SIZE
    parts, starts = zip(*parts)
    count = len(parts)
    columns = (0, GROUP * n)

    def kernel(meta, first_ref, small_ref, *refs):
        parts, refs = refs[:count], refs[count:]
        packed_ref, probs_ref, mixed_ref, weight_out, weight_ref, sems = refs
        head = pl.program_id(0)
        keep = pltpu.make_async_copy(weight_ref, weight_out, sems.at[1])

        @pl.when(head == 0)
        def _():
            fetch(meta, parts, starts, weight_ref, columns, sems.at[0])
            fetched(weight_ref, columns, sems.at[0])
            keep.start()

        here = span(base + head, SIZE)
        bias_q, bias_v = small_ref[BQ : BQ + 1, here], small_ref[BV : BV + 1, here]
        bias = jnp.concatenate([bias_q, jnp.zeros_like(bias_q), bias_v], axis=1)
        packed = (dot(first_ref[...], weight_ref[:, span(head, n)]) + bias).astype(BF)
        packed_ref[...] = packed
        for i in range(images):
            part = packed[i * length : (i + 1) * length]
            q, k, v = part[:, :SIZE], part[:, SIZE : 2 * SIZE], part[:, 2 * SIZE :]
            scores = dot(q, k, NT)
            top = jnp.max(scores, axis=-1, keepdims=True)
            raised = jnp.exp2((scores - top) * (SCALE * LOG2E))
            probs = raised * (1.0 / jnp.sum(raised, axis=-1, keepdims=True))
            probs = probs.astype(BF)
            probs_ref[0, i] = probs
            mixed_ref[i * length : (i + 1) * length, span(head, SIZE)] = dot(probs, v).astype(BF)

        @pl.when(head == GROUP - 1)
        def _():
            keep.wait()

    return call(
        kernel,
        meta,
        [(first, None), (small, None)] + [(p, ANY) for p in parts],
        [
            (HBM((rows, GROUP * n), BF), pl.BlockSpec((rows, n), lambda h, m: (0, h))),
            (
                HBM((GROUP, images, length, length), BF),
                pl.BlockSpec((1, images, length, length), lambda h, m: (h, 0, 0, 0)),
            ),
            (VMEM((rows, GROUP * SIZE), BF), None),
            (HBM((width, GROUP * n), BF), ANY),
        ],
        20,
        cost(
            2 * rows * width * GROUP * n * 2 + 8 * rows * length * SIZE * GROUP,
            2 * (rows * width + width * n * GROUP * 2 + rows * n * GROUP + GROUP * rows * length),
            GROUP * rows * length,
        ),
        "attention_forward",
        [pltpu.VMEM((width, GROUP * n), BF), pltpu.SemaphoreType.DMA((2,))],
        (GROUP,),
    )


def store_piece(owner, odd, piece_ref, at, values, y):
    rows = values.shape[0] // 8
    for z in range(4):
        for x in range(2):
            plain = owner == (1 if odd else 0)
            first = jnp.where(plain, x, y)
            second = jnp.where(plain, y, x)
            start = (z * 2 + x) * rows
            for j in range(values.shape[1] // 128):
                part = values[start : start + rows, j * 128 : (j + 1) * 128]
                piece_ref[first, second, z, at + j] = part.astype(BF)


def blocks(rows):
    size = min(256, rows)

    def over(body):
        pl.loop(0, rows // size)(lambda i: body(span(i, size), i))

    return over


def feed_forward_first(meta, x, small, mixed, parts):
    rows, width = x.shape
    parts, starts = zip(*parts)
    count = len(parts)

    def kernel(meta, x_ref, small_ref, *refs):
        mixed_refs, parts = refs[: len(mixed)], refs[len(mixed) : len(mixed) + count]
        middle_ref, second_ref, active_ref, slope_ref, whole, sems = refs[len(mixed) + count :]
        for j in range(2):
            fetch(meta, parts, starts, whole, (j * width, width), sems.at[j])

        def row(r):
            return small_ref[r : r + 1, :]

        fetched(whole, (0, width), sems.at[0])

        @blocks(rows)
        def _(here, i):
            values = jnp.concatenate([r[here, :] for r in mixed_refs], axis=1)
            middle = x_ref[here, :].astype(F32) + dot(values, whole[:, :width]) + row(BO)
            middle_ref[here, :] = middle
            normed, _ = normed_rows(middle)
            second = (normed * row(G2) + row(B2)).astype(BF)
            second_ref[here, :] = second

            @pl.when(i == 0)
            def _():
                fetched(whole, (width, width), sems.at[1])

            v = dot(second, whole[:, width:]) + row(BU)
            square = v * v
            half = 0.5 * jnp.tanh(v * (GELU + (GELU * CUBIC) * square)) + 0.5
            active = v * half
            active_ref[here, :] = active.astype(BF)
            slope = (1.0 - half) * active * (2 * GELU + (6 * GELU * CUBIC) * square)
            slope_ref[here, :] = (half + slope).astype(BF)

    return call(
        kernel,
        meta,
        [(x, None), (small, None)] + [(a, None) for a in mixed] + [(p, ANY) for p in parts],
        [
            (VMEM((rows, width), F32), None),
            (VMEM((rows, width), BF), None),
            (VMEM((rows, width), BF), None),
            (VMEM((rows, width), BF), None),
        ],
        24,
        cost(4 * rows * width * width, 2 * 9 * rows * width, rows * width),
        "feed_forward_first",
        [pltpu.VMEM((width, 2 * width), BF), pltpu.SemaphoreType.DMA((2,))],
    )


def store_grads(meta, pieces, m, left_ref, right_ref, odd):
    q = right_ref.shape[1] // 4

    @pl.loop(0, 4)
    def _(j):
        core, y = j // 2, j % 2
        values = dot(left_ref[...], right_ref[:, span(j, q)]).astype(BF)
        for piece_ref, half in zip(pieces, (THEIRS, OURS)):

            @pl.when(core == meta[half])
            def _(piece_ref=piece_ref):
                store_piece(core, odd, piece_ref, 2 * m, values, y)


def feed_forward_second(meta, cot, small, middle, second, active, slope, parts):
    rows, width = cot.shape
    parts, starts = zip(*parts)
    count = len(parts)

    def kernel(meta, cot_ref, small_ref, middle_ref, second_ref, active_ref, slope_ref, *refs):
        parts, refs = refs[:count], refs[count:]
        out_ref, hidden_ref, *pieces, sums_ref, whole, out, flipped, sems = refs
        fetch(meta, parts, starts, whole, (0, width), sems.at[0])
        flipped[...] = active_ref[...].T
        store_grads(meta, pieces, 0, flipped, cot_ref, False)
        fetched(whole, (0, width), sems.at[0])

        @blocks(rows)
        def _(here, _):
            grad = dot(cot_ref[here, :], whole[...], NT)
            hidden_ref[here, :] = (slope_ref[here, :].astype(F32) * grad).astype(BF)

        @blocks(rows)
        def _(here, _):
            values = middle_ref[here, :] + dot(active_ref[here, :], whole[...])
            out[here, :] = (values + small_ref[BD : BD + 1, :]).astype(BF)

        write = pltpu.make_async_copy(out, out_ref, sems.at[1])
        write.start()
        flipped[...] = second_ref[...].T
        store_grads(meta, pieces, 1, flipped, hidden_ref, False)
        sums_ref[...] = jnp.zeros_like(sums_ref)
        sums_ref[0:1, :] = column_sum(hidden_ref[...])
        sums_ref[1:2, :] = column_sum(cot_ref[...])
        write.wait()

    piece = VMEM((2, 2, 4, 4, width // 8, 128), BF)
    return call(
        kernel,
        meta,
        [(a, None) for a in (cot, small, middle, second, active, slope)]
        + [(p, ANY) for p in parts],
        [
            (HBM((rows, width), BF), ANY),
            (VMEM((rows, width), BF), None),
            (piece, None),
            (piece, None),
            (shaped(F32, 8, width), None),
        ],
        24,
        cost(8 * rows * width * width, 2 * 12 * rows * width),
        "feed_forward_second",
        [
            pltpu.VMEM((width, width), BF),
            pltpu.VMEM((rows, width), BF),
            pltpu.VMEM((width, rows), BF),
            pltpu.SemaphoreType.DMA((2,)),
        ],
    )


def feed_forward_third(meta, cot, small, middle, mixed, hidden, parts):
    rows, width = cot.shape
    parts, starts = zip(*parts)
    count = len(parts)

    def kernel(meta, cot_ref, small_ref, middle_ref, hidden_ref, *refs):
        mixed_refs, parts = refs[: len(mixed)], refs[len(mixed) : len(mixed) + count]
        attn_ref, *pieces, sums_ref, whole, flipped, sem = refs[len(mixed) + count :]
        fetch(meta, parts, starts, whole, (0, width), sem, width)
        fetched(whole, (0, width), sem)
        sums_ref[...] = jnp.zeros_like(sums_ref)

        @blocks(rows)
        def _(here, _):
            grad_second = dot(hidden_ref[here, :], whole[...], NT)
            normed, scale = normed_rows(middle_ref[here, :])
            back = norm_back(grad_second * small_ref[G2 : G2 + 1, :], normed, scale)
            grad_attn = (cot_ref[here, :].astype(F32) + back).astype(BF)
            attn_ref[here, :] = grad_attn
            sums_ref[0:1, :] += column_sum(grad_second * normed)
            sums_ref[1:2, :] += column_sum(grad_second)
            sums_ref[2:3, :] += column_sum(grad_attn)

        for i, ref in enumerate(mixed_refs):
            n = ref.shape[1]
            flipped[i * n : (i + 1) * n, :] = ref[...].T
        store_grads(meta, pieces, 0, flipped, attn_ref, True)

    piece = VMEM((2, 2, 4, 2, width // 8, 128), BF)
    return call(
        kernel,
        meta,
        [(a, None) for a in (cot, small, middle, hidden, *mixed)] + [(p, ANY) for p in parts],
        [(VMEM((rows, width), BF), None), (piece, None), (piece, None), (shaped(F32, 8, width), None)],
        20,
        cost(4 * rows * width * width, 2 * 12 * rows * width),
        "feed_forward_third",
        [
            pltpu.VMEM((width, width), BF),
            pltpu.VMEM((width, rows), BF),
            pltpu.SemaphoreType.DMA,
        ],
    )


def mixed_grad(meta, grad_attn, parts):
    rows, width = grad_attn.shape
    parts, starts = zip(*parts)
    count = len(parts)

    def kernel(meta, attn_ref, *refs):
        parts, (grad_ref, attn_out, whole, sems) = refs[:count], refs[count:]
        write = pltpu.make_async_copy(attn_ref, attn_out, sems.at[1])
        write.start()
        fetch(meta, parts, starts, whole, (0, width), sems.at[0])
        fetched(whole, (0, width), sems.at[0])

        @blocks(rows)
        def _(here, _):
            grad_ref[here, :] = dot(attn_ref[here, :], whole[...], NT).astype(BF)

        write.wait()

    return call(
        kernel,
        meta,
        [(grad_attn, None)] + [(p, ANY) for p in parts],
        [(VMEM((rows, width), BF), None), (HBM((rows, width), BF), ANY)],
        16,
        cost(2 * rows * width * width, 2 * 4 * rows * width),
        "mixed_grad",
        [pltpu.VMEM((width, width), BF), pltpu.SemaphoreType.DMA((2,))],
    )


def attention_backward(meta, first, packed, probs, grad_mixed, mixed, base, half, images, odd):
    rows, width = first.shape
    length, n = rows // images, 3 * SIZE
    pair = GROUP // 2

    def kernel(
        meta, first_ref, packed_ref, probs_ref, grad_ref, mixed_ref, grad_packed_ref, piece_ref
    ):
        j = pl.program_id(0)
        head = meta[half] * pair + j

        @pl.loop(0, images)
        def _(i):
            here = span(i, length)
            packed = packed_ref[here, :]
            q, k, v = packed[:, :SIZE], packed[:, SIZE : 2 * SIZE], packed[:, 2 * SIZE :]
            grad = grad_ref[here, span(base + head, SIZE)]
            mixed = mixed_ref[here, span(head, SIZE)]
            inner = jnp.sum(grad.astype(F32) * mixed.astype(F32), axis=-1, keepdims=True)
            probs = probs_ref[0, i]
            grad_v = dot(probs, grad, TN)
            grad_scores = (probs.astype(F32) * (dot(grad, v, NT) - inner)).astype(BF)
            grad_q = dot(grad_scores, k) * SCALE
            grad_k = dot(grad_scores, q, TN) * SCALE
            grad_packed_ref[here, :] = jnp.concatenate(
                [grad_q.astype(BF), grad_k.astype(BF), grad_v.astype(BF)], axis=1
            )

        values = dot(first_ref[...], grad_packed_ref[...], TN)
        store_piece(meta[half], odd, piece_ref, 0, values, j)

    return call(
        kernel,
        meta,
        [
            (first, None),
            (hbm(packed), pl.BlockSpec((rows, n), lambda j, m: (0, m[half] * pair + j))),
            (
                hbm(probs),
                pl.BlockSpec(
                    (1, images, length, length), lambda j, m: (m[half] * pair + j, 0, 0, 0)
                ),
            ),
            (grad_mixed, None),
            (mixed, None),
        ],
        [
            (HBM((rows, pair * n), BF), pl.BlockSpec((rows, n), lambda j, m: (0, j))),
            (VMEM((2, 2, 4, 3, width // 8, SIZE), BF), None),
        ],
        20,
        cost(
            pair * (2 * rows * width * n * 1.5 + 10 * rows * length * SIZE * 1.5),
            2 * (rows * width + pair * (rows * length + 3 * rows * n)),
        ),
        "attention_backward",
        grid=(pair,),
    )


def input_grad(meta, x, grad_attn, small, pieces, weights):
    rows, width = x.shape
    tm = min(256, rows)
    groups = len(weights)
    n = pieces[0].shape[1]

    def kernel(meta, x_ref, grad_ref, small_ref, *refs):
        pieces, weights = refs[: 2 * groups], refs[2 * groups : 3 * groups]
        out_ref, sums_ref, packed_sums_ref = refs[3 * groups :]

        @pl.when(pl.program_id(0) == 0)
        def _():
            sums_ref[...] = jnp.zeros_like(sums_ref)
            packed_sums_ref[...] = jnp.zeros_like(packed_sums_ref)

        grad = None
        for g in range(groups):
            for j, which in enumerate((THEIRS, OURS)):
                piece = pieces[2 * g + j][...]
                term = dot(piece, weights[g][:, span(meta[which], n)], NT)
                grad = term if grad is None else grad + term
                packed_sums_ref[0:1, span(2 * g + meta[which], n)] += column_sum(piece)
        normed, scale = normed_rows(x_ref[...].astype(F32))
        back = norm_back(grad * small_ref[G1 : G1 + 1, :], normed, scale)
        out_ref[...] = (grad_ref[...].astype(F32) + back).astype(BF)
        sums_ref[0:1, :] += column_sum(grad * normed)
        sums_ref[1:2, :] += column_sum(grad)

    block = pl.BlockSpec((tm, width), lambda i, m: (i, 0))
    return call(
        kernel,
        meta,
        [(hbm(x), block), (hbm(grad_attn), block), (small, None)]
        + [(hbm(p), pl.BlockSpec((tm, n), lambda i, m: (i, 0))) for p in pieces]
        + [(w, None) for w in weights],
        [
            (HBM((rows, width), BF), block),
            (shaped(F32, 8, width), None),
            (shaped(F32, 8, 3 * width), None),
        ],
        24,
        cost(6 * rows * width * width * 1.3, 2 * 9 * rows * width),
        "input_grad",
        grid=(rows // tm,),
    )


def quarter_of(meta, i):
    return (meta[CORE] ^ (i % 2)) * 2 + (meta[YPOS] ^ (i // 2))


def finish(meta, groups, places, widths, name):
    quarters = [q for group in groups for q in group]
    rows = quarters[0].shape[1]

    def kernel(meta, *refs):
        outs = refs[len(quarters) :]
        for g, place in enumerate(places):
            for i in range(4):
                part = refs[4 * g + i]
                for j in range(min(part.shape[0], len(widths) * widths[0] // 128 // 4 // len(groups))):
                    which, column = place(quarter_of(meta, i), j)
                    outs[which][:, span(column, 128)] = part[j].astype(F32)

    outs = [(shaped(F32, rows, n), None) for n in widths]
    return call(kernel, meta, [(a, None) for a in quarters], outs, 8, cost(1, 1), name)


def by_head(weight, base):
    rows = weight.shape[0]
    view = weight.reshape(rows, 3, HEADS, SIZE)[:, :, base : base + GROUP]
    return view.transpose(0, 2, 1, 3).reshape(rows, GROUP * 3 * SIZE)


def per_device(latents, w_qkv, w_out, w_up, w_down, gains, biases, ff_bias, cotangent, *, nb, nr):
    reps, images, length, width = latents.shape
    x = latents.reshape(-1, width)
    cot = cotangent.reshape(-1, width)
    count = reps * images
    bases = range(0, HEADS, GROUP)
    native = nb != 8 or nr != 4
    small = jnp.concatenate([gains, biases, ff_bias[None]], axis=0)
    small = jnp.pad(small, ((0, 16 - small.shape[0]), (0, 0)))
    if native:
        links = None
        zero = jnp.zeros((), jnp.int32)
        meta = jnp.stack([zero, zero, zero, zero, zero + 1, zero, zero, zero])

        def whole(w):
            return [(lax.all_gather(w, "batch", axis=0, tiled=True), 0)]

        table = lax.all_gather(small, "batch", axis=1, tiled=True)
        table = table.reshape(16, 4, 2, width // 8).transpose(2, 1, 0, 3)
        first, small = first_norm(meta, x, [table[0], table[1], table[1]])
        chunks = [whole(by_head(w_qkv, base)) for base in bases]
        chunks += [whole(jnp.concatenate([w_out, w_up], axis=1)), whole(w_down)]
    else:
        links = Links(nb, nr)
        mine_f = jnp.where(links.ci == 0, links.xi, links.yi)
        mine_s = jnp.where(links.ci == 0, links.yi, links.xi)
        meta = [links.ci, links.yi, links.xi, links.zi, 1 - links.ci, links.ci, mine_f, mine_s]
        meta = jnp.stack(meta).astype(jnp.int32)

        def quarter(w):
            rows = w.shape[0] // 4
            return lax.dynamic_slice_in_dim(w, (links.ci * 2 + links.yi) * rows, rows, 0)

        w_qkv = quarter(w_qkv)
        chunks = [by_head(w_qkv, base) for base in bases]
        extra = jnp.pad(small, ((0, w_qkv.shape[0] - 16), (0, 0)))
        chunks[0] = jnp.concatenate([chunks[0], extra], axis=1)
        chunks += [jnp.concatenate([quarter(w_out), quarter(w_up)], axis=1), quarter(w_down)]
        other = CoreSwap(links)

        def visit(i, chunks):
            if i == 0:
                return ()
            if i == 1:
                kept.extend(first_norm(meta, x, [part for part, _ in chunks[0][:3]]))
                return kept + other.early(chunks[0], 3)
            return other.early(chunks[i - 1], 2) + forward(i - 2, chunks[i - 2])

    packed, probs, mixed, weights, kept = [], [], [], [], []

    def forward(i, parts):
        parts = parts if native else other(parts, *mixed)
        a, b, c, d = attention_forward(meta, kept[0], kept[1], parts, bases[i], count)
        packed.append(a)
        probs.append(b)
        mixed.append(c)
        weights.append(d)
        return [c]

    if native:
        kept.extend((first, small))
        for i in range(len(bases)):
            forward(i, chunks[i])
    else:
        chunks = gather_chunks(chunks, links, visit)
        for i in range(len(mixed), len(bases)):
            forward(i, chunks[i])
        first, small = kept
    outer, inner = chunks[len(bases) :]
    outer = outer if native else other(outer, mixed[1])
    middle, second, active, slope = feed_forward_first(meta, x, small, mixed, outer)
    inner = inner if native else other(inner, mixed[1])
    out, hidden, send, keep, sums_two = feed_forward_second(
        meta, cot, small, middle, second, active, slope, inner
    )
    grad_attn, send_out, keep_out, sums_three = feed_forward_third(
        meta, cot, small, middle, mixed, hidden, outer
    )

    def backward(meta, g, half):
        return attention_backward(
            meta, first, packed[g], probs[g], grad_mixed, mixed[g], bases[g], half, count, g == 1
        )

    def collect(sums_one, sums_packed):
        sums_packed = sums_packed[0].reshape(HEADS, 3, SIZE)
        sums_q, sums_v = sums_packed[:, 0].reshape(width), sums_packed[:, 2].reshape(width)
        out, two, three = sums_three[2], sums_two, sums_three
        rows = [sums_one[0], three[0], sums_one[1], sums_q, sums_v, out, three[1], two[1], two[0]]
        return jnp.stack(rows)

    def sums_of(sums_one, sums_packed):
        two, three, one, packed = sums_two, sums_three, sums_one, sums_packed
        plain = [(one, 0), (three, 0), (one, 1), None, None, (three, 2), (three, 1), (two, 1), (two, 0)]
        sums = [entry and (*entry, 1, 0) for entry in plain]
        sums[3], sums[4] = (packed, 0, 3, 0), (packed, 0, 3, 2)
        return sums

    def result(grad_x, grads, smalls):
        return (
            out.reshape(latents.shape),
            grad_x.reshape(latents.shape),
            *grads,
            smalls[:2],
            smalls[2:8],
            smalls[8],
        )

    if native:
        grad_mixed, grad_attn = mixed_grad(meta, grad_attn, outer)
        halves = [[backward(meta, g, half) for half in (THEIRS, OURS)] for g in range(len(bases))]
        pieces = [half[0] for pair in halves for half in pair]
        grad_x, sums_one, sums_packed = input_grad(meta, x, grad_attn, small, pieces, weights)
        smalls = lax.psum_scatter(
            collect(sums_one, sums_packed), "batch", scatter_dimension=1, tiled=True
        )
        smalls = lax.psum(smalls, "rep")

        def reduced(send, keep, odd):
            keep, send = (jnp.swapaxes(keep, 0, 1), send) if odd else (keep, jnp.swapaxes(send, 0, 1))
            both = jnp.stack([keep, send])
            t = both.shape[4]
            both = both.transpose(3, 1, 5, 0, 2, 4, 6).reshape(width, t * 4 * 128)
            both = lax.psum_scatter(both, "batch", scatter_dimension=0, tiled=True)
            both = lax.psum(both.astype(BF), "rep").astype(F32)
            return both.reshape(-1, 4, t, 128)

        rest = [reduced(send_out, keep_out, True), reduced(send, keep, False)]
        rows = rest[0].shape[0]
        rest = [rest[0], rest[1][:, :, 2:], rest[1][:, :, :2]]
        rest = [g.reshape(rows, width) for g in rest]
        heads = [reduced(pair[0][1], pair[1][1], g == 1) for g, pair in enumerate(halves)]
        heads = jnp.concatenate(heads, axis=1).transpose(0, 2, 1, 3).reshape(rows, 3 * width)
        return result(grad_x, [heads, *rest], smalls)

    def to_core(value):
        return move(value, links.core)

    def along(arrays):
        return [arrays[0]] + [move(a, p) for a, p in zip(arrays[1:], links.z)]

    def share(value):
        return [value] + [move(value, p) for p in links.rep]

    both = Piece(keep, to_core(send), False)
    step = Step()
    step.swap(firsts=[both])
    (sent,) = step.run(after(meta, keep_out), "step_0")
    both.late.append((move(sent, links.x_or_y), 0))
    grad_mixed, grad_attn = mixed_grad(after(meta, sent), grad_attn, outer)
    packed_1, send_1 = backward(after(meta, sent), 0, THEIRS)

    outs = Piece(keep_out, to_core(send_out), True)
    step = Step()
    step.swap(firsts=[outs], seconds=[both])
    (sent,) = step.run(after(meta, send_1), "step_1")
    moved = move(sent, links.y_or_x)
    for piece in (outs, both):
        piece.late.append((moved, piece.next))
    packed_2, keep_1 = backward(after(meta, sent), 0, OURS)
    packed_3, send_2 = backward(after(meta, sent, keep_1), 1, THEIRS)

    one = Piece(keep_1, to_core(send_1), False)
    step = Step()
    step.swap(firsts=[one], seconds=[outs])
    step.along(both)
    sent, *z_both = step.run(after(meta, send_2), "step_2")
    moved = move(sent, links.x_or_y)
    for piece in (one, outs):
        piece.late.append((moved, piece.next))
    z_both = along(z_both)
    packed_4, keep_2 = backward(after(meta, sent), 1, OURS)

    two = Piece(keep_2, to_core(send_2), True)
    step = Step()
    step.swap(firsts=[two], seconds=[one])
    step.along(outs)
    sent, *z_outs = step.run(after(meta, keep_2, *z_both[1:]), "step_3")
    moved = move(sent, links.y_or_x)
    for piece in (two, one):
        piece.late.append((moved, piece.next))
    z_outs = along(z_outs)
    pieces = [packed_1, packed_2, packed_3, packed_4]
    grad_x, sums_one, sums_packed = input_grad(
        after(meta, sent), x, grad_attn, small, pieces, weights
    )

    step = Step()
    step.swap(seconds=[two])
    step.along(one, sums_of(sums_one, sums_packed))
    step.share([z_both, z_outs])
    sent, *z_one, r_rest = step.run(after(meta, grad_x), "step_4")
    two.late.append((move(sent, links.x_or_y), 0))
    z_one, r_rest = along(z_one), share(r_rest)

    step = Step()
    step.along(two)
    step.share([z_one])
    *z_two, r_one = step.run(meta, "step_5")
    z_two, r_one = along(z_two), share(r_one)

    step = Step()
    step.share([z_two])
    step.small(r_one)
    r_two, other, smalls = step.run(meta, "step_6")
    smalls = smalls + move(other, links.x)
    rest = finish(
        after(meta, r_two),
        [r_rest],
        [lambda q, j: (2 - j // 2, q * 2 + j % 2)],
        [width] * 3,
        "finish_rest",
    )
    (heads,) = finish(
        meta,
        [r_one, share(r_two)],
        [lambda q, j: (0, j * HEADS + q), lambda q, j: (0, j * HEADS + GROUP + q)],
        [3 * width],
        "finish_heads",
    )
    return result(grad_x, [heads, *rest], smalls)


def solution(mesh):
    nb, nr = mesh.shape["batch"], mesh.shape["rep"]

    def body(*args):
        return per_device(*args, nb=nb, nr=nr)

    rows = P("batch", None)
    cols = P(None, "batch")
    data = P("rep", "batch", None, None)
    return jax.shard_map(
        body,
        mesh=mesh,
        in_specs=(data, rows, rows, rows, rows, cols, cols, P("batch"), data),
        out_specs=(data, data, rows, rows, rows, rows, cols, cols, P("batch")),
        check_vma=False,
    )
```

```python
import functools

import jax
import jax.numpy as jnp
from jax import lax
from jax.experimental import pallas as pl
from jax.experimental.pallas import tpu as pltpu
from jax.sharding import PartitionSpec as P

HEADS = 8
SIZE = 128
GROUP = 4
EPS = 1e-05
AXES = ("batch", "rep")
BF = jnp.bfloat16
F32 = jnp.float32
NN, NT, TN = ((1,), (0,)), ((1,), (1,)), ((0,), (0,))
SCALE = SIZE ** (-0.5)
LOG2E = 1.4426950408889634
GELU = 0.7978845608028654
CUBIC = 0.044715
G1, G2, B1, BQ, BV, BO, B2, BD, BU = range(9)
CORE, YPOS, XPOS, ZPOS, THEIRS, OURS, MINE_F, MINE_S = range(8)


def dot(a, b, dims=NN):
    return lax.dot_general(a, b, (dims, ((), ())), preferred_element_type=F32)


HBM, VMEM = pltpu.HBM, pltpu.VMEM
ANY = pl.BlockSpec(memory_space=pl.ANY)


def call(kernel, meta, operands, outs, limit, estimate, name, scratch=(), grid=(1,)):
    shapes = [shape for shape, _ in outs]
    return pl.pallas_call(
        kernel,
        out_shape=shapes,
        grid_spec=pltpu.PrefetchScalarGridSpec(
            num_scalar_prefetch=1,
            grid=grid,
            in_specs=[spec or full(a) for a, spec in operands],
            out_specs=[spec or full(a) for a, spec in outs],
            scratch_shapes=scratch,
        ),
        compiler_params=pltpu.CompilerParams(vmem_limit_bytes=limit << 20),
        cost_estimate=estimate,
        name=name,
    )(meta, *[a for a, _ in operands])


def hbm(array):
    return pltpu.with_memory_space_constraint(array, HBM)


def shaped(dtype, *shape):
    return jax.ShapeDtypeStruct(shape, dtype)


def span(index, size):
    return pl.ds(pl.multiple_of(index * size, size), size)


def cost(flops, nbytes, trans=0):
    return pl.CostEstimate(flops=1, bytes_accessed=1, transcendentals=0)


def full(array):
    rank = len(array.shape)
    return pl.BlockSpec(array.shape, lambda *_: (0,) * rank)


def column_sum(values):
    return jnp.sum(values.astype(F32), axis=0, keepdims=True)


def permutation(target, nb, nr):
    pairs = []
    for b in range(nb):
        for r in range(nr):
            tb, tr = target(b, r)
            pairs.append((b * nr + r, tb * nr + tr))
    return pairs


class Links:
    def __init__(self, nb, nr):
        def swap(kb, kr):
            return permutation(lambda b, r: (b ^ kb, r ^ kr), nb, nr)

        self.core = swap(0, 1)
        self.rep = [swap(0, 1), swap(0, 2), swap(0, 3)]
        self.x = swap(1, 0)
        self.y = swap(0, 2)
        self.z = [swap(2, 0), swap(4, 0), swap(6, 0)]
        self.y_or_x = permutation(lambda b, r: (b, r ^ 2) if r % 2 == 0 else (b ^ 1, r), nb, nr)
        self.x_or_y = permutation(lambda b, r: (b ^ 1, r) if r % 2 == 0 else (b, r ^ 2), nb, nr)
        batch, rep = lax.axis_index("batch"), lax.axis_index("rep")
        self.xi, self.zi = batch % 2, batch // 2
        self.ci, self.yi = rep % 2, rep // 2


def move(value, pairs):
    return lax.ppermute(value, AXES, pairs)


def flip_if(bit, value, axis):
    return jnp.where(bit == 1, jnp.flip(value, axis), value)


def pick(value, axis, index):
    return lax.dynamic_index_in_dim(value, index, axis, keepdims=False)


def after(value, *others):
    return lax.optimization_barrier((value, *others))[0]


def gather_chunks(quarters, links, visit):
    chunks = []
    along, across = (), ()
    late = None
    for i, quarter in enumerate(quarters):
        quarter = after(quarter, *along)
        along = [move(quarter, p) for p in links.z]
        ahead = quarters[1:] if i == 0 else ()
        own = jnp.stack([after(quarter, *across, *ahead)] + along)
        first = move(own, links.y_or_x)
        both = own if late is None else jnp.concatenate([late, own], axis=2)
        both = move(both, links.x_or_y)
        if late is not None:
            chunks[-1].append((both, 0))
        chunks.append([(own, 0), (first, 0), (both, 0 if late is None else late.shape[2])])
        late = first
        across = (both, *visit(i, chunks))
    chunks[-1].append((move(after(late, *across[1:]), links.x_or_y), 0))
    return chunks


class CoreSwap:
    def __init__(self, links):
        self.pairs, self.moved = links.core, {}

    def __call__(self, chunk, *gates):
        for part, _ in chunk:
            if id(part) not in self.moved:
                self.moved[id(part)] = move(after(part, *gates), self.pairs)
        return chunk + [(self.moved[id(part)], start) for part, start in chunk]

    def early(self, chunk, count, *gates):
        moved = self(chunk[:count], *gates)
        return [part for part, _ in moved[count:]]


class Piece:
    def __init__(self, keep, other, odd):
        self.terms, self.t = [keep, other], keep.shape[3]
        self.odd = odd
        self.late = []

    def mine(self, meta):
        both = meta[MINE_F], meta[MINE_S]
        return both[::-1] if self.odd else both


class Step:
    def __init__(self):
        self.arrays, self.views, self.jobs, self.outs = [], [], [], []

    def load(self, array, shape, view):
        self.views.append((self.place(array), shape, view))
        return len(self.views) - 1

    def place(self, array):
        for i, known in enumerate(self.arrays):
            if known is array:
                return i
        self.arrays.append(array)
        return len(self.arrays) - 1

    def out(self, shape, dtype):
        self.outs.append((shaped(dtype, *shape), None))
        return len(self.outs) - 1

    def swap(self, firsts=(), seconds=()):
        at = 0
        out = len(self.outs)
        for piece in seconds:
            self.second(piece, out, at)
            piece.next, at = at, at + 4 * piece.t
        for piece in firsts:
            self.first(piece, out, at)
            piece.next, at = at, at + 8 * piece.t
        self.out((at, 128, 128), BF)

    def first(self, piece, out, at):
        def view(ref, meta):
            return ref.at[1 - piece.mine(meta)[0]]

        loads = [self.load(a, a.shape[1:], view) for a in piece.terms]
        n = 8 * piece.t

        def job(meta, got, outs):
            values = sum(got[i][...].astype(F32) for i in loads)
            outs[out][at : at + n] = values.astype(BF).reshape(n, 128, 128)

        self.jobs.append((job, len(self.views)))

    def second(self, piece, out, at):
        n = 4 * piece.t
        ((late, start),) = piece.late

        def view(ref, meta):
            f, s = piece.mine(meta)
            return ref.at[f, 1 - s]

        def late_view(ref, meta):
            return ref.at[pl.ds(start + (1 - piece.mine(meta)[1]) * n, n)]

        loads = [self.load(a, a.shape[2:], view) for a in piece.terms]
        loads.append(self.load(late, (n, 128, 128), late_view))

        def job(meta, got, outs):
            values = sum(got[i][...].reshape(n, 128, 128).astype(F32) for i in loads)
            outs[out][at : at + n] = values.astype(BF)

        self.jobs.append((job, len(self.views)))

    def along(self, piece, sums=()):
        t = piece.t
        (one, start_one), (two, start_two) = piece.late

        def view(ref, meta):
            f, s = piece.mine(meta)
            return ref.at[f, s]

        def view_one(ref, meta):
            return ref.at[pl.ds(start_one + piece.mine(meta)[1] * 4 * t, 4 * t)]

        def view_two(ref, meta):
            return ref.at[pl.ds(start_two, 4 * t)]

        loads = [self.load(a, a.shape[2:], view) for a in piece.terms]
        late = [self.load(one, (4 * t, 128, 128), view_one)]
        late.append(self.load(two, (4 * t, 128, 128), view_two))
        extra = [
            (self.load(a, a.shape, lambda ref, meta: ref), row, scale, shift)
            for a, row, scale, shift in sums
        ]
        out = len(self.outs)
        for k in range(4):
            self.out((t + bool(sums), 128, 128), BF if k else F32)

        def job(meta, got, outs):
            for k in range(4):
                z = meta[ZPOS] ^ k
                dtype = BF if k else F32
                values = sum(got[i][z].astype(F32) for i in loads)
                values += sum(got[i][pl.ds(z * t, t)].astype(F32) for i in late)
                outs[out + k][:t] = values.astype(dtype)
                if extra:
                    outs[out + k][t] = jnp.zeros((128, 128), dtype)
                    for x in range(2):
                        rows = [
                            got[i][row : row + 1, span((z * 2 + x) * scale + shift, 128)]
                            for i, row, scale, shift in extra
                        ]
                        rows += [jnp.zeros((16 - len(rows), 128), F32)]
                        rows = jnp.concatenate(rows, axis=0).astype(dtype)
                        outs[out + k][t, 16 * x : 16 * x + 16] = rows

        self.jobs.append((job, len(self.views)))

    def share(self, groups):
        loads = [
            [self.load(a, a.shape, lambda ref, meta: ref) for a in arrays] for arrays in groups
        ]
        sizes = [arrays[0].shape[0] for arrays in groups]
        out = self.out((sum(sizes), 128, 128), BF)

        def job(meta, got, outs):
            at = 0
            for slots, size in zip(loads, sizes):
                outs[out][at : at + size] = sum(got[i][...].astype(F32) for i in slots).astype(BF)
                at += size

        self.jobs.append((job, len(self.views)))

    def small(self, arrays):
        tile = arrays[0].shape[0] - 1
        loads = [self.load(a, (128, 128), lambda ref, meta: ref.at[tile]) for a in arrays]
        out = self.out((16, 128), F32)
        self.out((16, 128), F32)

        def job(meta, got, outs):
            for k in range(2):
                rows = span(meta[XPOS] if k else 1 - meta[XPOS], 16)
                outs[out + k][...] = sum(got[i][rows, :].astype(F32) for i in loads)

        self.jobs.append((job, len(self.views)))

    def run(self, meta, name):
        count, total = len(self.arrays), len(self.outs)

        def kernel(meta, *refs):
            outs, got, sems = refs[count : count + total], refs[count + total : -1], refs[-1]
            copies = [
                pltpu.make_async_copy(view(refs[i], meta), got[j], sems.at[j])
                for j, (i, _, view) in enumerate(self.views)
            ]
            for copy in copies:
                copy.start()
            ready = 0
            for job, last in self.jobs:
                for copy in copies[ready:last]:
                    copy.wait()
                ready = last
                job(meta, got, outs)

        return call(
            kernel,
            meta,
            [(a, ANY) for a in self.arrays],
            self.outs,
            12,
            cost(1, 1),
            name,
            [pltpu.VMEM(shape, self.arrays[i].dtype) for i, shape, _ in self.views]
            + [pltpu.SemaphoreType.DMA((len(self.views),))],
        )


def fetch(meta, parts, starts, whole, columns, sem, skip=0):
    first, n = columns
    if len(parts) == 1:
        source = parts[0].at[:, pl.ds(skip + first, n)]
        pltpu.make_async_copy(source, whole.at[:, pl.ds(first, n)], sem).start()
        return
    core, y, x, z = meta[CORE], meta[YPOS], meta[XPOS], meta[ZPOS]
    for i, (part, start) in enumerate(zip(parts, starts)):
        source = core if i < 4 else 1 - core
        dx = (0, source, 1 - source, 1)[i % 4]
        dy = (0, 1 - source, source, 1)[i % 4]
        for dz in range(4):
            block = (((z ^ dz) * 2 + (x ^ dx)) * 2 + source) * 2 + (y ^ dy)
            pltpu.make_async_copy(
                part.at[dz, :, pl.ds(start + skip + first, n)],
                whole.at[span(block, part.shape[1]), pl.ds(first, n)],
                sem,
            ).start()


def fetched(whole, columns, sem):
    first, n = columns
    here = whole.at[:, pl.ds(first, n)]
    pltpu.make_async_copy(here, here, sem).wait()


def normed_rows(values):
    centred = values - jnp.mean(values, axis=-1, keepdims=True)
    scale = lax.rsqrt(jnp.mean(centred * centred, axis=-1, keepdims=True) + EPS)
    return centred * scale, scale


def norm_back(grad, normed, scale):
    mean_one = jnp.mean(grad, axis=-1, keepdims=True)
    mean_two = jnp.mean(grad * normed, axis=-1, keepdims=True)
    return scale * (grad - mean_one - normed * mean_two)


def first_norm(meta, x, tables):
    rows, width = x.shape
    tm = 256
    last = tables[0].shape[2] - 128

    def kernel(meta, x_ref, *refs):
        parts, (first_ref, small_ref, table, sems) = refs[:3], refs[3:]
        copies = [
            pltpu.make_async_copy(ref.at[:, pl.ds(0, 16), pl.ds(last, 128)], table.at[i], sems.at[i])
            for i, ref in enumerate(parts)
        ]
        for copy in copies:
            copy.start()
        for copy in copies:
            copy.wait()
        x, z = meta[XPOS], meta[ZPOS]
        for dz in range(4):
            own, one, two = (table[i, dz].astype(F32) for i in range(3))
            for dx, values in enumerate((own, jnp.where(meta[CORE] == 1, one, two))):
                small_ref[:, span((z ^ dz) * 2 + (x ^ dx), 128)] = values

        @pl.loop(0, rows // tm)
        def _(i):
            normed, _ = normed_rows(x_ref[span(i, tm), :].astype(F32))
            first = normed * small_ref[G1 : G1 + 1, :] + small_ref[B1 : B1 + 1, :]
            first_ref[span(i, tm), :] = first.astype(BF)

    return call(
        kernel,
        meta,
        [(x, None)] + [(a, ANY) for a in tables],
        [(VMEM((rows, width), BF), None), (shaped(F32, 16, width), None)],
        16,
        cost(rows * width * 20, rows * width * 4),
        "first_norm",
        [pltpu.VMEM((3, 4, 16, 128), BF), pltpu.SemaphoreType.DMA((3,))],
    )


def attention_forward(meta, first, small, parts, base, images):
    rows, width = first.shape
    length, n = rows // images, 3 * SIZE
    parts, starts = zip(*parts)
    count = len(parts)
    columns = (0, GROUP * n)

    def kernel(meta, first_ref, small_ref, *refs):
        parts, refs = refs[:count], refs[count:]
        packed_ref, probs_ref, mixed_ref, weight_out, weight_ref, sems = refs
        head = pl.program_id(0)
        keep = pltpu.make_async_copy(weight_ref, weight_out, sems.at[1])

        @pl.when(head == 0)
        def _():
            fetch(meta, parts, starts, weight_ref, columns, sems.at[0])
            fetched(weight_ref, columns, sems.at[0])
            keep.start()

        here = span(base + head, SIZE)
        bias_q, bias_v = small_ref[BQ : BQ + 1, here], small_ref[BV : BV + 1, here]
        bias = jnp.concatenate([bias_q, jnp.zeros_like(bias_q), bias_v], axis=1)
        packed = (dot(first_ref[...], weight_ref[:, span(head, n)]) + bias).astype(BF)
        packed_ref[...] = packed
        for i in range(images):
            part = packed[i * length : (i + 1) * length]
            q, k, v = part[:, :SIZE], part[:, SIZE : 2 * SIZE], part[:, 2 * SIZE :]
            scores = dot(q, k, NT)
            top = jnp.max(scores, axis=-1, keepdims=True)
            raised = jnp.exp2((scores - top) * (SCALE * LOG2E))
            probs = raised * (1.0 / jnp.sum(raised, axis=-1, keepdims=True))
            probs = probs.astype(BF)
            probs_ref[0, i] = probs
            mixed_ref[i * length : (i + 1) * length, span(head, SIZE)] = dot(probs, v).astype(BF)

        @pl.when(head == GROUP - 1)
        def _():
            keep.wait()

    return call(
        kernel,
        meta,
        [(first, None), (small, None)] + [(p, ANY) for p in parts],
        [
            (HBM((rows, GROUP * n), BF), pl.BlockSpec((rows, n), lambda h, m: (0, h))),
            (
                HBM((GROUP, images, length, length), BF),
                pl.BlockSpec((1, images, length, length), lambda h, m: (h, 0, 0, 0)),
            ),
            (VMEM((rows, GROUP * SIZE), BF), None),
            (HBM((width, GROUP * n), BF), ANY),
        ],
        20,
        cost(
            2 * rows * width * GROUP * n * 2 + 8 * rows * length * SIZE * GROUP,
            2 * (rows * width + width * n * GROUP * 2 + rows * n * GROUP + GROUP * rows * length),
            GROUP * rows * length,
        ),
        "attention_forward",
        [pltpu.VMEM((width, GROUP * n), BF), pltpu.SemaphoreType.DMA((2,))],
        (GROUP,),
    )


def store_piece(owner, odd, piece_ref, at, values, y):
    rows = values.shape[0] // 8
    for z in range(4):
        for x in range(2):
            plain = owner == (1 if odd else 0)
            first = jnp.where(plain, x, y)
            second = jnp.where(plain, y, x)
            start = (z * 2 + x) * rows
            for j in range(values.shape[1] // 128):
                part = values[start : start + rows, j * 128 : (j + 1) * 128]
                piece_ref[first, second, z, at + j] = part.astype(BF)


def blocks(rows):
    size = min(256, rows)

    def over(body):
        pl.loop(0, rows // size)(lambda i: body(span(i, size), i))

    return over


def feed_forward_first(meta, x, small, mixed, parts):
    rows, width = x.shape
    parts, starts = zip(*parts)
    count = len(parts)

    def kernel(meta, x_ref, small_ref, *refs):
        mixed_refs, parts = refs[: len(mixed)], refs[len(mixed) : len(mixed) + count]
        middle_ref, second_ref, active_ref, slope_ref, whole, sems = refs[len(mixed) + count :]
        for j in range(2):
            fetch(meta, parts, starts, whole, (j * width, width), sems.at[j])

        def row(r):
            return small_ref[r : r + 1, :]

        fetched(whole, (0, width), sems.at[0])

        @blocks(rows)
        def _(here, i):
            values = jnp.concatenate([r[here, :] for r in mixed_refs], axis=1)
            middle = x_ref[here, :].astype(F32) + dot(values, whole[:, :width]) + row(BO)
            middle_ref[here, :] = middle
            normed, _ = normed_rows(middle)
            second = (normed * row(G2) + row(B2)).astype(BF)
            second_ref[here, :] = second

            @pl.when(i == 0)
            def _():
                fetched(whole, (width, width), sems.at[1])

            v = dot(second, whole[:, width:]) + row(BU)
            square = v * v
            half = 0.5 * jnp.tanh(v * (GELU + (GELU * CUBIC) * square)) + 0.5
            active = v * half
            active_ref[here, :] = active.astype(BF)
            slope = (1.0 - half) * active * (2 * GELU + (6 * GELU * CUBIC) * square)
            slope_ref[here, :] = (half + slope).astype(BF)

    return call(
        kernel,
        meta,
        [(x, None), (small, None)] + [(a, None) for a in mixed] + [(p, ANY) for p in parts],
        [
            (VMEM((rows, width), F32), None),
            (VMEM((rows, width), BF), None),
            (VMEM((rows, width), BF), None),
            (VMEM((rows, width), BF), None),
        ],
        24,
        cost(4 * rows * width * width, 2 * 9 * rows * width, rows * width),
        "feed_forward_first",
        [pltpu.VMEM((width, 2 * width), BF), pltpu.SemaphoreType.DMA((2,))],
    )


def store_grads(meta, pieces, m, left_ref, right_ref, odd):
    q = right_ref.shape[1] // 4

    @pl.loop(0, 4)
    def _(j):
        core, y = j // 2, j % 2
        values = dot(left_ref[...], right_ref[:, span(j, q)]).astype(BF)
        for piece_ref, half in zip(pieces, (THEIRS, OURS)):

            @pl.when(core == meta[half])
            def _(piece_ref=piece_ref):
                store_piece(core, odd, piece_ref, 2 * m, values, y)


def feed_forward_second(meta, cot, small, middle, second, active, slope, parts):
    rows, width = cot.shape
    parts, starts = zip(*parts)
    count = len(parts)

    def kernel(meta, cot_ref, small_ref, middle_ref, second_ref, active_ref, slope_ref, *refs):
        parts, refs = refs[:count], refs[count:]
        out_ref, hidden_ref, *pieces, sums_ref, whole, out, flipped, sems = refs
        fetch(meta, parts, starts, whole, (0, width), sems.at[0])
        flipped[...] = active_ref[...].T
        store_grads(meta, pieces, 0, flipped, cot_ref, False)
        fetched(whole, (0, width), sems.at[0])

        @blocks(rows)
        def _(here, _):
            grad = dot(cot_ref[here, :], whole[...], NT)
            hidden_ref[here, :] = (slope_ref[here, :].astype(F32) * grad).astype(BF)

        @blocks(rows)
        def _(here, _):
            values = middle_ref[here, :] + dot(active_ref[here, :], whole[...])
            out[here, :] = (values + small_ref[BD : BD + 1, :]).astype(BF)

        write = pltpu.make_async_copy(out, out_ref, sems.at[1])
        write.start()
        flipped[...] = second_ref[...].T
        store_grads(meta, pieces, 1, flipped, hidden_ref, False)
        sums_ref[...] = jnp.zeros_like(sums_ref)
        sums_ref[0:1, :] = column_sum(hidden_ref[...])
        sums_ref[1:2, :] = column_sum(cot_ref[...])
        write.wait()

    piece = VMEM((2, 2, 4, 4, width // 8, 128), BF)
    return call(
        kernel,
        meta,
        [(a, None) for a in (cot, small, middle, second, active, slope)]
        + [(p, ANY) for p in parts],
        [
            (HBM((rows, width), BF), ANY),
            (VMEM((rows, width), BF), None),
            (piece, None),
            (piece, None),
            (shaped(F32, 8, width), None),
        ],
        24,
        cost(8 * rows * width * width, 2 * 12 * rows * width),
        "feed_forward_second",
        [
            pltpu.VMEM((width, width), BF),
            pltpu.VMEM((rows, width), BF),
            pltpu.VMEM((width, rows), BF),
            pltpu.SemaphoreType.DMA((2,)),
        ],
    )


def feed_forward_third(meta, cot, small, middle, mixed, hidden, parts):
    rows, width = cot.shape
    parts, starts = zip(*parts)
    count = len(parts)

    def kernel(meta, cot_ref, small_ref, middle_ref, hidden_ref, *refs):
        mixed_refs, parts = refs[: len(mixed)], refs[len(mixed) : len(mixed) + count]
        attn_ref, *pieces, sums_ref, whole, flipped, sem = refs[len(mixed) + count :]
        fetch(meta, parts, starts, whole, (0, width), sem, width)
        fetched(whole, (0, width), sem)
        sums_ref[...] = jnp.zeros_like(sums_ref)

        @blocks(rows)
        def _(here, _):
            grad_second = dot(hidden_ref[here, :], whole[...], NT)
            normed, scale = normed_rows(middle_ref[here, :])
            back = norm_back(grad_second * small_ref[G2 : G2 + 1, :], normed, scale)
            grad_attn = (cot_ref[here, :].astype(F32) + back).astype(BF)
            attn_ref[here, :] = grad_attn
            sums_ref[0:1, :] += column_sum(grad_second * normed)
            sums_ref[1:2, :] += column_sum(grad_second)
            sums_ref[2:3, :] += column_sum(grad_attn)

        for i, ref in enumerate(mixed_refs):
            n = ref.shape[1]
            flipped[i * n : (i + 1) * n, :] = ref[...].T
        store_grads(meta, pieces, 0, flipped, attn_ref, True)

    piece = VMEM((2, 2, 4, 2, width // 8, 128), BF)
    return call(
        kernel,
        meta,
        [(a, None) for a in (cot, small, middle, hidden, *mixed)] + [(p, ANY) for p in parts],
        [(VMEM((rows, width), BF), None), (piece, None), (piece, None), (shaped(F32, 8, width), None)],
        20,
        cost(4 * rows * width * width, 2 * 12 * rows * width),
        "feed_forward_third",
        [
            pltpu.VMEM((width, width), BF),
            pltpu.VMEM((width, rows), BF),
            pltpu.SemaphoreType.DMA,
        ],
    )


def mixed_grad(meta, grad_attn, parts):
    rows, width = grad_attn.shape
    parts, starts = zip(*parts)
    count = len(parts)

    def kernel(meta, attn_ref, *refs):
        parts, (grad_ref, attn_out, whole, sems) = refs[:count], refs[count:]
        write = pltpu.make_async_copy(attn_ref, attn_out, sems.at[1])
        write.start()
        fetch(meta, parts, starts, whole, (0, width), sems.at[0])
        fetched(whole, (0, width), sems.at[0])

        @blocks(rows)
        def _(here, _):
            grad_ref[here, :] = dot(attn_ref[here, :], whole[...], NT).astype(BF)

        write.wait()

    return call(
        kernel,
        meta,
        [(grad_attn, None)] + [(p, ANY) for p in parts],
        [(VMEM((rows, width), BF), None), (HBM((rows, width), BF), ANY)],
        16,
        cost(2 * rows * width * width, 2 * 4 * rows * width),
        "mixed_grad",
        [pltpu.VMEM((width, width), BF), pltpu.SemaphoreType.DMA((2,))],
    )


def attention_backward(meta, first, packed, probs, grad_mixed, mixed, base, half, images, odd):
    rows, width = first.shape
    length, n = rows // images, 3 * SIZE
    pair = GROUP // 2

    def kernel(
        meta, first_ref, packed_ref, probs_ref, grad_ref, mixed_ref, grad_packed_ref, piece_ref
    ):
        j = pl.program_id(0)
        head = meta[half] * pair + j

        @pl.loop(0, images)
        def _(i):
            here = span(i, length)
            packed = packed_ref[here, :]
            q, k, v = packed[:, :SIZE], packed[:, SIZE : 2 * SIZE], packed[:, 2 * SIZE :]
            grad = grad_ref[here, span(base + head, SIZE)]
            mixed = mixed_ref[here, span(head, SIZE)]
            inner = jnp.sum(grad.astype(F32) * mixed.astype(F32), axis=-1, keepdims=True)
            probs = probs_ref[0, i]
            grad_v = dot(probs, grad, TN)
            grad_scores = (probs.astype(F32) * (dot(grad, v, NT) - inner)).astype(BF)
            grad_q = dot(grad_scores, k) * SCALE
            grad_k = dot(grad_scores, q, TN) * SCALE
            grad_packed_ref[here, :] = jnp.concatenate(
                [grad_q.astype(BF), grad_k.astype(BF), grad_v.astype(BF)], axis=1
            )

        values = dot(first_ref[...], grad_packed_ref[...], TN)
        store_piece(meta[half], odd, piece_ref, 0, values, j)

    return call(
        kernel,
        meta,
        [
            (first, None),
            (hbm(packed), pl.BlockSpec((rows, n), lambda j, m: (0, m[half] * pair + j))),
            (
                hbm(probs),
                pl.BlockSpec(
                    (1, images, length, length), lambda j, m: (m[half] * pair + j, 0, 0, 0)
                ),
            ),
            (grad_mixed, None),
            (mixed, None),
        ],
        [
            (HBM((rows, pair * n), BF), pl.BlockSpec((rows, n), lambda j, m: (0, j))),
            (VMEM((2, 2, 4, 3, width // 8, SIZE), BF), None),
        ],
        20,
        cost(
            pair * (2 * rows * width * n * 1.5 + 10 * rows * length * SIZE * 1.5),
            2 * (rows * width + pair * (rows * length + 3 * rows * n)),
        ),
        "attention_backward",
        grid=(pair,),
    )


def input_grad(meta, x, grad_attn, small, pieces, weights):
    rows, width = x.shape
    tm = min(256, rows)
    groups = len(weights)
    n = pieces[0].shape[1]

    def kernel(meta, x_ref, grad_ref, small_ref, *refs):
        pieces, weights = refs[: 2 * groups], refs[2 * groups : 3 * groups]
        out_ref, sums_ref, packed_sums_ref = refs[3 * groups :]

        @pl.when(pl.program_id(0) == 0)
        def _():
            sums_ref[...] = jnp.zeros_like(sums_ref)
            packed_sums_ref[...] = jnp.zeros_like(packed_sums_ref)

        grad = None
        for g in range(groups):
            for j, which in enumerate((THEIRS, OURS)):
                piece = pieces[2 * g + j][...]
                term = dot(piece, weights[g][:, span(meta[which], n)], NT)
                grad = term if grad is None else grad + term
                packed_sums_ref[0:1, span(2 * g + meta[which], n)] += column_sum(piece)
        normed, scale = normed_rows(x_ref[...].astype(F32))
        back = norm_back(grad * small_ref[G1 : G1 + 1, :], normed, scale)
        out_ref[...] = (grad_ref[...].astype(F32) + back).astype(BF)
        sums_ref[0:1, :] += column_sum(grad * normed)
        sums_ref[1:2, :] += column_sum(grad)

    block = pl.BlockSpec((tm, width), lambda i, m: (i, 0))
    return call(
        kernel,
        meta,
        [(hbm(x), block), (hbm(grad_attn), block), (small, None)]
        + [(hbm(p), pl.BlockSpec((tm, n), lambda i, m: (i, 0))) for p in pieces]
        + [(w, None) for w in weights],
        [
            (HBM((rows, width), BF), block),
            (shaped(F32, 8, width), None),
            (shaped(F32, 8, 3 * width), None),
        ],
        24,
        cost(6 * rows * width * width * 1.3, 2 * 9 * rows * width),
        "input_grad",
        grid=(rows // tm,),
    )


def quarter_of(meta, i):
    return (meta[CORE] ^ (i % 2)) * 2 + (meta[YPOS] ^ (i // 2))


def finish(meta, groups, places, widths, name):
    quarters = [q for group in groups for q in group]
    rows = quarters[0].shape[1]

    def kernel(meta, *refs):
        outs = refs[len(quarters) :]
        for g, place in enumerate(places):
            for i in range(4):
                part = refs[4 * g + i]
                for j in range(min(part.shape[0], len(widths) * widths[0] // 128 // 4 // len(groups))):
                    which, column = place(quarter_of(meta, i), j)
                    outs[which][:, span(column, 128)] = part[j].astype(F32)

    outs = [(shaped(F32, rows, n), None) for n in widths]
    return call(kernel, meta, [(a, None) for a in quarters], outs, 8, cost(1, 1), name)


def by_head(weight, base):
    rows = weight.shape[0]
    view = weight.reshape(rows, 3, HEADS, SIZE)[:, :, base : base + GROUP]
    return view.transpose(0, 2, 1, 3).reshape(rows, GROUP * 3 * SIZE)


def per_device(latents, w_qkv, w_out, w_up, w_down, gains, biases, ff_bias, cotangent, *, nb, nr):
    reps, images, length, width = latents.shape
    x = latents.reshape(-1, width)
    cot = cotangent.reshape(-1, width)
    count = reps * images
    bases = range(0, HEADS, GROUP)
    native = nb != 8 or nr != 4
    small = jnp.concatenate([gains, biases, ff_bias[None]], axis=0)
    small = jnp.pad(small, ((0, 16 - small.shape[0]), (0, 0)))
    if native:
        links = None
        zero = jnp.zeros((), jnp.int32)
        meta = jnp.stack([zero, zero, zero, zero, zero + 1, zero, zero, zero])

        def whole(w):
            return [(lax.all_gather(w, "batch", axis=0, tiled=True), 0)]

        table = lax.all_gather(small, "batch", axis=1, tiled=True)
        table = table.reshape(16, 4, 2, width // 8).transpose(2, 1, 0, 3)
        first, small = first_norm(meta, x, [table[0], table[1], table[1]])
        chunks = [whole(by_head(w_qkv, base)) for base in bases]
        chunks += [whole(jnp.concatenate([w_out, w_up], axis=1)), whole(w_down)]
    else:
        links = Links(nb, nr)
        mine_f = jnp.where(links.ci == 0, links.xi, links.yi)
        mine_s = jnp.where(links.ci == 0, links.yi, links.xi)
        meta = [links.ci, links.yi, links.xi, links.zi, 1 - links.ci, links.ci, mine_f, mine_s]
        meta = jnp.stack(meta).astype(jnp.int32)

        def quarter(w):
            rows = w.shape[0] // 4
            return lax.dynamic_slice_in_dim(w, (links.ci * 2 + links.yi) * rows, rows, 0)

        w_qkv = quarter(w_qkv)
        chunks = [by_head(w_qkv, base) for base in bases]
        extra = jnp.pad(small, ((0, w_qkv.shape[0] - 16), (0, 0)))
        chunks[0] = jnp.concatenate([chunks[0], extra], axis=1)
        chunks += [jnp.concatenate([quarter(w_out), quarter(w_up)], axis=1), quarter(w_down)]
        other = CoreSwap(links)

        def visit(i, chunks):
            if i == 0:
                return ()
            if i == 1:
                kept.extend(first_norm(meta, x, [part for part, _ in chunks[0][:3]]))
                return kept + other.early(chunks[0], 3)
            return other.early(chunks[i - 1], 2) + forward(i - 2, chunks[i - 2])

    packed, probs, mixed, weights, kept = [], [], [], [], []

    def forward(i, parts):
        parts = parts if native else other(parts, *mixed)
        a, b, c, d = attention_forward(meta, kept[0], kept[1], parts, bases[i], count)
        packed.append(a)
        probs.append(b)
        mixed.append(c)
        weights.append(d)
        return [c]

    if native:
        kept.extend((first, small))
        for i in range(len(bases)):
            forward(i, chunks[i])
    else:
        chunks = gather_chunks(chunks, links, visit)
        for i in range(len(mixed), len(bases)):
            forward(i, chunks[i])
        first, small = kept
    outer, inner = chunks[len(bases) :]
    outer = outer if native else other(outer, mixed[1])
    middle, second, active, slope = feed_forward_first(meta, x, small, mixed, outer)
    inner = inner if native else other(inner, mixed[1])
    out, hidden, send, keep, sums_two = feed_forward_second(
        meta, cot, small, middle, second, active, slope, inner
    )
    grad_attn, send_out, keep_out, sums_three = feed_forward_third(
        meta, cot, small, middle, mixed, hidden, outer
    )

    def backward(meta, g, half):
        return attention_backward(
            meta, first, packed[g], probs[g], grad_mixed, mixed[g], bases[g], half, count, g == 1
        )

    def collect(sums_one, sums_packed):
        sums_packed = sums_packed[0].reshape(HEADS, 3, SIZE)
        sums_q, sums_v = sums_packed[:, 0].reshape(width), sums_packed[:, 2].reshape(width)
        out, two, three = sums_three[2], sums_two, sums_three
        rows = [sums_one[0], three[0], sums_one[1], sums_q, sums_v, out, three[1], two[1], two[0]]
        return jnp.stack(rows)

    def sums_of(sums_one, sums_packed):
        two, three, one, packed = sums_two, sums_three, sums_one, sums_packed
        plain = [(one, 0), (three, 0), (one, 1), None, None, (three, 2), (three, 1), (two, 1), (two, 0)]
        sums = [entry and (*entry, 1, 0) for entry in plain]
        sums[3], sums[4] = (packed, 0, 3, 0), (packed, 0, 3, 2)
        return sums

    def result(grad_x, grads, smalls):
        return (
            out.reshape(latents.shape),
            grad_x.reshape(latents.shape),
            *grads,
            smalls[:2],
            smalls[2:8],
            smalls[8],
        )

    if native:
        grad_mixed, grad_attn = mixed_grad(meta, grad_attn, outer)
        halves = [[backward(meta, g, half) for half in (THEIRS, OURS)] for g in range(len(bases))]
        pieces = [half[0] for pair in halves for half in pair]
        grad_x, sums_one, sums_packed = input_grad(meta, x, grad_attn, small, pieces, weights)
        smalls = lax.psum_scatter(
            collect(sums_one, sums_packed), "batch", scatter_dimension=1, tiled=True
        )
        smalls = lax.psum(smalls, "rep")

        def reduced(send, keep, odd):
            keep, send = (jnp.swapaxes(keep, 0, 1), send) if odd else (keep, jnp.swapaxes(send, 0, 1))
            both = jnp.stack([keep, send])
            t = both.shape[4]
            both = both.transpose(3, 1, 5, 0, 2, 4, 6).reshape(width, t * 4 * 128)
            both = lax.psum_scatter(both, "batch", scatter_dimension=0, tiled=True)
            both = lax.psum(both.astype(BF), "rep").astype(F32)
            return both.reshape(-1, 4, t, 128)

        rest = [reduced(send_out, keep_out, True), reduced(send, keep, False)]
        rows = rest[0].shape[0]
        rest = [rest[0], rest[1][:, :, 2:], rest[1][:, :, :2]]
        rest = [g.reshape(rows, width) for g in rest]
        heads = [reduced(pair[0][1], pair[1][1], g == 1) for g, pair in enumerate(halves)]
        heads = jnp.concatenate(heads, axis=1).transpose(0, 2, 1, 3).reshape(rows, 3 * width)
        return result(grad_x, [heads, *rest], smalls)

    def to_core(value):
        return move(value, links.core)

    def along(arrays):
        return [arrays[0]] + [move(a, p) for a, p in zip(arrays[1:], links.z)]

    def share(value):
        return [value] + [move(value, p) for p in links.rep]

    both = Piece(keep, to_core(send), False)
    step = Step()
    step.swap(firsts=[both])
    (sent,) = step.run(after(meta, keep_out), "step_0")
    both.late.append((move(sent, links.x_or_y), 0))
    grad_mixed, grad_attn = mixed_grad(after(meta, sent), grad_attn, outer)
    packed_1, send_1 = backward(after(meta, sent), 0, THEIRS)

    outs = Piece(keep_out, to_core(send_out), True)
    step = Step()
    step.swap(firsts=[outs], seconds=[both])
    (sent,) = step.run(after(meta, send_1), "step_1")
    moved = move(sent, links.y_or_x)
    for piece in (outs, both):
        piece.late.append((moved, piece.next))
    packed_2, keep_1 = backward(after(meta, sent), 0, OURS)
    packed_3, send_2 = backward(after(meta, sent, keep_1), 1, THEIRS)

    one = Piece(keep_1, to_core(send_1), False)
    step = Step()
    step.swap(firsts=[one], seconds=[outs])
    step.along(both)
    sent, *z_both = step.run(after(meta, send_2), "step_2")
    moved = move(sent, links.x_or_y)
    for piece in (one, outs):
        piece.late.append((moved, piece.next))
    z_both = along(z_both)
    packed_4, keep_2 = backward(after(meta, sent), 1, OURS)

    two = Piece(keep_2, to_core(send_2), True)
    step = Step()
    step.swap(firsts=[two], seconds=[one])
    step.along(outs)
    sent, *z_outs = step.run(after(meta, keep_2, *z_both[1:]), "step_3")
    moved = move(sent, links.y_or_x)
    for piece in (two, one):
        piece.late.append((moved, piece.next))
    z_outs = along(z_outs)
    pieces = [packed_1, packed_2, packed_3, packed_4]
    grad_x, sums_one, sums_packed = input_grad(
        after(meta, sent), x, grad_attn, small, pieces, weights
    )

    step = Step()
    step.along(one, sums_of(sums_one, sums_packed))
    z_one = step.run(after(meta, grad_x, *z_outs[1:]), "step_4")
    step = Step()
    step.swap(seconds=[two])
    (sent,) = step.run(after(meta, z_one[0]), "step_5")
    two.late.append((move(sent, links.x_or_y), 0))
    step = Step()
    step.share([z_both, z_outs])
    (r_rest,) = step.run(after(meta, sent), "step_6")
    z_one = along(z_one)
    r_rest = share(after(r_rest, z_one[1]))

    step = Step()
    step.along(two)
    z_two = step.run(after(meta, z_one[1]), "step_7")
    step = Step()
    step.share([z_one])
    (r_one,) = step.run(after(meta, z_two[0], *r_rest[1:]), "step_8")
    z_two, r_one = along(z_two), share(r_one)

    step = Step()
    step.share([z_two])
    step.small(r_one)
    r_two, other, smalls = step.run(meta, "step_9")
    smalls = smalls + move(other, links.x)
    rest = finish(
        after(meta, r_two),
        [r_rest],
        [lambda q, j: (2 - j // 2, q * 2 + j % 2)],
        [width] * 3,
        "finish_rest",
    )
    (heads,) = finish(
        meta,
        [r_one, share(r_two)],
        [lambda q, j: (0, j * HEADS + q), lambda q, j: (0, j * HEADS + GROUP + q)],
        [3 * width],
        "finish_heads",
    )
    return result(grad_x, [heads, *rest], smalls)


def solution(mesh):
    nb, nr = mesh.shape["batch"], mesh.shape["rep"]

    def body(*args):
        return per_device(*args, nb=nb, nr=nr)

    rows = P("batch", None)
    cols = P(None, "batch")
    data = P("rep", "batch", None, None)
    return jax.shard_map(
        body,
        mesh=mesh,
        in_specs=(data, rows, rows, rows, rows, cols, cols, P("batch"), data),
        out_specs=(data, data, rows, rows, rows, rows, cols, cols, P("batch")),
        check_vma=False,
    )
```

```python
import functools

import jax
import jax.numpy as jnp
from jax import lax
from jax.experimental import pallas as pl
from jax.experimental.pallas import tpu as pltpu
from jax.sharding import PartitionSpec as P

HEADS = 8
SIZE = 128
GROUP = 4
EPS = 1e-05
AXES = ("batch", "rep")
BF = jnp.bfloat16
F32 = jnp.float32
NN, NT, TN = ((1,), (0,)), ((1,), (1,)), ((0,), (0,))
SCALE = SIZE ** (-0.5)
LOG2E = 1.4426950408889634
GELU = 0.7978845608028654
CUBIC = 0.044715
G1, G2, B1, BQ, BV, BO, B2, BD, BU = range(9)
CORE, YPOS, XPOS, ZPOS, THEIRS, OURS, MINE_F, MINE_S = range(8)


def dot(a, b, dims=NN):
    return lax.dot_general(a, b, (dims, ((), ())), preferred_element_type=F32)


HBM, VMEM = pltpu.HBM, pltpu.VMEM
ANY = pl.BlockSpec(memory_space=pl.ANY)


def call(kernel, meta, operands, outs, limit, estimate, name, scratch=(), grid=(1,)):
    shapes = [shape for shape, _ in outs]
    return pl.pallas_call(
        kernel,
        out_shape=shapes,
        grid_spec=pltpu.PrefetchScalarGridSpec(
            num_scalar_prefetch=1,
            grid=grid,
            in_specs=[spec or full(a) for a, spec in operands],
            out_specs=[spec or full(a) for a, spec in outs],
            scratch_shapes=scratch,
        ),
        compiler_params=pltpu.CompilerParams(vmem_limit_bytes=limit << 20),
        cost_estimate=estimate,
        name=name,
    )(meta, *[a for a, _ in operands])


def hbm(array):
    return pltpu.with_memory_space_constraint(array, HBM)


def shaped(dtype, *shape):
    return jax.ShapeDtypeStruct(shape, dtype)


def span(index, size):
    return pl.ds(pl.multiple_of(index * size, size), size)


def cost(flops, nbytes, trans=0):
    return pl.CostEstimate(flops=1, bytes_accessed=1, transcendentals=0)


def full(array):
    rank = len(array.shape)
    return pl.BlockSpec(array.shape, lambda *_: (0,) * rank)


def column_sum(values):
    return jnp.sum(values.astype(F32), axis=0, keepdims=True)


def permutation(target, nb, nr):
    pairs = []
    for b in range(nb):
        for r in range(nr):
            tb, tr = target(b, r)
            pairs.append((b * nr + r, tb * nr + tr))
    return pairs


class Links:
    def __init__(self, nb, nr):
        def swap(kb, kr):
            return permutation(lambda b, r: (b ^ kb, r ^ kr), nb, nr)

        self.core = swap(0, 1)
        self.rep = [swap(0, 1), swap(0, 2), swap(0, 3)]
        self.x = swap(1, 0)
        self.y = swap(0, 2)
        self.z = [swap(2, 0), swap(4, 0), swap(6, 0)]
        self.y_or_x = permutation(lambda b, r: (b, r ^ 2) if r % 2 == 0 else (b ^ 1, r), nb, nr)
        self.x_or_y = permutation(lambda b, r: (b ^ 1, r) if r % 2 == 0 else (b, r ^ 2), nb, nr)
        batch, rep = lax.axis_index("batch"), lax.axis_index("rep")
        self.xi, self.zi = batch % 2, batch // 2
        self.ci, self.yi = rep % 2, rep // 2


def move(value, pairs):
    return lax.ppermute(value, AXES, pairs)


def flip_if(bit, value, axis):
    return jnp.where(bit == 1, jnp.flip(value, axis), value)


def pick(value, axis, index):
    return lax.dynamic_index_in_dim(value, index, axis, keepdims=False)


def after(value, *others):
    return lax.optimization_barrier((value, *others))[0]


def gather_chunks(quarters, links, visit):
    chunks = []
    along, across = (), ()
    late = None
    for i, quarter in enumerate(quarters):
        quarter = after(quarter, *along)
        along = [move(quarter, p) for p in links.z]
        ahead = quarters[1:] if i == 0 else ()
        own = jnp.stack([after(quarter, *across, *ahead)] + along)
        first = move(own, links.y_or_x)
        both = own if late is None else jnp.concatenate([late, own], axis=2)
        both = move(both, links.x_or_y)
        if late is not None:
            chunks[-1].append((both, 0))
        chunks.append([(own, 0), (first, 0), (both, 0 if late is None else late.shape[2])])
        late = first
        across = (both, *visit(i, chunks))
    chunks[-1].append((move(after(late, *across[1:]), links.x_or_y), 0))
    return chunks


class CoreSwap:
    def __init__(self, links):
        self.pairs, self.moved = links.core, {}

    def __call__(self, chunk, *gates):
        for part, _ in chunk:
            if id(part) not in self.moved:
                self.moved[id(part)] = move(after(part, *gates), self.pairs)
        return chunk + [(self.moved[id(part)], start) for part, start in chunk]

    def early(self, chunk, count, *gates):
        moved = self(chunk[:count], *gates)
        return [part for part, _ in moved[count:]]


class Piece:
    def __init__(self, keep, other, odd):
        self.terms, self.t = [keep, other], keep.shape[3]
        self.odd = odd
        self.late = []

    def mine(self, meta):
        both = meta[MINE_F], meta[MINE_S]
        return both[::-1] if self.odd else both


class Step:
    def __init__(self):
        self.arrays, self.views, self.jobs, self.outs = [], [], [], []

    def load(self, array, shape, view):
        self.views.append((self.place(array), shape, view))
        return len(self.views) - 1

    def place(self, array):
        for i, known in enumerate(self.arrays):
            if known is array:
                return i
        self.arrays.append(array)
        return len(self.arrays) - 1

    def out(self, shape, dtype):
        self.outs.append((shaped(dtype, *shape), None))
        return len(self.outs) - 1

    def swap(self, firsts=(), seconds=()):
        at = 0
        out = len(self.outs)
        for piece in seconds:
            self.second(piece, out, at)
            piece.next, at = at, at + 4 * piece.t
        for piece in firsts:
            self.first(piece, out, at)
            piece.next, at = at, at + 8 * piece.t
        self.out((at, 128, 128), BF)

    def first(self, piece, out, at):
        def view(ref, meta):
            return ref.at[1 - piece.mine(meta)[0]]

        loads = [self.load(a, a.shape[1:], view) for a in piece.terms]
        n = 8 * piece.t

        def job(meta, got, outs):
            values = sum(got[i][...].astype(F32) for i in loads)
            outs[out][at : at + n] = values.astype(BF).reshape(n, 128, 128)

        self.jobs.append((job, len(self.views)))

    def second(self, piece, out, at):
        n = 4 * piece.t
        ((late, start),) = piece.late

        def view(ref, meta):
            f, s = piece.mine(meta)
            return ref.at[f, 1 - s]

        def late_view(ref, meta):
            return ref.at[pl.ds(start + (1 - piece.mine(meta)[1]) * n, n)]

        loads = [self.load(a, a.shape[2:], view) for a in piece.terms]
        loads.append(self.load(late, (n, 128, 128), late_view))

        def job(meta, got, outs):
            values = sum(got[i][...].reshape(n, 128, 128).astype(F32) for i in loads)
            outs[out][at : at + n] = values.astype(BF)

        self.jobs.append((job, len(self.views)))

    def along(self, piece, sums=()):
        t = piece.t
        (one, start_one), (two, start_two) = piece.late

        def view(ref, meta):
            f, s = piece.mine(meta)
            return ref.at[f, s]

        def view_one(ref, meta):
            return ref.at[pl.ds(start_one + piece.mine(meta)[1] * 4 * t, 4 * t)]

        def view_two(ref, meta):
            return ref.at[pl.ds(start_two, 4 * t)]

        loads = [self.load(a, a.shape[2:], view) for a in piece.terms]
        late = [self.load(one, (4 * t, 128, 128), view_one)]
        late.append(self.load(two, (4 * t, 128, 128), view_two))
        extra = [
            (self.load(a, a.shape, lambda ref, meta: ref), row, scale, shift)
            for a, row, scale, shift in sums
        ]
        out = len(self.outs)
        for k in range(4):
            self.out((t + bool(sums), 128, 128), BF if k else F32)

        def job(meta, got, outs):
            for k in range(4):
                z = meta[ZPOS] ^ k
                dtype = BF if k else F32
                values = sum(got[i][z].astype(F32) for i in loads)
                values += sum(got[i][pl.ds(z * t, t)].astype(F32) for i in late)
                outs[out + k][:t] = values.astype(dtype)
                if extra:
                    outs[out + k][t] = jnp.zeros((128, 128), dtype)
                    for x in range(2):
                        rows = [
                            got[i][row : row + 1, span((z * 2 + x) * scale + shift, 128)]
                            for i, row, scale, shift in extra
                        ]
                        rows += [jnp.zeros((16 - len(rows), 128), F32)]
                        rows = jnp.concatenate(rows, axis=0).astype(dtype)
                        outs[out + k][t, 16 * x : 16 * x + 16] = rows

        self.jobs.append((job, len(self.views)))

    def share(self, groups):
        loads = [
            [self.load(a, a.shape, lambda ref, meta: ref) for a in arrays] for arrays in groups
        ]
        sizes = [arrays[0].shape[0] for arrays in groups]
        out = self.out((sum(sizes), 128, 128), BF)

        def job(meta, got, outs):
            at = 0
            for slots, size in zip(loads, sizes):
                outs[out][at : at + size] = sum(got[i][...].astype(F32) for i in slots).astype(BF)
                at += size

        self.jobs.append((job, len(self.views)))

    def small(self, arrays):
        tile = arrays[0].shape[0] - 1
        loads = [self.load(a, (128, 128), lambda ref, meta: ref.at[tile]) for a in arrays]
        out = self.out((16, 128), F32)
        self.out((16, 128), F32)

        def job(meta, got, outs):
            for k in range(2):
                rows = span(meta[XPOS] if k else 1 - meta[XPOS], 16)
                outs[out + k][...] = sum(got[i][rows, :].astype(F32) for i in loads)

        self.jobs.append((job, len(self.views)))

    def run(self, meta, name):
        count, total = len(self.arrays), len(self.outs)

        def kernel(meta, *refs):
            outs, got, sems = refs[count : count + total], refs[count + total : -1], refs[-1]
            copies = [
                pltpu.make_async_copy(view(refs[i], meta), got[j], sems.at[j])
                for j, (i, _, view) in enumerate(self.views)
            ]
            for copy in copies:
                copy.start()
            ready = 0
            for job, last in self.jobs:
                for copy in copies[ready:last]:
                    copy.wait()
                ready = last
                job(meta, got, outs)

        return call(
            kernel,
            meta,
            [(a, ANY) for a in self.arrays],
            self.outs,
            12,
            cost(1, 1),
            name,
            [pltpu.VMEM(shape, self.arrays[i].dtype) for i, shape, _ in self.views]
            + [pltpu.SemaphoreType.DMA((len(self.views),))],
        )


def fetch(meta, parts, starts, whole, columns, sem, skip=0):
    first, n = columns
    if len(parts) == 1:
        source = parts[0].at[:, pl.ds(skip + first, n)]
        pltpu.make_async_copy(source, whole.at[:, pl.ds(first, n)], sem).start()
        return
    core, y, x, z = meta[CORE], meta[YPOS], meta[XPOS], meta[ZPOS]
    for i, (part, start) in enumerate(zip(parts, starts)):
        source = core if i < 4 else 1 - core
        dx = (0, source, 1 - source, 1)[i % 4]
        dy = (0, 1 - source, source, 1)[i % 4]
        for dz in range(4):
            block = (((z ^ dz) * 2 + (x ^ dx)) * 2 + source) * 2 + (y ^ dy)
            pltpu.make_async_copy(
                part.at[dz, :, pl.ds(start + skip + first, n)],
                whole.at[span(block, part.shape[1]), pl.ds(first, n)],
                sem,
            ).start()


def fetched(whole, columns, sem):
    first, n = columns
    here = whole.at[:, pl.ds(first, n)]
    pltpu.make_async_copy(here, here, sem).wait()


def normed_rows(values):
    centred = values - jnp.mean(values, axis=-1, keepdims=True)
    scale = lax.rsqrt(jnp.mean(centred * centred, axis=-1, keepdims=True) + EPS)
    return centred * scale, scale


def norm_back(grad, normed, scale):
    mean_one = jnp.mean(grad, axis=-1, keepdims=True)
    mean_two = jnp.mean(grad * normed, axis=-1, keepdims=True)
    return scale * (grad - mean_one - normed * mean_two)


def first_norm(meta, x, tables):
    rows, width = x.shape
    tm = 256
    last = tables[0].shape[2] - 128

    def kernel(meta, x_ref, *refs):
        parts, (first_ref, small_ref, table, sems) = refs[:3], refs[3:]
        copies = [
            pltpu.make_async_copy(ref.at[:, pl.ds(0, 16), pl.ds(last, 128)], table.at[i], sems.at[i])
            for i, ref in enumerate(parts)
        ]
        for copy in copies:
            copy.start()
        for copy in copies:
            copy.wait()
        x, z = meta[XPOS], meta[ZPOS]
        for dz in range(4):
            own, one, two = (table[i, dz].astype(F32) for i in range(3))
            for dx, values in enumerate((own, jnp.where(meta[CORE] == 1, one, two))):
                small_ref[:, span((z ^ dz) * 2 + (x ^ dx), 128)] = values

        @pl.loop(0, rows // tm)
        def _(i):
            normed, _ = normed_rows(x_ref[span(i, tm), :].astype(F32))
            first = normed * small_ref[G1 : G1 + 1, :] + small_ref[B1 : B1 + 1, :]
            first_ref[span(i, tm), :] = first.astype(BF)

    return call(
        kernel,
        meta,
        [(x, None)] + [(a, ANY) for a in tables],
        [(VMEM((rows, width), BF), None), (shaped(F32, 16, width), None)],
        16,
        cost(rows * width * 20, rows * width * 4),
        "first_norm",
        [pltpu.VMEM((3, 4, 16, 128), BF), pltpu.SemaphoreType.DMA((3,))],
    )


def attention_forward(meta, first, small, parts, base, images):
    rows, width = first.shape
    length, n = rows // images, 3 * SIZE
    parts, starts = zip(*parts)
    count = len(parts)
    columns = (0, GROUP * n)

    def kernel(meta, first_ref, small_ref, *refs):
        parts, refs = refs[:count], refs[count:]
        packed_ref, probs_ref, mixed_ref, weight_out, weight_ref, sems = refs
        head = pl.program_id(0)
        keep = pltpu.make_async_copy(weight_ref, weight_out, sems.at[1])

        @pl.when(head == 0)
        def _():
            fetch(meta, parts, starts, weight_ref, columns, sems.at[0])
            fetched(weight_ref, columns, sems.at[0])
            keep.start()

        here = span(base + head, SIZE)
        bias_q, bias_v = small_ref[BQ : BQ + 1, here], small_ref[BV : BV + 1, here]
        bias = jnp.concatenate([bias_q, jnp.zeros_like(bias_q), bias_v], axis=1)
        packed = (dot(first_ref[...], weight_ref[:, span(head, n)]) + bias).astype(BF)
        packed_ref[...] = packed
        for i in range(images):
            part = packed[i * length : (i + 1) * length]
            q, k, v = part[:, :SIZE], part[:, SIZE : 2 * SIZE], part[:, 2 * SIZE :]
            scores = dot(q, k, NT)
            top = jnp.max(scores, axis=-1, keepdims=True)
            raised = jnp.exp2((scores - top) * (SCALE * LOG2E))
            probs = raised * (1.0 / jnp.sum(raised, axis=-1, keepdims=True))
            probs = probs.astype(BF)
            probs_ref[0, i] = probs
            mixed_ref[i * length : (i + 1) * length, span(head, SIZE)] = dot(probs, v).astype(BF)

        @pl.when(head == GROUP - 1)
        def _():
            keep.wait()

    return call(
        kernel,
        meta,
        [(first, None), (small, None)] + [(p, ANY) for p in parts],
        [
            (HBM((rows, GROUP * n), BF), pl.BlockSpec((rows, n), lambda h, m: (0, h))),
            (
                HBM((GROUP, images, length, length), BF),
                pl.BlockSpec((1, images, length, length), lambda h, m: (h, 0, 0, 0)),
            ),
            (VMEM((rows, GROUP * SIZE), BF), None),
            (HBM((width, GROUP * n), BF), ANY),
        ],
        20,
        cost(
            2 * rows * width * GROUP * n * 2 + 8 * rows * length * SIZE * GROUP,
            2 * (rows * width + width * n * GROUP * 2 + rows * n * GROUP + GROUP * rows * length),
            GROUP * rows * length,
        ),
        "attention_forward",
        [pltpu.VMEM((width, GROUP * n), BF), pltpu.SemaphoreType.DMA((2,))],
        (GROUP,),
    )


def store_piece(owner, odd, piece_ref, at, values, y):
    rows = values.shape[0] // 8
    for z in range(4):
        for x in range(2):
            plain = owner == (1 if odd else 0)
            first = jnp.where(plain, x, y)
            second = jnp.where(plain, y, x)
            start = (z * 2 + x) * rows
            for j in range(values.shape[1] // 128):
                part = values[start : start + rows, j * 128 : (j + 1) * 128]
                piece_ref[first, second, z, at + j] = part.astype(BF)


def blocks(rows):
    size = min(256, rows)

    def over(body):
        pl.loop(0, rows // size)(lambda i: body(span(i, size), i))

    return over


def feed_forward_first(meta, x, small, mixed, parts):
    rows, width = x.shape
    parts, starts = zip(*parts)
    count = len(parts)

    def kernel(meta, x_ref, small_ref, *refs):
        mixed_refs, parts = refs[: len(mixed)], refs[len(mixed) : len(mixed) + count]
        middle_ref, second_ref, active_ref, slope_ref, whole, sems = refs[len(mixed) + count :]
        for j in range(2):
            fetch(meta, parts, starts, whole, (j * width, width), sems.at[j])

        def row(r):
            return small_ref[r : r + 1, :]

        fetched(whole, (0, width), sems.at[0])

        @blocks(rows)
        def _(here, i):
            values = jnp.concatenate([r[here, :] for r in mixed_refs], axis=1)
            middle = x_ref[here, :].astype(F32) + dot(values, whole[:, :width]) + row(BO)
            middle_ref[here, :] = middle
            normed, _ = normed_rows(middle)
            second = (normed * row(G2) + row(B2)).astype(BF)
            second_ref[here, :] = second

            @pl.when(i == 0)
            def _():
                fetched(whole, (width, width), sems.at[1])

            v = dot(second, whole[:, width:]) + row(BU)
            square = v * v
            half = 0.5 * jnp.tanh(v * (GELU + (GELU * CUBIC) * square)) + 0.5
            active = v * half
            active_ref[here, :] = active.astype(BF)
            slope = (1.0 - half) * active * (2 * GELU + (6 * GELU * CUBIC) * square)
            slope_ref[here, :] = (half + slope).astype(BF)

    return call(
        kernel,
        meta,
        [(x, None), (small, None)] + [(a, None) for a in mixed] + [(p, ANY) for p in parts],
        [
            (VMEM((rows, width), F32), None),
            (VMEM((rows, width), BF), None),
            (VMEM((rows, width), BF), None),
            (VMEM((rows, width), BF), None),
        ],
        24,
        cost(4 * rows * width * width, 2 * 9 * rows * width, rows * width),
        "feed_forward_first",
        [pltpu.VMEM((width, 2 * width), BF), pltpu.SemaphoreType.DMA((2,))],
    )


def store_grads(meta, both, m, left_ref, right_ref, odd):
    half = right_ref.shape[1] // 2

    @pl.loop(0, 2)
    def _(core):
        values = dot(left_ref[...], right_ref[:, span(core, half)]).astype(BF)
        for y in range(2):
            part = values[:, y * half // 2 : (y + 1) * half // 2]
            store_piece(core, odd, both.at[core], 2 * m, part, y)


def send_grads(meta, both, m, pieces, sems):
    tiles = pl.ds(2 * m, 2)
    copies = [
        pltpu.make_async_copy(
            both.at[meta[half], :, :, :, tiles], piece.at[:, :, :, tiles], sems.at[2 * m + i]
        )
        for i, (half, piece) in enumerate(zip((THEIRS, OURS), pieces))
    ]
    for copy in copies:
        copy.start()
    return copies


def feed_forward_second(meta, cot, small, middle, second, active, slope, parts):
    rows, width = cot.shape
    parts, starts = zip(*parts)
    count = len(parts)

    def kernel(meta, cot_ref, small_ref, middle_ref, second_ref, active_ref, slope_ref, *refs):
        parts, refs = refs[:count], refs[count:]
        out_ref, hidden_ref, *pieces, sums_ref, whole, out, flipped, halves, sems = refs
        fetch(meta, parts, starts, whole, (0, width), sems.at[4])
        flipped[...] = active_ref[...].T
        store_grads(meta, halves, 0, flipped, cot_ref, False)
        copies = send_grads(meta, halves, 0, pieces, sems)
        fetched(whole, (0, width), sems.at[4])

        @blocks(width)
        def _(here, _):
            grad = dot(cot_ref[...], whole[here, :], NT)
            hidden_ref[:, here] = (slope_ref[:, here].astype(F32) * grad).astype(BF)

        flipped[...] = second_ref[...].T
        store_grads(meta, halves, 1, flipped, hidden_ref, False)
        copies += send_grads(meta, halves, 1, pieces, sems)

        def write(here):
            return pltpu.make_async_copy(out.at[:, here], out_ref.at[:, here], sems.at[5])

        @blocks(width)
        def _(here, _):
            values = middle_ref[:, here] + dot(active_ref[...], whole[:, here])
            out[:, here] = (values + small_ref[BD : BD + 1, here]).astype(BF)
            write(here).start()

        sums_ref[...] = jnp.zeros_like(sums_ref)
        sums_ref[0:1, :] = column_sum(hidden_ref[...])
        sums_ref[1:2, :] = column_sum(cot_ref[...])
        for copy in (write(pl.ds(0, width)), *copies):
            copy.wait()

    shape = (2, 2, 4, 4, width // 8, 128)
    piece = VMEM(shape, BF)
    return call(
        kernel,
        meta,
        [(a, None) for a in (cot, small, middle, second, active, slope)]
        + [(p, ANY) for p in parts],
        [
            (HBM((rows, width), BF), ANY),
            (VMEM((rows, width), BF), None),
            (piece, ANY),
            (piece, ANY),
            (shaped(F32, 8, width), None),
        ],
        24,
        cost(8 * rows * width * width, 2 * 12 * rows * width),
        "feed_forward_second",
        [
            pltpu.VMEM((width, width), BF),
            pltpu.VMEM((rows, width), BF),
            pltpu.VMEM((width, rows), BF),
            pltpu.VMEM((2, *shape), BF),
            pltpu.SemaphoreType.DMA((6,)),
        ],
    )


def feed_forward_third(meta, cot, small, middle, mixed, hidden, parts):
    rows, width = cot.shape
    parts, starts = zip(*parts)
    count = len(parts)

    def kernel(meta, cot_ref, small_ref, middle_ref, hidden_ref, *refs):
        mixed_refs, parts = refs[: len(mixed)], refs[len(mixed) : len(mixed) + count]
        attn_ref, *pieces, sums_ref, whole, flipped, halves, sem, sems = refs[len(mixed) + count :]
        fetch(meta, parts, starts, whole, (0, width), sem, width)
        fetched(whole, (0, width), sem)
        sums_ref[...] = jnp.zeros_like(sums_ref)

        @blocks(rows)
        def _(here, _):
            grad_second = dot(hidden_ref[here, :], whole[...], NT)
            normed, scale = normed_rows(middle_ref[here, :])
            back = norm_back(grad_second * small_ref[G2 : G2 + 1, :], normed, scale)
            grad_attn = (cot_ref[here, :].astype(F32) + back).astype(BF)
            attn_ref[here, :] = grad_attn
            sums_ref[0:1, :] += column_sum(grad_second * normed)
            sums_ref[1:2, :] += column_sum(grad_second)
            sums_ref[2:3, :] += column_sum(grad_attn)

        for i, ref in enumerate(mixed_refs):
            n = ref.shape[1]
            flipped[i * n : (i + 1) * n, :] = ref[...].T
        store_grads(meta, halves, 0, flipped, attn_ref, True)
        for copy in send_grads(meta, halves, 0, pieces, sems):
            copy.wait()

    shape = (2, 2, 4, 2, width // 8, 128)
    piece = VMEM(shape, BF)
    return call(
        kernel,
        meta,
        [(a, None) for a in (cot, small, middle, hidden, *mixed)] + [(p, ANY) for p in parts],
        [(VMEM((rows, width), BF), None), (piece, ANY), (piece, ANY), (shaped(F32, 8, width), None)],
        20,
        cost(4 * rows * width * width, 2 * 12 * rows * width),
        "feed_forward_third",
        [
            pltpu.VMEM((width, width), BF),
            pltpu.VMEM((width, rows), BF),
            pltpu.VMEM((2, *shape), BF),
            pltpu.SemaphoreType.DMA,
            pltpu.SemaphoreType.DMA((2,)),
        ],
    )


def mixed_grad(meta, grad_attn, parts):
    rows, width = grad_attn.shape
    parts, starts = zip(*parts)
    count = len(parts)

    def kernel(meta, attn_ref, *refs):
        parts, (grad_ref, attn_out, whole, sems) = refs[:count], refs[count:]
        write = pltpu.make_async_copy(attn_ref, attn_out, sems.at[1])
        write.start()
        fetch(meta, parts, starts, whole, (0, width), sems.at[0])
        fetched(whole, (0, width), sems.at[0])

        @blocks(rows)
        def _(here, _):
            grad_ref[here, :] = dot(attn_ref[here, :], whole[...], NT).astype(BF)

        write.wait()

    return call(
        kernel,
        meta,
        [(grad_attn, None)] + [(p, ANY) for p in parts],
        [(VMEM((rows, width), BF), None), (HBM((rows, width), BF), ANY)],
        16,
        cost(2 * rows * width * width, 2 * 4 * rows * width),
        "mixed_grad",
        [pltpu.VMEM((width, width), BF), pltpu.SemaphoreType.DMA((2,))],
    )


def attention_backward(meta, first, packed, probs, grad_mixed, mixed, base, half, images, odd):
    rows, width = first.shape
    length, n = rows // images, 3 * SIZE
    pair = GROUP // 2

    def kernel(
        meta, first_ref, packed_ref, probs_ref, grad_ref, mixed_ref, grad_packed_ref, piece_ref
    ):
        j = pl.program_id(0)
        head = meta[half] * pair + j

        @pl.loop(0, images)
        def _(i):
            here = span(i, length)
            packed = packed_ref[here, :]
            q, k, v = packed[:, :SIZE], packed[:, SIZE : 2 * SIZE], packed[:, 2 * SIZE :]
            grad = grad_ref[here, span(base + head, SIZE)]
            mixed = mixed_ref[here, span(head, SIZE)]
            inner = jnp.sum(grad.astype(F32) * mixed.astype(F32), axis=-1, keepdims=True)
            probs = probs_ref[0, i]
            grad_v = dot(probs, grad, TN)
            grad_scores = (probs.astype(F32) * (dot(grad, v, NT) - inner)).astype(BF)
            grad_q = dot(grad_scores, k) * SCALE
            grad_k = dot(grad_scores, q, TN) * SCALE
            grad_packed_ref[here, :] = jnp.concatenate(
                [grad_q.astype(BF), grad_k.astype(BF), grad_v.astype(BF)], axis=1
            )

        values = dot(first_ref[...], grad_packed_ref[...], TN)
        store_piece(meta[half], odd, piece_ref, 0, values, j)

    return call(
        kernel,
        meta,
        [
            (first, None),
            (hbm(packed), pl.BlockSpec((rows, n), lambda j, m: (0, m[half] * pair + j))),
            (
                hbm(probs),
                pl.BlockSpec(
                    (1, images, length, length), lambda j, m: (m[half] * pair + j, 0, 0, 0)
                ),
            ),
            (grad_mixed, None),
            (mixed, None),
        ],
        [
            (HBM((rows, pair * n), BF), pl.BlockSpec((rows, n), lambda j, m: (0, j))),
            (VMEM((2, 2, 4, 3, width // 8, SIZE), BF), None),
        ],
        20,
        cost(
            pair * (2 * rows * width * n * 1.5 + 10 * rows * length * SIZE * 1.5),
            2 * (rows * width + pair * (rows * length + 3 * rows * n)),
        ),
        "attention_backward",
        grid=(pair,),
    )


def input_grad(meta, x, grad_attn, small, pieces, weights):
    rows, width = x.shape
    tm = min(256, rows)
    groups = len(weights)
    n = pieces[0].shape[1]

    def kernel(meta, x_ref, grad_ref, small_ref, *refs):
        pieces, weights = refs[: 2 * groups], refs[2 * groups : 3 * groups]
        out_ref, sums_ref, packed_sums_ref = refs[3 * groups :]

        @pl.when(pl.program_id(0) == 0)
        def _():
            sums_ref[...] = jnp.zeros_like(sums_ref)
            packed_sums_ref[...] = jnp.zeros_like(packed_sums_ref)

        grad = None
        for g in range(groups):
            for j, which in enumerate((THEIRS, OURS)):
                piece = pieces[2 * g + j][...]
                term = dot(piece, weights[g][:, span(meta[which], n)], NT)
                grad = term if grad is None else grad + term
                packed_sums_ref[0:1, span(2 * g + meta[which], n)] += column_sum(piece)
        normed, scale = normed_rows(x_ref[...].astype(F32))
        back = norm_back(grad * small_ref[G1 : G1 + 1, :], normed, scale)
        out_ref[...] = (grad_ref[...].astype(F32) + back).astype(BF)
        sums_ref[0:1, :] += column_sum(grad * normed)
        sums_ref[1:2, :] += column_sum(grad)

    block = pl.BlockSpec((tm, width), lambda i, m: (i, 0))
    return call(
        kernel,
        meta,
        [(hbm(x), block), (hbm(grad_attn), block), (small, None)]
        + [(hbm(p), pl.BlockSpec((tm, n), lambda i, m: (i, 0))) for p in pieces]
        + [(w, None) for w in weights],
        [
            (HBM((rows, width), BF), block),
            (shaped(F32, 8, width), None),
            (shaped(F32, 8, 3 * width), None),
        ],
        24,
        cost(6 * rows * width * width * 1.3, 2 * 9 * rows * width),
        "input_grad",
        grid=(rows // tm,),
    )


def quarter_of(meta, i):
    return (meta[CORE] ^ (i % 2)) * 2 + (meta[YPOS] ^ (i // 2))


def finish(meta, groups, places, widths, name):
    quarters = [q for group in groups for q in group]
    rows = quarters[0].shape[1]

    def kernel(meta, *refs):
        outs = refs[len(quarters) :]
        for g, place in enumerate(places):
            for i in range(4):
                part = refs[4 * g + i]
                for j in range(min(part.shape[0], len(widths) * widths[0] // 128 // 4 // len(groups))):
                    which, column = place(quarter_of(meta, i), j)
                    outs[which][:, span(column, 128)] = part[j].astype(F32)

    outs = [(shaped(F32, rows, n), None) for n in widths]
    return call(kernel, meta, [(a, None) for a in quarters], outs, 8, cost(1, 1), name)


def by_head(weight, base):
    rows = weight.shape[0]
    view = weight.reshape(rows, 3, HEADS, SIZE)[:, :, base : base + GROUP]
    return view.transpose(0, 2, 1, 3).reshape(rows, GROUP * 3 * SIZE)


def per_device(latents, w_qkv, w_out, w_up, w_down, gains, biases, ff_bias, cotangent, *, nb, nr):
    reps, images, length, width = latents.shape
    x = latents.reshape(-1, width)
    cot = cotangent.reshape(-1, width)
    count = reps * images
    bases = range(0, HEADS, GROUP)
    native = nb != 8 or nr != 4
    small = jnp.concatenate([gains, biases, ff_bias[None]], axis=0)
    small = jnp.pad(small, ((0, 16 - small.shape[0]), (0, 0)))
    if native:
        links = None
        zero = jnp.zeros((), jnp.int32)
        meta = jnp.stack([zero, zero, zero, zero, zero + 1, zero, zero, zero])

        def whole(w):
            return [(lax.all_gather(w, "batch", axis=0, tiled=True), 0)]

        table = lax.all_gather(small, "batch", axis=1, tiled=True)
        table = table.reshape(16, 4, 2, width // 8).transpose(2, 1, 0, 3)
        first, small = first_norm(meta, x, [table[0], table[1], table[1]])
        chunks = [whole(by_head(w_qkv, base)) for base in bases]
        chunks += [whole(jnp.concatenate([w_out, w_up], axis=1)), whole(w_down)]
    else:
        links = Links(nb, nr)
        mine_f = jnp.where(links.ci == 0, links.xi, links.yi)
        mine_s = jnp.where(links.ci == 0, links.yi, links.xi)
        meta = [links.ci, links.yi, links.xi, links.zi, 1 - links.ci, links.ci, mine_f, mine_s]
        meta = jnp.stack(meta).astype(jnp.int32)

        def quarter(w):
            rows = w.shape[0] // 4
            return lax.dynamic_slice_in_dim(w, (links.ci * 2 + links.yi) * rows, rows, 0)

        w_qkv = quarter(w_qkv)
        chunks = [by_head(w_qkv, base) for base in bases]
        extra = jnp.pad(small, ((0, w_qkv.shape[0] - 16), (0, 0)))
        chunks[0] = jnp.concatenate([chunks[0], extra], axis=1)
        chunks += [jnp.concatenate([quarter(w_out), quarter(w_up)], axis=1), quarter(w_down)]
        other = CoreSwap(links)

        def visit(i, chunks):
            if i == 0:
                return ()
            if i == 1:
                kept.extend(first_norm(meta, x, [part for part, _ in chunks[0][:3]]))
                return kept + other.early(chunks[0], 3)
            return other.early(chunks[i - 1], 2) + forward(i - 2, chunks[i - 2])

    packed, probs, mixed, weights, kept = [], [], [], [], []

    def forward(i, parts):
        parts = parts if native else other(parts, *mixed)
        a, b, c, d = attention_forward(meta, kept[0], kept[1], parts, bases[i], count)
        packed.append(a)
        probs.append(b)
        mixed.append(c)
        weights.append(d)
        return [c]

    if native:
        kept.extend((first, small))
        for i in range(len(bases)):
            forward(i, chunks[i])
    else:
        chunks = gather_chunks(chunks, links, visit)
        for i in range(len(mixed), len(bases)):
            forward(i, chunks[i])
        first, small = kept
    outer, inner = chunks[len(bases) :]
    outer = outer if native else other(outer, mixed[1])
    middle, second, active, slope = feed_forward_first(meta, x, small, mixed, outer)
    inner = inner if native else other(inner, mixed[1])
    out, hidden, send, keep, sums_two = feed_forward_second(
        meta, cot, small, middle, second, active, slope, inner
    )
    grad_attn, send_out, keep_out, sums_three = feed_forward_third(
        meta, cot, small, middle, mixed, hidden, outer
    )

    def backward(meta, g, half):
        return attention_backward(
            meta, first, packed[g], probs[g], grad_mixed, mixed[g], bases[g], half, count, g == 1
        )

    def collect(sums_one, sums_packed):
        sums_packed = sums_packed[0].reshape(HEADS, 3, SIZE)
        sums_q, sums_v = sums_packed[:, 0].reshape(width), sums_packed[:, 2].reshape(width)
        out, two, three = sums_three[2], sums_two, sums_three
        rows = [sums_one[0], three[0], sums_one[1], sums_q, sums_v, out, three[1], two[1], two[0]]
        return jnp.stack(rows)

    def sums_of(sums_one, sums_packed):
        two, three, one, packed = sums_two, sums_three, sums_one, sums_packed
        plain = [(one, 0), (three, 0), (one, 1), None, None, (three, 2), (three, 1), (two, 1), (two, 0)]
        sums = [entry and (*entry, 1, 0) for entry in plain]
        sums[3], sums[4] = (packed, 0, 3, 0), (packed, 0, 3, 2)
        return sums

    def result(grad_x, grads, smalls):
        return (
            out.reshape(latents.shape),
            grad_x.reshape(latents.shape),
            *grads,
            smalls[:2],
            smalls[2:8],
            smalls[8],
        )

    if native:
        grad_mixed, grad_attn = mixed_grad(meta, grad_attn, outer)
        halves = [[backward(meta, g, half) for half in (THEIRS, OURS)] for g in range(len(bases))]
        pieces = [half[0] for pair in halves for half in pair]
        grad_x, sums_one, sums_packed = input_grad(meta, x, grad_attn, small, pieces, weights)
        smalls = lax.psum_scatter(
            collect(sums_one, sums_packed), "batch", scatter_dimension=1, tiled=True
        )
        smalls = lax.psum(smalls, "rep")

        def reduced(send, keep, odd):
            keep, send = (jnp.swapaxes(keep, 0, 1), send) if odd else (keep, jnp.swapaxes(send, 0, 1))
            both = jnp.stack([keep, send])
            t = both.shape[4]
            both = both.transpose(3, 1, 5, 0, 2, 4, 6).reshape(width, t * 4 * 128)
            both = lax.psum_scatter(both, "batch", scatter_dimension=0, tiled=True)
            both = lax.psum(both.astype(BF), "rep").astype(F32)
            return both.reshape(-1, 4, t, 128)

        rest = [reduced(send_out, keep_out, True), reduced(send, keep, False)]
        rows = rest[0].shape[0]
        rest = [rest[0], rest[1][:, :, 2:], rest[1][:, :, :2]]
        rest = [g.reshape(rows, width) for g in rest]
        heads = [reduced(pair[0][1], pair[1][1], g == 1) for g, pair in enumerate(halves)]
        heads = jnp.concatenate(heads, axis=1).transpose(0, 2, 1, 3).reshape(rows, 3 * width)
        return result(grad_x, [heads, *rest], smalls)

    def to_core(value):
        return move(value, links.core)

    def along(arrays):
        return [arrays[0]] + [move(a, p) for a, p in zip(arrays[1:], links.z)]

    def share(value):
        by_y = move(value, links.y)
        return [value, move(value, links.core), by_y, move(by_y, links.core)]

    both = Piece(keep, to_core(send), False)
    step = Step()
    step.swap(firsts=[both])
    (sent,) = step.run(after(meta, keep_out), "step_0")
    both.late.append((move(sent, links.x_or_y), 0))
    grad_mixed, grad_attn = mixed_grad(after(meta, sent), grad_attn, outer)
    packed_1, send_1 = backward(after(meta, sent), 0, THEIRS)

    outs = Piece(keep_out, to_core(send_out), True)
    step = Step()
    step.swap(firsts=[outs], seconds=[both])
    (sent,) = step.run(after(meta, send_1), "step_1")
    moved = move(sent, links.y_or_x)
    for piece in (outs, both):
        piece.late.append((moved, piece.next))
    packed_2, keep_1 = backward(after(meta, sent), 0, OURS)
    packed_3, send_2 = backward(after(meta, sent, keep_1), 1, THEIRS)

    one = Piece(keep_1, to_core(send_1), False)
    step = Step()
    step.swap(firsts=[one], seconds=[outs])
    step.along(both)
    sent, *z_both = step.run(after(meta, send_2), "step_2")
    moved = move(sent, links.x_or_y)
    for piece in (one, outs):
        piece.late.append((moved, piece.next))
    z_both = along(z_both)
    packed_4, keep_2 = backward(after(meta, sent), 1, OURS)

    two = Piece(keep_2, to_core(send_2), True)
    step = Step()
    step.swap(firsts=[two], seconds=[one])
    step.along(outs)
    sent, *z_outs = step.run(after(meta, keep_2, *z_both[1:]), "step_3")
    moved = move(sent, links.y_or_x)
    for piece in (two, one):
        piece.late.append((moved, piece.next))
    z_outs = along(z_outs)
    pieces = [packed_1, packed_2, packed_3, packed_4]
    grad_x, sums_one, sums_packed = input_grad(
        after(meta, sent), x, grad_attn, small, pieces, weights
    )

    step = Step()
    step.along(one, sums_of(sums_one, sums_packed))
    z_one = step.run(after(meta, grad_x, *z_outs[1:]), "step_4")
    step = Step()
    step.swap(seconds=[two])
    (sent,) = step.run(after(meta, z_one[0]), "step_5")
    two.late.append((move(sent, links.x_or_y), 0))
    step = Step()
    step.share([z_both, z_outs])
    (r_rest,) = step.run(after(meta, sent), "step_6")
    z_one = along(z_one)
    r_rest = share(after(r_rest, z_one[1]))

    step = Step()
    step.along(two)
    z_two = step.run(after(meta, z_one[1]), "step_7")
    step = Step()
    step.share([z_one])
    (r_one,) = step.run(after(meta, z_two[0]), "step_8")
    z_two = along(z_two)
    r_one = share(after(r_one, z_two[1]))

    step = Step()
    step.share([z_two])
    step.small(r_one)
    r_two, other, smalls = step.run(meta, "step_9")
    smalls = smalls + move(other, links.x)
    rest = finish(
        after(meta, r_two),
        [r_rest],
        [lambda q, j: (2 - j // 2, q * 2 + j % 2)],
        [width] * 3,
        "finish_rest",
    )
    (heads,) = finish(
        meta,
        [r_one, share(r_two)],
        [lambda q, j: (0, j * HEADS + q), lambda q, j: (0, j * HEADS + GROUP + q)],
        [3 * width],
        "finish_heads",
    )
    return result(grad_x, [heads, *rest], smalls)


def solution(mesh):
    nb, nr = mesh.shape["batch"], mesh.shape["rep"]

    def body(*args):
        return per_device(*args, nb=nb, nr=nr)

    rows = P("batch", None)
    cols = P(None, "batch")
    data = P("rep", "batch", None, None)
    return jax.shard_map(
        body,
        mesh=mesh,
        in_specs=(data, rows, rows, rows, rows, cols, cols, P("batch"), data),
        out_specs=(data, data, rows, rows, rows, rows, cols, cols, P("batch")),
        check_vma=False,
    )
```

```python
import functools

import jax
import jax.numpy as jnp
from jax import lax
from jax.experimental import pallas as pl
from jax.experimental.pallas import tpu as pltpu
from jax.sharding import PartitionSpec as P

HEADS = 8
SIZE = 128
GROUP = 4
EPS = 1e-05
AXES = ("batch", "rep")
BF = jnp.bfloat16
F32 = jnp.float32
NN, NT, TN = ((1,), (0,)), ((1,), (1,)), ((0,), (0,))
SCALE = SIZE ** (-0.5)
LOG2E = 1.4426950408889634
GELU = 0.7978845608028654
CUBIC = 0.044715
G1, G2, B1, BQ, BV, BO, B2, BD, BU = range(9)
CORE, YPOS, XPOS, ZPOS, THEIRS, OURS, MINE_F, MINE_S = range(8)


def dot(a, b, dims=NN):
    return lax.dot_general(a, b, (dims, ((), ())), preferred_element_type=F32)


HBM, VMEM = pltpu.HBM, pltpu.VMEM
ANY = pl.BlockSpec(memory_space=pl.ANY)


def call(kernel, meta, operands, outs, limit, estimate, name, scratch=(), grid=(1,)):
    shapes = [shape for shape, _ in outs]
    return pl.pallas_call(
        kernel,
        out_shape=shapes,
        grid_spec=pltpu.PrefetchScalarGridSpec(
            num_scalar_prefetch=1,
            grid=grid,
            in_specs=[spec or full(a) for a, spec in operands],
            out_specs=[spec or full(a) for a, spec in outs],
            scratch_shapes=scratch,
        ),
        compiler_params=pltpu.CompilerParams(vmem_limit_bytes=limit << 20),
        cost_estimate=estimate,
        name=name,
    )(meta, *[a for a, _ in operands])


def hbm(array):
    return pltpu.with_memory_space_constraint(array, HBM)


def shaped(dtype, *shape):
    return jax.ShapeDtypeStruct(shape, dtype)


def span(index, size):
    return pl.ds(pl.multiple_of(index * size, size), size)


def cost(flops, nbytes, trans=0):
    return pl.CostEstimate(flops=1, bytes_accessed=1, transcendentals=0)


def full(array):
    rank = len(array.shape)
    return pl.BlockSpec(array.shape, lambda *_: (0,) * rank)


def column_sum(values):
    return jnp.sum(values.astype(F32), axis=0, keepdims=True)


def permutation(target, nb, nr):
    pairs = []
    for b in range(nb):
        for r in range(nr):
            tb, tr = target(b, r)
            pairs.append((b * nr + r, tb * nr + tr))
    return pairs


class Links:
    def __init__(self, nb, nr):
        def swap(kb, kr):
            return permutation(lambda b, r: (b ^ kb, r ^ kr), nb, nr)

        self.core = swap(0, 1)
        self.rep = [swap(0, 1), swap(0, 2), swap(0, 3)]
        self.x = swap(1, 0)
        self.y = swap(0, 2)
        self.z = [swap(2, 0), swap(4, 0), swap(6, 0)]
        self.y_or_x = permutation(lambda b, r: (b, r ^ 2) if r % 2 == 0 else (b ^ 1, r), nb, nr)
        self.x_or_y = permutation(lambda b, r: (b ^ 1, r) if r % 2 == 0 else (b, r ^ 2), nb, nr)
        batch, rep = lax.axis_index("batch"), lax.axis_index("rep")
        self.xi, self.zi = batch % 2, batch // 2
        self.ci, self.yi = rep % 2, rep // 2


def move(value, pairs):
    return lax.ppermute(value, AXES, pairs)


def flip_if(bit, value, axis):
    return jnp.where(bit == 1, jnp.flip(value, axis), value)


def pick(value, axis, index):
    return lax.dynamic_index_in_dim(value, index, axis, keepdims=False)


def after(value, *others):
    return lax.optimization_barrier((value, *others))[0]


def gather_chunks(quarters, links, visit):
    chunks = []
    along, across = (), ()
    late = None
    for i, quarter in enumerate(quarters):
        quarter = after(quarter, *along)
        along = [move(quarter, p) for p in links.z]
        ahead = quarters[1:] if i == 0 else ()
        own = jnp.stack([after(quarter, *across, *ahead)] + along)
        first = move(own, links.y_or_x)
        both = own if late is None else jnp.concatenate([late, own], axis=2)
        both = move(both, links.x_or_y)
        if late is not None:
            chunks[-1].append((both, 0))
        chunks.append([(own, 0), (first, 0), (both, 0 if late is None else late.shape[2])])
        late = first
        across = (both, *visit(i, chunks))
    chunks[-1].append((move(after(late, *across[1:]), links.x_or_y), 0))
    return chunks


class CoreSwap:
    def __init__(self, links):
        self.pairs, self.moved = links.core, {}

    def __call__(self, chunk, *gates):
        for part, _ in chunk:
            if id(part) not in self.moved:
                self.moved[id(part)] = move(after(part, *gates), self.pairs)
        return chunk + [(self.moved[id(part)], start) for part, start in chunk]

    def early(self, chunk, count, *gates):
        moved = self(chunk[:count], *gates)
        return [part for part, _ in moved[count:]]


class Piece:
    def __init__(self, keep, other, odd):
        self.terms, self.t = [keep, other], keep.shape[3]
        self.odd = odd
        self.late = []

    def mine(self, meta):
        both = meta[MINE_F], meta[MINE_S]
        return both[::-1] if self.odd else both


class Step:
    def __init__(self):
        self.arrays, self.views, self.jobs, self.outs = [], [], [], []

    def load(self, array, shape, view):
        self.views.append((self.place(array), shape, view))
        return len(self.views) - 1

    def place(self, array):
        for i, known in enumerate(self.arrays):
            if known is array:
                return i
        self.arrays.append(array)
        return len(self.arrays) - 1

    def out(self, shape, dtype):
        self.outs.append((shaped(dtype, *shape), None))
        return len(self.outs) - 1

    def swap(self, firsts=(), seconds=()):
        at = 0
        out = len(self.outs)
        for piece in seconds:
            self.second(piece, out, at)
            piece.next, at = at, at + 4 * piece.t
        for piece in firsts:
            self.first(piece, out, at)
            piece.next, at = at, at + 8 * piece.t
        self.out((at, 128, 128), BF)

    def first(self, piece, out, at):
        def view(ref, meta):
            return ref.at[1 - piece.mine(meta)[0]]

        loads = [self.load(a, a.shape[1:], view) for a in piece.terms]
        n = 8 * piece.t

        def job(meta, got, outs):
            values = sum(got[i][...].astype(F32) for i in loads)
            outs[out][at : at + n] = values.astype(BF).reshape(n, 128, 128)

        self.jobs.append((job, len(self.views)))

    def second(self, piece, out, at):
        n = 4 * piece.t
        ((late, start),) = piece.late

        def view(ref, meta):
            f, s = piece.mine(meta)
            return ref.at[f, 1 - s]

        def late_view(ref, meta):
            return ref.at[pl.ds(start + (1 - piece.mine(meta)[1]) * n, n)]

        loads = [self.load(a, a.shape[2:], view) for a in piece.terms]
        loads.append(self.load(late, (n, 128, 128), late_view))

        def job(meta, got, outs):
            values = sum(got[i][...].reshape(n, 128, 128).astype(F32) for i in loads)
            outs[out][at : at + n] = values.astype(BF)

        self.jobs.append((job, len(self.views)))

    def along(self, piece, sums=()):
        t = piece.t
        (one, start_one), (two, start_two) = piece.late

        def view(ref, meta):
            f, s = piece.mine(meta)
            return ref.at[f, s]

        def view_one(ref, meta):
            return ref.at[pl.ds(start_one + piece.mine(meta)[1] * 4 * t, 4 * t)]

        def view_two(ref, meta):
            return ref.at[pl.ds(start_two, 4 * t)]

        loads = [self.load(a, a.shape[2:], view) for a in piece.terms]
        late = [self.load(one, (4 * t, 128, 128), view_one)]
        late.append(self.load(two, (4 * t, 128, 128), view_two))
        extra = [
            (self.load(a, a.shape, lambda ref, meta: ref), row, scale, shift)
            for a, row, scale, shift in sums
        ]
        out = len(self.outs)
        for k in range(4):
            self.out((t + bool(sums), 128, 128), BF if k else F32)

        def job(meta, got, outs):
            for k in range(4):
                z = meta[ZPOS] ^ k
                dtype = BF if k else F32
                values = sum(got[i][z].astype(F32) for i in loads)
                values += sum(got[i][pl.ds(z * t, t)].astype(F32) for i in late)
                outs[out + k][:t] = values.astype(dtype)
                if extra:
                    outs[out + k][t] = jnp.zeros((128, 128), dtype)
                    for x in range(2):
                        rows = [
                            got[i][row : row + 1, span((z * 2 + x) * scale + shift, 128)]
                            for i, row, scale, shift in extra
                        ]
                        rows += [jnp.zeros((16 - len(rows), 128), F32)]
                        rows = jnp.concatenate(rows, axis=0).astype(dtype)
                        outs[out + k][t, 16 * x : 16 * x + 16] = rows

        self.jobs.append((job, len(self.views)))

    def share(self, groups):
        loads = [
            [self.load(a, a.shape, lambda ref, meta: ref) for a in arrays] for arrays in groups
        ]
        sizes = [arrays[0].shape[0] for arrays in groups]
        out = self.out((sum(sizes), 128, 128), BF)

        def job(meta, got, outs):
            at = 0
            for slots, size in zip(loads, sizes):
                outs[out][at : at + size] = sum(got[i][...].astype(F32) for i in slots).astype(BF)
                at += size

        self.jobs.append((job, len(self.views)))

    def small(self, arrays):
        tile = arrays[0].shape[0] - 1
        loads = [self.load(a, (128, 128), lambda ref, meta: ref.at[tile]) for a in arrays]
        out = self.out((16, 128), F32)
        self.out((16, 128), F32)

        def job(meta, got, outs):
            for k in range(2):
                rows = span(meta[XPOS] if k else 1 - meta[XPOS], 16)
                outs[out + k][...] = sum(got[i][rows, :].astype(F32) for i in loads)

        self.jobs.append((job, len(self.views)))

    def run(self, meta, name):
        count, total = len(self.arrays), len(self.outs)

        def kernel(meta, *refs):
            outs, got, sems = refs[count : count + total], refs[count + total : -1], refs[-1]
            copies = [
                pltpu.make_async_copy(view(refs[i], meta), got[j], sems.at[j])
                for j, (i, _, view) in enumerate(self.views)
            ]
            for copy in copies:
                copy.start()
            ready = 0
            for job, last in self.jobs:
                for copy in copies[ready:last]:
                    copy.wait()
                ready = last
                job(meta, got, outs)

        return call(
            kernel,
            meta,
            [(a, ANY) for a in self.arrays],
            self.outs,
            12,
            cost(1, 1),
            name,
            [pltpu.VMEM(shape, self.arrays[i].dtype) for i, shape, _ in self.views]
            + [pltpu.SemaphoreType.DMA((len(self.views),))],
        )


def fetch(meta, parts, starts, whole, columns, sem, skip=0):
    first, n = columns
    if len(parts) == 1:
        source = parts[0].at[:, pl.ds(skip + first, n)]
        pltpu.make_async_copy(source, whole.at[:, pl.ds(first, n)], sem).start()
        return
    core, y, x, z = meta[CORE], meta[YPOS], meta[XPOS], meta[ZPOS]
    for i, (part, start) in enumerate(zip(parts, starts)):
        source = core if i < 4 else 1 - core
        dx = (0, source, 1 - source, 1)[i % 4]
        dy = (0, 1 - source, source, 1)[i % 4]
        for dz in range(4):
            block = (((z ^ dz) * 2 + (x ^ dx)) * 2 + source) * 2 + (y ^ dy)
            pltpu.make_async_copy(
                part.at[dz, :, pl.ds(start + skip + first, n)],
                whole.at[span(block, part.shape[1]), pl.ds(first, n)],
                sem,
            ).start()


def fetched(whole, columns, sem):
    first, n = columns
    here = whole.at[:, pl.ds(first, n)]
    pltpu.make_async_copy(here, here, sem).wait()


def normed_rows(values):
    centred = values - jnp.mean(values, axis=-1, keepdims=True)
    scale = lax.rsqrt(jnp.mean(centred * centred, axis=-1, keepdims=True) + EPS)
    return centred * scale, scale


def norm_back(grad, normed, scale):
    mean_one = jnp.mean(grad, axis=-1, keepdims=True)
    mean_two = jnp.mean(grad * normed, axis=-1, keepdims=True)
    return scale * (grad - mean_one - normed * mean_two)


def first_norm(meta, x, tables):
    rows, width = x.shape
    tm = 256
    last = tables[0].shape[2] - 128

    def kernel(meta, x_ref, *refs):
        parts, (first_ref, small_ref, table, sems) = refs[:3], refs[3:]
        copies = [
            pltpu.make_async_copy(ref.at[:, pl.ds(0, 16), pl.ds(last, 128)], table.at[i], sems.at[i])
            for i, ref in enumerate(parts)
        ]
        for copy in copies:
            copy.start()
        for copy in copies:
            copy.wait()
        x, z = meta[XPOS], meta[ZPOS]
        for dz in range(4):
            own, one, two = (table[i, dz].astype(F32) for i in range(3))
            for dx, values in enumerate((own, jnp.where(meta[CORE] == 1, one, two))):
                small_ref[:, span((z ^ dz) * 2 + (x ^ dx), 128)] = values

        @pl.loop(0, rows // tm)
        def _(i):
            normed, _ = normed_rows(x_ref[span(i, tm), :].astype(F32))
            first = normed * small_ref[G1 : G1 + 1, :] + small_ref[B1 : B1 + 1, :]
            first_ref[span(i, tm), :] = first.astype(BF)

    return call(
        kernel,
        meta,
        [(x, None)] + [(a, ANY) for a in tables],
        [(VMEM((rows, width), BF), None), (shaped(F32, 16, width), None)],
        16,
        cost(rows * width * 20, rows * width * 4),
        "first_norm",
        [pltpu.VMEM((3, 4, 16, 128), BF), pltpu.SemaphoreType.DMA((3,))],
    )


def attention_forward(meta, first, small, parts, base, images):
    rows, width = first.shape
    length, n = rows // images, 3 * SIZE
    parts, starts = zip(*parts)
    count = len(parts)
    columns = (0, GROUP * n)

    def kernel(meta, first_ref, small_ref, *refs):
        parts, refs = refs[:count], refs[count:]
        packed_ref, probs_ref, mixed_ref, weight_out, weight_ref, sems = refs
        head = pl.program_id(0)
        keep = pltpu.make_async_copy(weight_ref, weight_out, sems.at[1])

        @pl.when(head == 0)
        def _():
            fetch(meta, parts, starts, weight_ref, columns, sems.at[0])
            fetched(weight_ref, columns, sems.at[0])
            keep.start()

        here = span(base + head, SIZE)
        bias_q, bias_v = small_ref[BQ : BQ + 1, here], small_ref[BV : BV + 1, here]
        bias = jnp.concatenate([bias_q, jnp.zeros_like(bias_q), bias_v], axis=1)
        packed = (dot(first_ref[...], weight_ref[:, span(head, n)]) + bias).astype(BF)
        packed_ref[...] = packed
        for i in range(images):
            part = packed[i * length : (i + 1) * length]
            q, k, v = part[:, :SIZE], part[:, SIZE : 2 * SIZE], part[:, 2 * SIZE :]
            scores = dot(q, k, NT)
            top = jnp.max(scores, axis=-1, keepdims=True)
            raised = jnp.exp2((scores - top) * (SCALE * LOG2E))
            probs = raised * (1.0 / jnp.sum(raised, axis=-1, keepdims=True))
            probs = probs.astype(BF)
            probs_ref[0, i] = probs
            mixed_ref[i * length : (i + 1) * length, span(head, SIZE)] = dot(probs, v).astype(BF)

        @pl.when(head == GROUP - 1)
        def _():
            keep.wait()

    return call(
        kernel,
        meta,
        [(first, None), (small, None)] + [(p, ANY) for p in parts],
        [
            (HBM((rows, GROUP * n), BF), pl.BlockSpec((rows, n), lambda h, m: (0, h))),
            (
                HBM((GROUP, images, length, length), BF),
                pl.BlockSpec((1, images, length, length), lambda h, m: (h, 0, 0, 0)),
            ),
            (VMEM((rows, GROUP * SIZE), BF), None),
            (HBM((width, GROUP * n), BF), ANY),
        ],
        20,
        cost(
            2 * rows * width * GROUP * n * 2 + 8 * rows * length * SIZE * GROUP,
            2 * (rows * width + width * n * GROUP * 2 + rows * n * GROUP + GROUP * rows * length),
            GROUP * rows * length,
        ),
        "attention_forward",
        [pltpu.VMEM((width, GROUP * n), BF), pltpu.SemaphoreType.DMA((2,))],
        (GROUP,),
    )


def store_piece(owner, odd, piece_ref, at, values, y):
    rows = values.shape[0] // 8
    for z in range(4):
        for x in range(2):
            plain = owner == (1 if odd else 0)
            first = jnp.where(plain, x, y)
            second = jnp.where(plain, y, x)
            start = (z * 2 + x) * rows
            for j in range(values.shape[1] // 128):
                part = values[start : start + rows, j * 128 : (j + 1) * 128]
                piece_ref[first, second, z, at + j] = part.astype(BF)


def blocks(rows):
    size = min(256, rows)

    def over(body):
        pl.loop(0, rows // size)(lambda i: body(span(i, size), i))

    return over


def feed_forward_first(meta, x, small, mixed, parts):
    rows, width = x.shape
    parts, starts = zip(*parts)
    count = len(parts)

    def kernel(meta, x_ref, small_ref, *refs):
        mixed_refs, parts = refs[: len(mixed)], refs[len(mixed) : len(mixed) + count]
        middle_ref, second_ref, active_ref, slope_ref, whole, sems = refs[len(mixed) + count :]
        for j in range(2):
            fetch(meta, parts, starts, whole, (j * width, width), sems.at[j])

        def row(r):
            return small_ref[r : r + 1, :]

        fetched(whole, (0, width), sems.at[0])

        @blocks(rows)
        def _(here, i):
            values = jnp.concatenate([r[here, :] for r in mixed_refs], axis=1)
            middle = x_ref[here, :].astype(F32) + dot(values, whole[:, :width]) + row(BO)
            middle_ref[here, :] = middle
            normed, _ = normed_rows(middle)
            second = (normed * row(G2) + row(B2)).astype(BF)
            second_ref[here, :] = second

            @pl.when(i == 0)
            def _():
                fetched(whole, (width, width), sems.at[1])

            v = dot(second, whole[:, width:]) + row(BU)
            square = v * v
            half = 0.5 * jnp.tanh(v * (GELU + (GELU * CUBIC) * square)) + 0.5
            active = v * half
            active_ref[here, :] = active.astype(BF)
            slope = (1.0 - half) * active * (2 * GELU + (6 * GELU * CUBIC) * square)
            slope_ref[here, :] = (half + slope).astype(BF)

    return call(
        kernel,
        meta,
        [(x, None), (small, None)] + [(a, None) for a in mixed] + [(p, ANY) for p in parts],
        [
            (VMEM((rows, width), F32), None),
            (VMEM((rows, width), BF), None),
            (VMEM((rows, width), BF), None),
            (VMEM((rows, width), BF), None),
        ],
        24,
        cost(4 * rows * width * width, 2 * 9 * rows * width, rows * width),
        "feed_forward_first",
        [pltpu.VMEM((width, 2 * width), BF), pltpu.SemaphoreType.DMA((2,))],
    )


def store_grads(meta, both, m, left_ref, right_ref, odd):
    half = right_ref.shape[1] // 2

    @pl.loop(0, 2)
    def _(core):
        values = dot(left_ref[...], right_ref[:, span(core, half)]).astype(BF)
        for y in range(2):
            part = values[:, y * half // 2 : (y + 1) * half // 2]
            store_piece(core, odd, both.at[core], 2 * m, part, y)


def send_grads(meta, both, m, pieces, sems):
    tiles = pl.ds(2 * m, 2)
    copies = [
        pltpu.make_async_copy(
            both.at[meta[half], :, :, :, tiles], piece.at[:, :, :, tiles], sems.at[2 * m + i]
        )
        for i, (half, piece) in enumerate(zip((THEIRS, OURS), pieces))
    ]
    for copy in copies:
        copy.start()
    return copies


def feed_forward_second(meta, cot, small, middle, second, active, slope, parts):
    rows, width = cot.shape
    parts, starts = zip(*parts)
    count = len(parts)

    def kernel(meta, cot_ref, small_ref, middle_ref, second_ref, active_ref, slope_ref, *refs):
        parts, refs = refs[:count], refs[count:]
        out_ref, hidden_ref, *pieces, sums_ref, whole, out, flipped, halves, sems = refs
        fetch(meta, parts, starts, whole, (0, width), sems.at[4])
        flipped[...] = active_ref[...].T
        store_grads(meta, halves, 0, flipped, cot_ref, False)
        copies = send_grads(meta, halves, 0, pieces, sems)
        fetched(whole, (0, width), sems.at[4])

        @blocks(width)
        def _(here, _):
            grad = dot(cot_ref[...], whole[here, :], NT)
            hidden_ref[:, here] = (slope_ref[:, here].astype(F32) * grad).astype(BF)

        flipped[...] = second_ref[...].T
        store_grads(meta, halves, 1, flipped, hidden_ref, False)
        copies += send_grads(meta, halves, 1, pieces, sems)

        def write(here):
            return pltpu.make_async_copy(out.at[:, here], out_ref.at[:, here], sems.at[5])

        @blocks(width)
        def _(here, _):
            values = middle_ref[:, here] + dot(active_ref[...], whole[:, here])
            out[:, here] = (values + small_ref[BD : BD + 1, here]).astype(BF)
            write(here).start()

        sums_ref[...] = jnp.zeros_like(sums_ref)
        sums_ref[0:1, :] = column_sum(hidden_ref[...])
        sums_ref[1:2, :] = column_sum(cot_ref[...])
        for copy in (write(pl.ds(0, width)), *copies):
            copy.wait()

    shape = (2, 2, 4, 4, width // 8, 128)
    piece = VMEM(shape, BF)
    return call(
        kernel,
        meta,
        [(a, None) for a in (cot, small, middle, second, active, slope)]
        + [(p, ANY) for p in parts],
        [
            (HBM((rows, width), BF), ANY),
            (VMEM((rows, width), BF), None),
            (piece, ANY),
            (piece, ANY),
            (shaped(F32, 8, width), None),
        ],
        24,
        cost(8 * rows * width * width, 2 * 12 * rows * width),
        "feed_forward_second",
        [
            pltpu.VMEM((width, width), BF),
            pltpu.VMEM((rows, width), BF),
            pltpu.VMEM((width, rows), BF),
            pltpu.VMEM((2, *shape), BF),
            pltpu.SemaphoreType.DMA((6,)),
        ],
    )


def feed_forward_third(meta, cot, small, middle, mixed, hidden, parts):
    rows, width = cot.shape
    parts, starts = zip(*parts)
    count = len(parts)

    def kernel(meta, cot_ref, small_ref, middle_ref, hidden_ref, *refs):
        mixed_refs, parts = refs[: len(mixed)], refs[len(mixed) : len(mixed) + count]
        attn_ref, *pieces, sums_ref, whole, flipped, halves, sem, sems = refs[len(mixed) + count :]
        fetch(meta, parts, starts, whole, (0, width), sem, width)
        fetched(whole, (0, width), sem)
        sums_ref[...] = jnp.zeros_like(sums_ref)

        @blocks(rows)
        def _(here, _):
            grad_second = dot(hidden_ref[here, :], whole[...], NT)
            normed, scale = normed_rows(middle_ref[here, :])
            back = norm_back(grad_second * small_ref[G2 : G2 + 1, :], normed, scale)
            grad_attn = (cot_ref[here, :].astype(F32) + back).astype(BF)
            attn_ref[here, :] = grad_attn
            sums_ref[0:1, :] += column_sum(grad_second * normed)
            sums_ref[1:2, :] += column_sum(grad_second)
            sums_ref[2:3, :] += column_sum(grad_attn)

        for i, ref in enumerate(mixed_refs):
            n = ref.shape[1]
            flipped[i * n : (i + 1) * n, :] = ref[...].T
        store_grads(meta, halves, 0, flipped, attn_ref, True)
        for copy in send_grads(meta, halves, 0, pieces, sems):
            copy.wait()

    shape = (2, 2, 4, 2, width // 8, 128)
    piece = VMEM(shape, BF)
    return call(
        kernel,
        meta,
        [(a, None) for a in (cot, small, middle, hidden, *mixed)] + [(p, ANY) for p in parts],
        [(VMEM((rows, width), BF), None), (piece, ANY), (piece, ANY), (shaped(F32, 8, width), None)],
        20,
        cost(4 * rows * width * width, 2 * 12 * rows * width),
        "feed_forward_third",
        [
            pltpu.VMEM((width, width), BF),
            pltpu.VMEM((width, rows), BF),
            pltpu.VMEM((2, *shape), BF),
            pltpu.SemaphoreType.DMA,
            pltpu.SemaphoreType.DMA((2,)),
        ],
    )


def mixed_grad(meta, grad_attn, parts):
    rows, width = grad_attn.shape
    parts, starts = zip(*parts)
    count = len(parts)

    def kernel(meta, attn_ref, *refs):
        parts, (grad_ref, attn_out, whole, sems) = refs[:count], refs[count:]
        write = pltpu.make_async_copy(attn_ref, attn_out, sems.at[1])
        write.start()
        fetch(meta, parts, starts, whole, (0, width), sems.at[0])
        fetched(whole, (0, width), sems.at[0])

        @blocks(rows)
        def _(here, _):
            grad_ref[here, :] = dot(attn_ref[here, :], whole[...], NT).astype(BF)

        write.wait()

    return call(
        kernel,
        meta,
        [(grad_attn, None)] + [(p, ANY) for p in parts],
        [(VMEM((rows, width), BF), None), (HBM((rows, width), BF), ANY)],
        16,
        cost(2 * rows * width * width, 2 * 4 * rows * width),
        "mixed_grad",
        [pltpu.VMEM((width, width), BF), pltpu.SemaphoreType.DMA((2,))],
    )


def attention_backward(meta, first, packed, probs, grad_mixed, mixed, base, half, images, odd):
    rows, width = first.shape
    length, n = rows // images, 3 * SIZE
    pair = GROUP // 2

    def kernel(
        meta, first_ref, packed_ref, probs_ref, grad_ref, mixed_ref, grad_packed_ref, piece_ref
    ):
        j = pl.program_id(0)
        head = meta[half] * pair + j

        @pl.loop(0, images)
        def _(i):
            here = span(i, length)
            packed = packed_ref[here, :]
            q, k, v = packed[:, :SIZE], packed[:, SIZE : 2 * SIZE], packed[:, 2 * SIZE :]
            grad = grad_ref[here, span(base + head, SIZE)]
            mixed = mixed_ref[here, span(head, SIZE)]
            inner = jnp.sum(grad.astype(F32) * mixed.astype(F32), axis=-1, keepdims=True)
            probs = probs_ref[0, i]
            grad_v = dot(probs, grad, TN)
            grad_scores = (probs.astype(F32) * (dot(grad, v, NT) - inner)).astype(BF)
            grad_q = dot(grad_scores, k) * SCALE
            grad_k = dot(grad_scores, q, TN) * SCALE
            grad_packed_ref[here, :] = jnp.concatenate(
                [grad_q.astype(BF), grad_k.astype(BF), grad_v.astype(BF)], axis=1
            )

        values = dot(first_ref[...], grad_packed_ref[...], TN)
        store_piece(meta[half], odd, piece_ref, 0, values, j)

    return call(
        kernel,
        meta,
        [
            (first, None),
            (hbm(packed), pl.BlockSpec((rows, n), lambda j, m: (0, m[half] * pair + j))),
            (
                hbm(probs),
                pl.BlockSpec(
                    (1, images, length, length), lambda j, m: (m[half] * pair + j, 0, 0, 0)
                ),
            ),
            (grad_mixed, None),
            (mixed, None),
        ],
        [
            (HBM((rows, pair * n), BF), pl.BlockSpec((rows, n), lambda j, m: (0, j))),
            (VMEM((2, 2, 4, 3, width // 8, SIZE), BF), None),
        ],
        20,
        cost(
            pair * (2 * rows * width * n * 1.5 + 10 * rows * length * SIZE * 1.5),
            2 * (rows * width + pair * (rows * length + 3 * rows * n)),
        ),
        "attention_backward",
        grid=(pair,),
    )


def input_grad(meta, x, grad_attn, small, pieces, weights):
    rows, width = x.shape
    tm = min(256, rows)
    groups = len(weights)
    n = pieces[0].shape[1]

    def kernel(meta, x_ref, grad_ref, small_ref, *refs):
        pieces, weights = refs[: 2 * groups], refs[2 * groups : 3 * groups]
        out_ref, sums_ref, packed_sums_ref = refs[3 * groups :]

        @pl.when(pl.program_id(0) == 0)
        def _():
            sums_ref[...] = jnp.zeros_like(sums_ref)
            packed_sums_ref[...] = jnp.zeros_like(packed_sums_ref)

        grad = None
        for g in range(groups):
            for j, which in enumerate((THEIRS, OURS)):
                piece = pieces[2 * g + j][...]
                term = dot(piece, weights[g][:, span(meta[which], n)], NT)
                grad = term if grad is None else grad + term
                packed_sums_ref[0:1, span(2 * g + meta[which], n)] += column_sum(piece)
        normed, scale = normed_rows(x_ref[...].astype(F32))
        back = norm_back(grad * small_ref[G1 : G1 + 1, :], normed, scale)
        out_ref[...] = (grad_ref[...].astype(F32) + back).astype(BF)
        sums_ref[0:1, :] += column_sum(grad * normed)
        sums_ref[1:2, :] += column_sum(grad)

    block = pl.BlockSpec((tm, width), lambda i, m: (i, 0))
    return call(
        kernel,
        meta,
        [(hbm(x), block), (hbm(grad_attn), block), (small, None)]
        + [(hbm(p), pl.BlockSpec((tm, n), lambda i, m: (i, 0))) for p in pieces]
        + [(w, None) for w in weights],
        [
            (HBM((rows, width), BF), block),
            (shaped(F32, 8, width), None),
            (shaped(F32, 8, 3 * width), None),
        ],
        24,
        cost(6 * rows * width * width * 1.3, 2 * 9 * rows * width),
        "input_grad",
        grid=(rows // tm,),
    )


def quarter_of(meta, i):
    return (meta[CORE] ^ (i % 2)) * 2 + (meta[YPOS] ^ (i // 2))


def finish(meta, groups, places, widths, name):
    quarters = [q for group in groups for q in group]
    rows = quarters[0].shape[1]

    def kernel(meta, *refs):
        outs = refs[len(quarters) :]
        for g, place in enumerate(places):
            for i in range(4):
                part = refs[4 * g + i]
                for j in range(min(part.shape[0], len(widths) * widths[0] // 128 // 4 // len(groups))):
                    which, column = place(quarter_of(meta, i), j)
                    outs[which][:, span(column, 128)] = part[j].astype(F32)

    outs = [(shaped(F32, rows, n), None) for n in widths]
    return call(kernel, meta, [(a, None) for a in quarters], outs, 8, cost(1, 1), name)


def by_head(weight, base):
    rows = weight.shape[0]
    view = weight.reshape(rows, 3, HEADS, SIZE)[:, :, base : base + GROUP]
    return view.transpose(0, 2, 1, 3).reshape(rows, GROUP * 3 * SIZE)


def per_device(latents, w_qkv, w_out, w_up, w_down, gains, biases, ff_bias, cotangent, *, nb, nr):
    reps, images, length, width = latents.shape
    x = latents.reshape(-1, width)
    cot = cotangent.reshape(-1, width)
    count = reps * images
    bases = range(0, HEADS, GROUP)
    native = nb != 8 or nr != 4
    small = jnp.concatenate([gains, biases, ff_bias[None]], axis=0)
    small = jnp.pad(small, ((0, 16 - small.shape[0]), (0, 0)))
    if native:
        links = None
        zero = jnp.zeros((), jnp.int32)
        meta = jnp.stack([zero, zero, zero, zero, zero + 1, zero, zero, zero])

        def whole(w):
            return [(lax.all_gather(w, "batch", axis=0, tiled=True), 0)]

        table = lax.all_gather(small, "batch", axis=1, tiled=True)
        table = table.reshape(16, 4, 2, width // 8).transpose(2, 1, 0, 3)
        first, small = first_norm(meta, x, [table[0], table[1], table[1]])
        chunks = [whole(by_head(w_qkv, base)) for base in bases]
        chunks += [whole(jnp.concatenate([w_out, w_up], axis=1)), whole(w_down)]
    else:
        links = Links(nb, nr)
        mine_f = jnp.where(links.ci == 0, links.xi, links.yi)
        mine_s = jnp.where(links.ci == 0, links.yi, links.xi)
        meta = [links.ci, links.yi, links.xi, links.zi, 1 - links.ci, links.ci, mine_f, mine_s]
        meta = jnp.stack(meta).astype(jnp.int32)

        def quarter(w):
            rows = w.shape[0] // 4
            return lax.dynamic_slice_in_dim(w, (links.ci * 2 + links.yi) * rows, rows, 0)

        w_qkv = quarter(w_qkv)
        chunks = [by_head(w_qkv, base) for base in bases]
        extra = jnp.pad(small, ((0, w_qkv.shape[0] - 16), (0, 0)))
        chunks[0] = jnp.concatenate([chunks[0], extra], axis=1)
        chunks += [jnp.concatenate([quarter(w_out), quarter(w_up)], axis=1), quarter(w_down)]
        other = CoreSwap(links)

        def visit(i, chunks):
            if i == 0:
                return ()
            if i == 1:
                kept.extend(first_norm(meta, x, [part for part, _ in chunks[0][:3]]))
                return kept + other.early(chunks[0], 3)
            gates = other.early(chunks[i - 1], 2) + forward(i - 2, chunks[i - 2])
            return gates + other.early(chunks[i], 2, *mixed) if i == 3 else gates

    packed, probs, mixed, weights, kept = [], [], [], [], []

    def forward(i, parts):
        parts = parts if native else other(parts, *mixed)
        a, b, c, d = attention_forward(meta, kept[0], kept[1], parts, bases[i], count)
        packed.append(a)
        probs.append(b)
        mixed.append(c)
        weights.append(d)
        return [c]

    if native:
        kept.extend((first, small))
        for i in range(len(bases)):
            forward(i, chunks[i])
    else:
        chunks = gather_chunks(chunks, links, visit)
        for i in range(len(mixed), len(bases)):
            forward(i, chunks[i])
        first, small = kept
    outer, inner = chunks[len(bases) :]
    outer = outer if native else other(outer, mixed[1])
    middle, second, active, slope = feed_forward_first(meta, x, small, mixed, outer)
    inner = inner if native else other(inner, active)
    out, hidden, send, keep, sums_two = feed_forward_second(
        meta, cot, small, middle, second, active, slope, inner
    )
    grad_attn, send_out, keep_out, sums_three = feed_forward_third(
        meta, cot, small, middle, mixed, hidden, outer
    )

    def backward(meta, g, half):
        return attention_backward(
            meta, first, packed[g], probs[g], grad_mixed, mixed[g], bases[g], half, count, g == 1
        )

    def collect(sums_one, sums_packed):
        sums_packed = sums_packed[0].reshape(HEADS, 3, SIZE)
        sums_q, sums_v = sums_packed[:, 0].reshape(width), sums_packed[:, 2].reshape(width)
        out, two, three = sums_three[2], sums_two, sums_three
        rows = [sums_one[0], three[0], sums_one[1], sums_q, sums_v, out, three[1], two[1], two[0]]
        return jnp.stack(rows)

    def sums_of(sums_one, sums_packed):
        two, three, one, packed = sums_two, sums_three, sums_one, sums_packed
        plain = [(one, 0), (three, 0), (one, 1), None, None, (three, 2), (three, 1), (two, 1), (two, 0)]
        sums = [entry and (*entry, 1, 0) for entry in plain]
        sums[3], sums[4] = (packed, 0, 3, 0), (packed, 0, 3, 2)
        return sums

    def result(grad_x, grads, smalls):
        return (
            out.reshape(latents.shape),
            grad_x.reshape(latents.shape),
            *grads,
            smalls[:2],
            smalls[2:8],
            smalls[8],
        )

    if native:
        grad_mixed, grad_attn = mixed_grad(meta, grad_attn, outer)
        halves = [[backward(meta, g, half) for half in (THEIRS, OURS)] for g in range(len(bases))]
        pieces = [half[0] for pair in halves for half in pair]
        grad_x, sums_one, sums_packed = input_grad(meta, x, grad_attn, small, pieces, weights)
        smalls = lax.psum_scatter(
            collect(sums_one, sums_packed), "batch", scatter_dimension=1, tiled=True
        )
        smalls = lax.psum(smalls, "rep")

        def reduced(send, keep, odd):
            keep, send = (jnp.swapaxes(keep, 0, 1), send) if odd else (keep, jnp.swapaxes(send, 0, 1))
            both = jnp.stack([keep, send])
            t = both.shape[4]
            both = both.transpose(3, 1, 5, 0, 2, 4, 6).reshape(width, t * 4 * 128)
            both = lax.psum_scatter(both, "batch", scatter_dimension=0, tiled=True)
            both = lax.psum(both.astype(BF), "rep").astype(F32)
            return both.reshape(-1, 4, t, 128)

        rest = [reduced(send_out, keep_out, True), reduced(send, keep, False)]
        rows = rest[0].shape[0]
        rest = [rest[0], rest[1][:, :, 2:], rest[1][:, :, :2]]
        rest = [g.reshape(rows, width) for g in rest]
        heads = [reduced(pair[0][1], pair[1][1], g == 1) for g, pair in enumerate(halves)]
        heads = jnp.concatenate(heads, axis=1).transpose(0, 2, 1, 3).reshape(rows, 3 * width)
        return result(grad_x, [heads, *rest], smalls)

    def to_core(value):
        return move(value, links.core)

    def along(arrays):
        return [arrays[0]] + [move(a, p) for a, p in zip(arrays[1:], links.z)]

    def share(value, *gates):
        by_y = move(value, links.y)
        own, theirs = (move(after(v, *gates), links.core) for v in (value, by_y))
        return [value, own, by_y, theirs]

    both = Piece(keep, to_core(send), False)
    step = Step()
    step.swap(firsts=[both])
    (sent,) = step.run(after(meta, keep_out), "step_0")
    both.late.append((move(sent, links.x_or_y), 0))
    grad_mixed, grad_attn = mixed_grad(after(meta, sent), grad_attn, outer)
    packed_1, send_1 = backward(after(meta, sent), 0, THEIRS)

    outs = Piece(keep_out, to_core(send_out), True)
    step = Step()
    step.swap(firsts=[outs], seconds=[both])
    (sent,) = step.run(after(meta, send_1), "step_1")
    moved = move(sent, links.y_or_x)
    for piece in (outs, both):
        piece.late.append((moved, piece.next))
    packed_2, keep_1 = backward(after(meta, sent), 0, OURS)
    packed_3, send_2 = backward(after(meta, sent, keep_1), 1, THEIRS)

    one = Piece(keep_1, to_core(send_1), False)
    step = Step()
    step.swap(firsts=[one], seconds=[outs])
    step.along(both)
    sent, *z_both = step.run(after(meta, send_2), "step_2")
    moved = move(sent, links.x_or_y)
    for piece in (one, outs):
        piece.late.append((moved, piece.next))
    z_both = along(z_both)
    packed_4, keep_2 = backward(after(meta, sent), 1, OURS)

    two = Piece(keep_2, to_core(send_2), True)
    step = Step()
    step.swap(firsts=[two], seconds=[one])
    step.along(outs)
    sent, *z_outs = step.run(after(meta, keep_2, *z_both[1:]), "step_3")
    moved = move(sent, links.y_or_x)
    for piece in (two, one):
        piece.late.append((moved, piece.next))
    z_outs = along(z_outs)
    pieces = [packed_1, packed_2, packed_3, packed_4]
    grad_x, sums_one, sums_packed = input_grad(
        after(meta, sent), x, grad_attn, small, pieces, weights
    )

    step = Step()
    step.along(one, sums_of(sums_one, sums_packed))
    z_one = step.run(after(meta, grad_x, *z_outs[1:]), "step_4")
    step = Step()
    step.swap(seconds=[two])
    (sent,) = step.run(after(meta, z_one[0]), "step_5")
    two.late.append((move(sent, links.x_or_y), 0))
    step = Step()
    step.share([z_both, z_outs])
    (r_rest,) = step.run(after(meta, sent), "step_6")
    z_one = along(z_one)
    r_rest = share(after(r_rest, z_one[1]))

    step = Step()
    step.along(two)
    z_two = step.run(after(meta, z_one[1]), "step_7")
    step = Step()
    step.share([z_one])
    (r_one,) = step.run(after(meta, z_two[0]), "step_8")
    z_two = along(z_two)
    r_one = after(r_one, z_two[1])

    step = Step()
    step.share([z_two])
    (r_two,) = step.run(meta, "step_9")
    r_one = share(r_one, r_two)
    step = Step()
    step.small(r_one)
    other, smalls = step.run(after(meta, r_two), "step_10")
    rest = finish(
        after(meta, other),
        [r_rest],
        [lambda q, j: (2 - j // 2, q * 2 + j % 2)],
        [width] * 3,
        "finish_rest",
    )
    r_two = share(r_two, rest[0])
    smalls = smalls + move(other, links.x)
    (heads,) = finish(
        meta,
        [r_one, r_two],
        [lambda q, j: (0, j * HEADS + q), lambda q, j: (0, j * HEADS + GROUP + q)],
        [3 * width],
        "finish_heads",
    )
    return result(grad_x, [heads, *rest], smalls)


def solution(mesh):
    nb, nr = mesh.shape["batch"], mesh.shape["rep"]

    def body(*args):
        return per_device(*args, nb=nb, nr=nr)

    rows = P("batch", None)
    cols = P(None, "batch")
    data = P("rep", "batch", None, None)
    return jax.shard_map(
        body,
        mesh=mesh,
        in_specs=(data, rows, rows, rows, rows, cols, cols, P("batch"), data),
        out_specs=(data, data, rows, rows, rows, rows, cols, cols, P("batch")),
        check_vma=False,
    )
```

```python
import functools

import jax
import jax.numpy as jnp
from jax import lax
from jax.experimental import pallas as pl
from jax.experimental.pallas import tpu as pltpu
from jax.sharding import PartitionSpec as P

HEADS = 8
SIZE = 128
GROUP = 4
EPS = 1e-05
AXES = ("batch", "rep")
BF = jnp.bfloat16
F32 = jnp.float32
NN, NT, TN = ((1,), (0,)), ((1,), (1,)), ((0,), (0,))
SCALE = SIZE ** (-0.5)
LOG2E = 1.4426950408889634
GELU = 0.7978845608028654
CUBIC = 0.044715
G1, G2, B1, BQ, BV, BO, B2, BD, BU = range(9)
CORE, YPOS, XPOS, ZPOS, THEIRS, OURS, MINE_F, MINE_S = range(8)


def dot(a, b, dims=NN):
    return lax.dot_general(a, b, (dims, ((), ())), preferred_element_type=F32)


HBM, VMEM = pltpu.HBM, pltpu.VMEM
ANY = pl.BlockSpec(memory_space=pl.ANY)


def call(kernel, meta, operands, outs, limit, estimate, name, scratch=(), grid=(1,)):
    shapes = [shape for shape, _ in outs]
    return pl.pallas_call(
        kernel,
        out_shape=shapes,
        grid_spec=pltpu.PrefetchScalarGridSpec(
            num_scalar_prefetch=1,
            grid=grid,
            in_specs=[spec or full(a) for a, spec in operands],
            out_specs=[spec or full(a) for a, spec in outs],
            scratch_shapes=scratch,
        ),
        compiler_params=pltpu.CompilerParams(vmem_limit_bytes=limit << 20),
        cost_estimate=estimate,
        name=name,
    )(meta, *[a for a, _ in operands])


def hbm(array):
    return pltpu.with_memory_space_constraint(array, HBM)


def shaped(dtype, *shape):
    return jax.ShapeDtypeStruct(shape, dtype)


def span(index, size):
    return pl.ds(pl.multiple_of(index * size, size), size)


def cost(flops, nbytes, trans=0):
    return pl.CostEstimate(flops=1, bytes_accessed=1, transcendentals=0)


def full(array):
    rank = len(array.shape)
    return pl.BlockSpec(array.shape, lambda *_: (0,) * rank)


def column_sum(values):
    return jnp.sum(values.astype(F32), axis=0, keepdims=True)


def permutation(target, nb, nr):
    pairs = []
    for b in range(nb):
        for r in range(nr):
            tb, tr = target(b, r)
            pairs.append((b * nr + r, tb * nr + tr))
    return pairs


class Links:
    def __init__(self, nb, nr):
        def swap(kb, kr):
            return permutation(lambda b, r: (b ^ kb, r ^ kr), nb, nr)

        self.core = swap(0, 1)
        self.rep = [swap(0, 1), swap(0, 2), swap(0, 3)]
        self.x = swap(1, 0)
        self.y = swap(0, 2)
        self.z = [swap(2, 0), swap(4, 0), swap(6, 0)]
        self.y_or_x = permutation(lambda b, r: (b, r ^ 2) if r % 2 == 0 else (b ^ 1, r), nb, nr)
        self.x_or_y = permutation(lambda b, r: (b ^ 1, r) if r % 2 == 0 else (b, r ^ 2), nb, nr)
        batch, rep = lax.axis_index("batch"), lax.axis_index("rep")
        self.xi, self.zi = batch % 2, batch // 2
        self.ci, self.yi = rep % 2, rep // 2


def move(value, pairs):
    return lax.ppermute(value, AXES, pairs)


def flip_if(bit, value, axis):
    return jnp.where(bit == 1, jnp.flip(value, axis), value)


def pick(value, axis, index):
    return lax.dynamic_index_in_dim(value, index, axis, keepdims=False)


def after(value, *others):
    return lax.optimization_barrier((value, *others))[0]


def gather_chunks(quarters, links, visit):
    chunks = []
    along, across = (), ()
    late = None
    for i, quarter in enumerate(quarters):
        quarter = after(quarter, *along)
        along = [move(quarter, p) for p in links.z]
        ahead = quarters[1:] if i == 0 else ()
        own = jnp.stack([after(quarter, *across, *ahead)] + along)
        first = move(own, links.y_or_x)
        both = own if late is None else jnp.concatenate([late, own], axis=2)
        both = move(both, links.x_or_y)
        if late is not None:
            chunks[-1].append((both, 0))
        chunks.append([(own, 0), (first, 0), (both, 0 if late is None else late.shape[2])])
        late = first
        across = (both, *visit(i, chunks))
    chunks[-1].append((move(after(late, *across[1:]), links.x_or_y), 0))
    return chunks


class CoreSwap:
    def __init__(self, links):
        self.pairs, self.moved = links.core, {}

    def __call__(self, chunk, *gates):
        for part, _ in chunk:
            if id(part) not in self.moved:
                self.moved[id(part)] = move(after(part, *gates), self.pairs)
        return chunk + [(self.moved[id(part)], start) for part, start in chunk]

    def early(self, chunk, count, *gates):
        moved = self(chunk[:count], *gates)
        return [part for part, _ in moved[count:]]


class Piece:
    def __init__(self, keep, other, odd):
        self.terms, self.t = [keep, other], keep.shape[3]
        self.odd = odd
        self.late = []

    def mine(self, meta):
        both = meta[MINE_F], meta[MINE_S]
        return both[::-1] if self.odd else both


class Step:
    def __init__(self):
        self.arrays, self.views, self.jobs, self.outs = [], [], [], []

    def load(self, array, shape, view):
        self.views.append((self.place(array), shape, view))
        return len(self.views) - 1

    def place(self, array):
        for i, known in enumerate(self.arrays):
            if known is array:
                return i
        self.arrays.append(array)
        return len(self.arrays) - 1

    def out(self, shape, dtype):
        self.outs.append((shaped(dtype, *shape), None))
        return len(self.outs) - 1

    def swap(self, firsts=(), seconds=()):
        at = 0
        out = len(self.outs)
        for piece in seconds:
            self.second(piece, out, at)
            piece.next, at = at, at + 4 * piece.t
        for piece in firsts:
            self.first(piece, out, at)
            piece.next, at = at, at + 8 * piece.t
        self.out((at, 128, 128), BF)

    def first(self, piece, out, at):
        def view(ref, meta):
            return ref.at[1 - piece.mine(meta)[0]]

        loads = [self.load(a, a.shape[1:], view) for a in piece.terms]
        n = 8 * piece.t

        def job(meta, got, outs):
            values = sum(got[i][...].astype(F32) for i in loads)
            outs[out][at : at + n] = values.astype(BF).reshape(n, 128, 128)

        self.jobs.append((job, len(self.views)))

    def second(self, piece, out, at):
        n = 4 * piece.t
        ((late, start),) = piece.late

        def view(ref, meta):
            f, s = piece.mine(meta)
            return ref.at[f, 1 - s]

        def late_view(ref, meta):
            return ref.at[pl.ds(start + (1 - piece.mine(meta)[1]) * n, n)]

        loads = [self.load(a, a.shape[2:], view) for a in piece.terms]
        loads.append(self.load(late, (n, 128, 128), late_view))

        def job(meta, got, outs):
            values = sum(got[i][...].reshape(n, 128, 128).astype(F32) for i in loads)
            outs[out][at : at + n] = values.astype(BF)

        self.jobs.append((job, len(self.views)))

    def along(self, piece, sums=()):
        t = piece.t
        (one, start_one), (two, start_two) = piece.late

        def view(ref, meta):
            f, s = piece.mine(meta)
            return ref.at[f, s]

        def view_one(ref, meta):
            return ref.at[pl.ds(start_one + piece.mine(meta)[1] * 4 * t, 4 * t)]

        def view_two(ref, meta):
            return ref.at[pl.ds(start_two, 4 * t)]

        loads = [self.load(a, a.shape[2:], view) for a in piece.terms]
        late = [self.load(one, (4 * t, 128, 128), view_one)]
        late.append(self.load(two, (4 * t, 128, 128), view_two))
        extra = [
            (self.load(a, a.shape, lambda ref, meta: ref), row, scale, shift)
            for a, row, scale, shift in sums
        ]
        out = len(self.outs)
        for k in range(4):
            self.out((t + bool(sums), 128, 128), BF if k else F32)

        def job(meta, got, outs):
            for k in range(4):
                z = meta[ZPOS] ^ k
                dtype = BF if k else F32
                values = sum(got[i][z].astype(F32) for i in loads)
                values += sum(got[i][pl.ds(z * t, t)].astype(F32) for i in late)
                outs[out + k][:t] = values.astype(dtype)
                if extra:
                    outs[out + k][t] = jnp.zeros((128, 128), dtype)
                    for x in range(2):
                        rows = [
                            got[i][row : row + 1, span((z * 2 + x) * scale + shift, 128)]
                            for i, row, scale, shift in extra
                        ]
                        rows += [jnp.zeros((16 - len(rows), 128), F32)]
                        rows = jnp.concatenate(rows, axis=0).astype(dtype)
                        outs[out + k][t, 16 * x : 16 * x + 16] = rows

        self.jobs.append((job, len(self.views)))

    def share(self, groups):
        loads = [
            [self.load(a, a.shape, lambda ref, meta: ref) for a in arrays] for arrays in groups
        ]
        sizes = [arrays[0].shape[0] for arrays in groups]
        out = self.out((sum(sizes), 128, 128), BF)

        def job(meta, got, outs):
            at = 0
            for slots, size in zip(loads, sizes):
                outs[out][at : at + size] = sum(got[i][...].astype(F32) for i in slots).astype(BF)
                at += size

        self.jobs.append((job, len(self.views)))

    def small(self, arrays):
        tile = arrays[0].shape[0] - 1
        loads = [self.load(a, (128, 128), lambda ref, meta: ref.at[tile]) for a in arrays]
        out = self.out((16, 128), F32)
        self.out((16, 128), F32)

        def job(meta, got, outs):
            for k in range(2):
                rows = span(meta[XPOS] if k else 1 - meta[XPOS], 16)
                outs[out + k][...] = sum(got[i][rows, :].astype(F32) for i in loads)

        self.jobs.append((job, len(self.views)))

    def run(self, meta, name):
        count, total = len(self.arrays), len(self.outs)

        def kernel(meta, *refs):
            outs, got, sems = refs[count : count + total], refs[count + total : -1], refs[-1]
            copies = [
                pltpu.make_async_copy(view(refs[i], meta), got[j], sems.at[j])
                for j, (i, _, view) in enumerate(self.views)
            ]
            for copy in copies:
                copy.start()
            ready = 0
            for job, last in self.jobs:
                for copy in copies[ready:last]:
                    copy.wait()
                ready = last
                job(meta, got, outs)

        return call(
            kernel,
            meta,
            [(a, ANY) for a in self.arrays],
            self.outs,
            12,
            cost(1, 1),
            name,
            [pltpu.VMEM(shape, self.arrays[i].dtype) for i, shape, _ in self.views]
            + [pltpu.SemaphoreType.DMA((len(self.views),))],
        )


def fetch(meta, parts, starts, whole, columns, sem, skip=0):
    first, n = columns
    if len(parts) == 1:
        source = parts[0].at[:, pl.ds(skip + first, n)]
        pltpu.make_async_copy(source, whole.at[:, pl.ds(first, n)], sem).start()
        return
    core, y, x, z = meta[CORE], meta[YPOS], meta[XPOS], meta[ZPOS]
    for i, (part, start) in enumerate(zip(parts, starts)):
        source = core if i < 4 else 1 - core
        dx = (0, source, 1 - source, 1)[i % 4]
        dy = (0, 1 - source, source, 1)[i % 4]
        for dz in range(4):
            block = (((z ^ dz) * 2 + (x ^ dx)) * 2 + source) * 2 + (y ^ dy)
            pltpu.make_async_copy(
                part.at[dz, :, pl.ds(start + skip + first, n)],
                whole.at[span(block, part.shape[1]), pl.ds(first, n)],
                sem,
            ).start()


def fetched(whole, columns, sem):
    first, n = columns
    here = whole.at[:, pl.ds(first, n)]
    pltpu.make_async_copy(here, here, sem).wait()


def normed_rows(values):
    centred = values - jnp.mean(values, axis=-1, keepdims=True)
    scale = lax.rsqrt(jnp.mean(centred * centred, axis=-1, keepdims=True) + EPS)
    return centred * scale, scale


def norm_back(grad, normed, scale):
    mean_one = jnp.mean(grad, axis=-1, keepdims=True)
    mean_two = jnp.mean(grad * normed, axis=-1, keepdims=True)
    return scale * (grad - mean_one - normed * mean_two)


def first_norm(meta, x, tables):
    rows, width = x.shape
    tm = 256
    last = tables[0].shape[2] - 128

    def kernel(meta, x_ref, *refs):
        parts, (first_ref, small_ref, table, sems) = refs[:3], refs[3:]
        copies = [
            pltpu.make_async_copy(ref.at[:, pl.ds(0, 16), pl.ds(last, 128)], table.at[i], sems.at[i])
            for i, ref in enumerate(parts)
        ]
        for copy in copies:
            copy.start()
        for copy in copies:
            copy.wait()
        x, z = meta[XPOS], meta[ZPOS]
        for dz in range(4):
            own, one, two = (table[i, dz].astype(F32) for i in range(3))
            for dx, values in enumerate((own, jnp.where(meta[CORE] == 1, one, two))):
                small_ref[:, span((z ^ dz) * 2 + (x ^ dx), 128)] = values

        @pl.loop(0, rows // tm)
        def _(i):
            normed, _ = normed_rows(x_ref[span(i, tm), :].astype(F32))
            first = normed * small_ref[G1 : G1 + 1, :] + small_ref[B1 : B1 + 1, :]
            first_ref[span(i, tm), :] = first.astype(BF)

    return call(
        kernel,
        meta,
        [(x, None)] + [(a, ANY) for a in tables],
        [(VMEM((rows, width), BF), None), (shaped(F32, 16, width), None)],
        16,
        cost(rows * width * 20, rows * width * 4),
        "first_norm",
        [pltpu.VMEM((3, 4, 16, 128), BF), pltpu.SemaphoreType.DMA((3,))],
    )


def attention_forward(meta, first, small, parts, base, images):
    rows, width = first.shape
    length, n = rows // images, 3 * SIZE
    parts, starts = zip(*parts)
    count = len(parts)
    columns = (0, GROUP * n)

    def kernel(meta, first_ref, small_ref, *refs):
        parts, refs = refs[:count], refs[count:]
        packed_ref, probs_ref, mixed_ref, weight_out, weight_ref, sems = refs
        head = pl.program_id(0)
        keep = pltpu.make_async_copy(weight_ref, weight_out, sems.at[1])

        @pl.when(head == 0)
        def _():
            fetch(meta, parts, starts, weight_ref, columns, sems.at[0])
            fetched(weight_ref, columns, sems.at[0])
            keep.start()

        here = span(base + head, SIZE)
        bias_q, bias_v = small_ref[BQ : BQ + 1, here], small_ref[BV : BV + 1, here]
        bias = jnp.concatenate([bias_q, jnp.zeros_like(bias_q), bias_v], axis=1)
        packed = (dot(first_ref[...], weight_ref[:, span(head, n)]) + bias).astype(BF)
        packed_ref[...] = packed
        for i in range(images):
            part = packed[i * length : (i + 1) * length]
            q, k, v = part[:, :SIZE], part[:, SIZE : 2 * SIZE], part[:, 2 * SIZE :]
            scores = dot(q, k, NT)
            top = jnp.max(scores, axis=-1, keepdims=True)
            raised = jnp.exp2((scores - top) * (SCALE * LOG2E))
            probs = raised * (1.0 / jnp.sum(raised, axis=-1, keepdims=True))
            probs = probs.astype(BF)
            probs_ref[0, i] = probs
            mixed_ref[i * length : (i + 1) * length, span(head, SIZE)] = dot(probs, v).astype(BF)

        @pl.when(head == GROUP - 1)
        def _():
            keep.wait()

    return call(
        kernel,
        meta,
        [(first, None), (small, None)] + [(p, ANY) for p in parts],
        [
            (HBM((rows, GROUP * n), BF), pl.BlockSpec((rows, n), lambda h, m: (0, h))),
            (
                HBM((GROUP, images, length, length), BF),
                pl.BlockSpec((1, images, length, length), lambda h, m: (h, 0, 0, 0)),
            ),
            (VMEM((rows, GROUP * SIZE), BF), None),
            (HBM((width, GROUP * n), BF), ANY),
        ],
        20,
        cost(
            2 * rows * width * GROUP * n * 2 + 8 * rows * length * SIZE * GROUP,
            2 * (rows * width + width * n * GROUP * 2 + rows * n * GROUP + GROUP * rows * length),
            GROUP * rows * length,
        ),
        "attention_forward",
        [pltpu.VMEM((width, GROUP * n), BF), pltpu.SemaphoreType.DMA((2,))],
        (GROUP,),
    )


def store_piece(owner, odd, piece_ref, at, values, y):
    rows = values.shape[0] // 8
    for z in range(4):
        for x in range(2):
            plain = owner == (1 if odd else 0)
            first = jnp.where(plain, x, y)
            second = jnp.where(plain, y, x)
            start = (z * 2 + x) * rows
            for j in range(values.shape[1] // 128):
                part = values[start : start + rows, j * 128 : (j + 1) * 128]
                piece_ref[first, second, z, at + j] = part.astype(BF)


def blocks(rows):
    size = min(256, rows)

    def over(body):
        pl.loop(0, rows // size)(lambda i: body(span(i, size), i))

    return over


def feed_forward_first(meta, x, small, mixed, parts):
    rows, width = x.shape
    parts, starts = zip(*parts)
    count = len(parts)

    def kernel(meta, x_ref, small_ref, *refs):
        mixed_refs, parts = refs[: len(mixed)], refs[len(mixed) : len(mixed) + count]
        middle_ref, second_ref, active_ref, slope_ref, whole, sems = refs[len(mixed) + count :]
        for j in range(2):
            fetch(meta, parts, starts, whole, (j * width, width), sems.at[j])

        def row(r):
            return small_ref[r : r + 1, :]

        fetched(whole, (0, width), sems.at[0])

        @blocks(rows)
        def _(here, i):
            values = jnp.concatenate([r[here, :] for r in mixed_refs], axis=1)
            middle = x_ref[here, :].astype(F32) + dot(values, whole[:, :width]) + row(BO)
            middle_ref[here, :] = middle
            normed, _ = normed_rows(middle)
            second = (normed * row(G2) + row(B2)).astype(BF)
            second_ref[here, :] = second

            @pl.when(i == 0)
            def _():
                fetched(whole, (width, width), sems.at[1])

            v = dot(second, whole[:, width:]) + row(BU)
            square = v * v
            half = 0.5 * jnp.tanh(v * (GELU + (GELU * CUBIC) * square)) + 0.5
            active = v * half
            active_ref[here, :] = active.astype(BF)
            slope = (1.0 - half) * active * (2 * GELU + (6 * GELU * CUBIC) * square)
            slope_ref[here, :] = (half + slope).astype(BF)

    return call(
        kernel,
        meta,
        [(x, None), (small, None)] + [(a, None) for a in mixed] + [(p, ANY) for p in parts],
        [
            (VMEM((rows, width), F32), None),
            (VMEM((rows, width), BF), None),
            (VMEM((rows, width), BF), None),
            (VMEM((rows, width), BF), None),
        ],
        24,
        cost(4 * rows * width * width, 2 * 9 * rows * width, rows * width),
        "feed_forward_first",
        [pltpu.VMEM((width, 2 * width), BF), pltpu.SemaphoreType.DMA((2,))],
    )


def store_grads(meta, both, m, left_ref, right_ref, odd):
    half = right_ref.shape[1] // 2

    @pl.loop(0, 2)
    def _(core):
        values = dot(left_ref[...], right_ref[:, span(core, half)]).astype(BF)
        for y in range(2):
            part = values[:, y * half // 2 : (y + 1) * half // 2]
            store_piece(core, odd, both.at[core], 2 * m, part, y)


def send_grads(meta, both, m, pieces, sems):
    tiles = pl.ds(2 * m, 2)
    copies = [
        pltpu.make_async_copy(
            both.at[meta[half], :, :, :, tiles], piece.at[:, :, :, tiles], sems.at[2 * m + i]
        )
        for i, (half, piece) in enumerate(zip((THEIRS, OURS), pieces))
    ]
    for copy in copies:
        copy.start()
    return copies


def feed_forward_second(meta, cot, small, middle, second, active, slope, parts):
    rows, width = cot.shape
    parts, starts = zip(*parts)
    count = len(parts)

    def kernel(meta, cot_ref, small_ref, middle_ref, second_ref, active_ref, slope_ref, *refs):
        parts, refs = refs[:count], refs[count:]
        out_ref, hidden_ref, *pieces, sums_ref, whole, out, flipped, halves, sems = refs
        fetch(meta, parts, starts, whole, (0, width), sems.at[4])
        flipped[...] = active_ref[...].T
        store_grads(meta, halves, 0, flipped, cot_ref, False)
        copies = send_grads(meta, halves, 0, pieces, sems)
        fetched(whole, (0, width), sems.at[4])

        @blocks(width)
        def _(here, _):
            grad = dot(cot_ref[...], whole[here, :], NT)
            hidden_ref[:, here] = (slope_ref[:, here].astype(F32) * grad).astype(BF)

        flipped[...] = second_ref[...].T
        store_grads(meta, halves, 1, flipped, hidden_ref, False)
        copies += send_grads(meta, halves, 1, pieces, sems)

        def write(here):
            return pltpu.make_async_copy(out.at[:, here], out_ref.at[:, here], sems.at[5])

        @blocks(width)
        def _(here, _):
            values = middle_ref[:, here] + dot(active_ref[...], whole[:, here])
            out[:, here] = (values + small_ref[BD : BD + 1, here]).astype(BF)
            write(here).start()

        sums_ref[...] = jnp.zeros_like(sums_ref)
        sums_ref[0:1, :] = column_sum(hidden_ref[...])
        sums_ref[1:2, :] = column_sum(cot_ref[...])
        for copy in (write(pl.ds(0, width)), *copies):
            copy.wait()

    shape = (2, 2, 4, 4, width // 8, 128)
    piece = VMEM(shape, BF)
    return call(
        kernel,
        meta,
        [(a, None) for a in (cot, small, middle, second, active, slope)]
        + [(p, ANY) for p in parts],
        [
            (HBM((rows, width), BF), ANY),
            (VMEM((rows, width), BF), None),
            (piece, ANY),
            (piece, ANY),
            (shaped(F32, 8, width), None),
        ],
        24,
        cost(8 * rows * width * width, 2 * 12 * rows * width),
        "feed_forward_second",
        [
            pltpu.VMEM((width, width), BF),
            pltpu.VMEM((rows, width), BF),
            pltpu.VMEM((width, rows), BF),
            pltpu.VMEM((2, *shape), BF),
            pltpu.SemaphoreType.DMA((6,)),
        ],
    )


def feed_forward_third(meta, cot, small, middle, mixed, hidden, parts):
    rows, width = cot.shape
    parts, starts = zip(*parts)
    count = len(parts)

    def kernel(meta, cot_ref, small_ref, middle_ref, hidden_ref, *refs):
        mixed_refs, parts = refs[: len(mixed)], refs[len(mixed) : len(mixed) + count]
        attn_ref, *pieces, sums_ref, whole, flipped, halves, sem, sems = refs[len(mixed) + count :]
        fetch(meta, parts, starts, whole, (0, width), sem, width)
        fetched(whole, (0, width), sem)
        sums_ref[...] = jnp.zeros_like(sums_ref)

        @blocks(rows)
        def _(here, _):
            grad_second = dot(hidden_ref[here, :], whole[...], NT)
            normed, scale = normed_rows(middle_ref[here, :])
            back = norm_back(grad_second * small_ref[G2 : G2 + 1, :], normed, scale)
            grad_attn = (cot_ref[here, :].astype(F32) + back).astype(BF)
            attn_ref[here, :] = grad_attn
            sums_ref[0:1, :] += column_sum(grad_second * normed)
            sums_ref[1:2, :] += column_sum(grad_second)
            sums_ref[2:3, :] += column_sum(grad_attn)

        for i, ref in enumerate(mixed_refs):
            n = ref.shape[1]
            flipped[i * n : (i + 1) * n, :] = ref[...].T
        store_grads(meta, halves, 0, flipped, attn_ref, True)
        for copy in send_grads(meta, halves, 0, pieces, sems):
            copy.wait()

    shape = (2, 2, 4, 2, width // 8, 128)
    piece = VMEM(shape, BF)
    return call(
        kernel,
        meta,
        [(a, None) for a in (cot, small, middle, hidden, *mixed)] + [(p, ANY) for p in parts],
        [(VMEM((rows, width), BF), None), (piece, ANY), (piece, ANY), (shaped(F32, 8, width), None)],
        20,
        cost(4 * rows * width * width, 2 * 12 * rows * width),
        "feed_forward_third",
        [
            pltpu.VMEM((width, width), BF),
            pltpu.VMEM((width, rows), BF),
            pltpu.VMEM((2, *shape), BF),
            pltpu.SemaphoreType.DMA,
            pltpu.SemaphoreType.DMA((2,)),
        ],
    )


def mixed_grad(meta, grad_attn, parts):
    rows, width = grad_attn.shape
    parts, starts = zip(*parts)
    count = len(parts)

    def kernel(meta, attn_ref, *refs):
        parts, (grad_ref, attn_out, whole, sems) = refs[:count], refs[count:]
        write = pltpu.make_async_copy(attn_ref, attn_out, sems.at[1])
        write.start()
        fetch(meta, parts, starts, whole, (0, width), sems.at[0])
        fetched(whole, (0, width), sems.at[0])

        @blocks(rows)
        def _(here, _):
            grad_ref[here, :] = dot(attn_ref[here, :], whole[...], NT).astype(BF)

        write.wait()

    return call(
        kernel,
        meta,
        [(grad_attn, None)] + [(p, ANY) for p in parts],
        [(VMEM((rows, width), BF), None), (HBM((rows, width), BF), ANY)],
        16,
        cost(2 * rows * width * width, 2 * 4 * rows * width),
        "mixed_grad",
        [pltpu.VMEM((width, width), BF), pltpu.SemaphoreType.DMA((2,))],
    )


def attention_backward(meta, first, packed, probs, grad_mixed, mixed, base, half, images, odd):
    rows, width = first.shape
    length, n = rows // images, 3 * SIZE
    pair = GROUP // 2

    def kernel(
        meta, first_ref, packed_ref, probs_ref, grad_ref, mixed_ref, grad_packed_ref, piece_ref
    ):
        j = pl.program_id(0)
        head = meta[half] * pair + j

        @pl.loop(0, images)
        def _(i):
            here = span(i, length)
            packed = packed_ref[here, :]
            q, k, v = packed[:, :SIZE], packed[:, SIZE : 2 * SIZE], packed[:, 2 * SIZE :]
            grad = grad_ref[here, span(base + head, SIZE)]
            mixed = mixed_ref[here, span(head, SIZE)]
            inner = jnp.sum(grad.astype(F32) * mixed.astype(F32), axis=-1, keepdims=True)
            probs = probs_ref[0, i]
            grad_v = dot(probs, grad, TN)
            grad_scores = (probs.astype(F32) * (dot(grad, v, NT) - inner)).astype(BF)
            grad_q = dot(grad_scores, k) * SCALE
            grad_k = dot(grad_scores, q, TN) * SCALE
            grad_packed_ref[here, :] = jnp.concatenate(
                [grad_q.astype(BF), grad_k.astype(BF), grad_v.astype(BF)], axis=1
            )

        values = dot(first_ref[...], grad_packed_ref[...], TN)
        store_piece(meta[half], odd, piece_ref, 0, values, j)

    return call(
        kernel,
        meta,
        [
            (first, None),
            (hbm(packed), pl.BlockSpec((rows, n), lambda j, m: (0, m[half] * pair + j))),
            (
                hbm(probs),
                pl.BlockSpec(
                    (1, images, length, length), lambda j, m: (m[half] * pair + j, 0, 0, 0)
                ),
            ),
            (grad_mixed, None),
            (mixed, None),
        ],
        [
            (HBM((rows, pair * n), BF), pl.BlockSpec((rows, n), lambda j, m: (0, j))),
            (VMEM((2, 2, 4, 3, width // 8, SIZE), BF), None),
        ],
        20,
        cost(
            pair * (2 * rows * width * n * 1.5 + 10 * rows * length * SIZE * 1.5),
            2 * (rows * width + pair * (rows * length + 3 * rows * n)),
        ),
        "attention_backward",
        grid=(pair,),
    )


def input_grad(meta, x, grad_attn, small, pieces, weights):
    rows, width = x.shape
    tm = min(256, rows)
    groups = len(weights)
    n = pieces[0].shape[1]

    def kernel(meta, x_ref, grad_ref, small_ref, *refs):
        pieces, weights = refs[: 2 * groups], refs[2 * groups : 3 * groups]
        out_ref, sums_ref, packed_sums_ref = refs[3 * groups :]

        @pl.when(pl.program_id(0) == 0)
        def _():
            sums_ref[...] = jnp.zeros_like(sums_ref)
            packed_sums_ref[...] = jnp.zeros_like(packed_sums_ref)

        grad = None
        for g in range(groups):
            for j, which in enumerate((THEIRS, OURS)):
                piece = pieces[2 * g + j][...]
                term = dot(piece, weights[g][:, span(meta[which], n)], NT)
                grad = term if grad is None else grad + term
                packed_sums_ref[0:1, span(2 * g + meta[which], n)] += column_sum(piece)
        normed, scale = normed_rows(x_ref[...].astype(F32))
        back = norm_back(grad * small_ref[G1 : G1 + 1, :], normed, scale)
        out_ref[...] = (grad_ref[...].astype(F32) + back).astype(BF)
        sums_ref[0:1, :] += column_sum(grad * normed)
        sums_ref[1:2, :] += column_sum(grad)

    block = pl.BlockSpec((tm, width), lambda i, m: (i, 0))
    return call(
        kernel,
        meta,
        [(hbm(x), block), (hbm(grad_attn), block), (small, None)]
        + [(hbm(p), pl.BlockSpec((tm, n), lambda i, m: (i, 0))) for p in pieces]
        + [(w, None) for w in weights],
        [
            (HBM((rows, width), BF), block),
            (shaped(F32, 8, width), None),
            (shaped(F32, 8, 3 * width), None),
        ],
        24,
        cost(6 * rows * width * width * 1.3, 2 * 9 * rows * width),
        "input_grad",
        grid=(rows // tm,),
    )


def quarter_of(meta, i):
    return (meta[CORE] ^ (i % 2)) * 2 + (meta[YPOS] ^ (i // 2))


def finish(meta, groups, places, widths, name):
    quarters = [q for group in groups for q in group]
    rows = quarters[0].shape[1]

    def kernel(meta, *refs):
        outs = refs[len(quarters) :]
        for g, place in enumerate(places):
            for i in range(4):
                part = refs[4 * g + i]
                for j in range(min(part.shape[0], len(widths) * widths[0] // 128 // 4 // len(groups))):
                    which, column = place(quarter_of(meta, i), j)
                    outs[which][:, span(column, 128)] = part[j].astype(F32)

    outs = [(shaped(F32, rows, n), None) for n in widths]
    return call(kernel, meta, [(a, None) for a in quarters], outs, 8, cost(1, 1), name)


def by_head(weight, base):
    rows = weight.shape[0]
    view = weight.reshape(rows, 3, HEADS, SIZE)[:, :, base : base + GROUP]
    return view.transpose(0, 2, 1, 3).reshape(rows, GROUP * 3 * SIZE)


def per_device(latents, w_qkv, w_out, w_up, w_down, gains, biases, ff_bias, cotangent, *, nb, nr):
    reps, images, length, width = latents.shape
    x = latents.reshape(-1, width)
    cot = cotangent.reshape(-1, width)
    count = reps * images
    bases = range(0, HEADS, GROUP)
    native = nb != 8 or nr != 4
    small = jnp.concatenate([gains, biases, ff_bias[None]], axis=0)
    small = jnp.pad(small, ((0, 16 - small.shape[0]), (0, 0)))
    if native:
        links = None
        zero = jnp.zeros((), jnp.int32)
        meta = jnp.stack([zero, zero, zero, zero, zero + 1, zero, zero, zero])

        def whole(w):
            return [(lax.all_gather(w, "batch", axis=0, tiled=True), 0)]

        table = lax.all_gather(small, "batch", axis=1, tiled=True)
        table = table.reshape(16, 4, 2, width // 8).transpose(2, 1, 0, 3)
        first, small = first_norm(meta, x, [table[0], table[1], table[1]])
        chunks = [whole(by_head(w_qkv, base)) for base in bases]
        chunks += [whole(jnp.concatenate([w_out, w_up], axis=1)), whole(w_down)]
    else:
        links = Links(nb, nr)
        mine_f = jnp.where(links.ci == 0, links.xi, links.yi)
        mine_s = jnp.where(links.ci == 0, links.yi, links.xi)
        meta = [links.ci, links.yi, links.xi, links.zi, 1 - links.ci, links.ci, mine_f, mine_s]
        meta = jnp.stack(meta).astype(jnp.int32)

        def quarter(w):
            rows = w.shape[0] // 4
            return lax.dynamic_slice_in_dim(w, (links.ci * 2 + links.yi) * rows, rows, 0)

        w_qkv = quarter(w_qkv)
        chunks = [by_head(w_qkv, base) for base in bases]
        extra = jnp.pad(small, ((0, w_qkv.shape[0] - 16), (0, 0)))
        chunks[0] = jnp.concatenate([chunks[0], extra], axis=1)
        chunks += [jnp.concatenate([quarter(w_out), quarter(w_up)], axis=1), quarter(w_down)]
        other = CoreSwap(links)

        def visit(i, chunks):
            if i == 0:
                return ()
            if i == 1:
                kept.extend(first_norm(meta, x, [part for part, _ in chunks[0][:3]]))
                return kept + other.early(chunks[0], 3)
            gates = other.early(chunks[i - 1], 2) + forward(i - 2, chunks[i - 2])
            return gates + other.early(chunks[i], 2, *mixed) if i == 3 else gates

    packed, probs, mixed, weights, kept = [], [], [], [], []

    def forward(i, parts):
        parts = parts if native else other(parts, *mixed)
        a, b, c, d = attention_forward(meta, kept[0], kept[1], parts, bases[i], count)
        packed.append(a)
        probs.append(b)
        mixed.append(c)
        weights.append(d)
        return [c]

    if native:
        kept.extend((first, small))
        for i in range(len(bases)):
            forward(i, chunks[i])
    else:
        chunks = gather_chunks(chunks, links, visit)
        for i in range(len(mixed), len(bases)):
            forward(i, chunks[i])
        first, small = kept
    outer, inner = chunks[len(bases) :]
    outer = outer if native else other(outer, mixed[1])
    middle, second, active, slope = feed_forward_first(meta, x, small, mixed, outer)
    inner = inner if native else other(inner, active)
    out, hidden, send, keep, sums_two = feed_forward_second(
        meta, cot, small, middle, second, active, slope, inner
    )
    grad_attn, send_out, keep_out, sums_three = feed_forward_third(
        meta, cot, small, middle, mixed, hidden, outer
    )

    def backward(meta, g, half):
        return attention_backward(
            meta, first, packed[g], probs[g], grad_mixed, mixed[g], bases[g], half, count, g == 1
        )

    def collect(sums_one, sums_packed):
        sums_packed = sums_packed[0].reshape(HEADS, 3, SIZE)
        sums_q, sums_v = sums_packed[:, 0].reshape(width), sums_packed[:, 2].reshape(width)
        out, two, three = sums_three[2], sums_two, sums_three
        rows = [sums_one[0], three[0], sums_one[1], sums_q, sums_v, out, three[1], two[1], two[0]]
        return jnp.stack(rows)

    def sums_of(sums_one, sums_packed):
        two, three, one, packed = sums_two, sums_three, sums_one, sums_packed
        plain = [(one, 0), (three, 0), (one, 1), None, None, (three, 2), (three, 1), (two, 1), (two, 0)]
        sums = [entry and (*entry, 1, 0) for entry in plain]
        sums[3], sums[4] = (packed, 0, 3, 0), (packed, 0, 3, 2)
        return sums

    def result(grad_x, grads, smalls):
        return (
            out.reshape(latents.shape),
            grad_x.reshape(latents.shape),
            *grads,
            smalls[:2],
            smalls[2:8],
            smalls[8],
        )

    if native:
        grad_mixed, grad_attn = mixed_grad(meta, grad_attn, outer)
        halves = [[backward(meta, g, half) for half in (THEIRS, OURS)] for g in range(len(bases))]
        pieces = [half[0] for pair in halves for half in pair]
        grad_x, sums_one, sums_packed = input_grad(meta, x, grad_attn, small, pieces, weights)
        smalls = lax.psum_scatter(
            collect(sums_one, sums_packed), "batch", scatter_dimension=1, tiled=True
        )
        smalls = lax.psum(smalls, "rep")

        def reduced(send, keep, odd):
            keep, send = (jnp.swapaxes(keep, 0, 1), send) if odd else (keep, jnp.swapaxes(send, 0, 1))
            both = jnp.stack([keep, send])
            t = both.shape[4]
            both = both.transpose(3, 1, 5, 0, 2, 4, 6).reshape(width, t * 4 * 128)
            both = lax.psum_scatter(both, "batch", scatter_dimension=0, tiled=True)
            both = lax.psum(both.astype(BF), "rep").astype(F32)
            return both.reshape(-1, 4, t, 128)

        rest = [reduced(send_out, keep_out, True), reduced(send, keep, False)]
        rows = rest[0].shape[0]
        rest = [rest[0], rest[1][:, :, 2:], rest[1][:, :, :2]]
        rest = [g.reshape(rows, width) for g in rest]
        heads = [reduced(pair[0][1], pair[1][1], g == 1) for g, pair in enumerate(halves)]
        heads = jnp.concatenate(heads, axis=1).transpose(0, 2, 1, 3).reshape(rows, 3 * width)
        return result(grad_x, [heads, *rest], smalls)

    def to_core(value):
        return move(value, links.core)

    def along(arrays):
        return [arrays[0]] + [move(a, p) for a, p in zip(arrays[1:], links.z)]

    def share(value, *gates):
        by_y = move(value, links.y)
        own, theirs = (move(after(v, *gates), links.core) for v in (value, by_y))
        return [value, own, by_y, theirs]

    both = Piece(keep, to_core(send), False)
    step = Step()
    step.swap(firsts=[both])
    (sent,) = step.run(after(meta, keep_out), "step_0")
    both.late.append((move(sent, links.x_or_y), 0))
    grad_mixed, grad_attn = mixed_grad(after(meta, sent), grad_attn, outer)
    packed_1, send_1 = backward(after(meta, sent), 0, THEIRS)

    outs = Piece(keep_out, to_core(send_out), True)
    step = Step()
    step.swap(firsts=[outs], seconds=[both])
    (sent,) = step.run(after(meta, send_1), "step_1")
    moved = move(sent, links.y_or_x)
    for piece in (outs, both):
        piece.late.append((moved, piece.next))
    packed_2, keep_1 = backward(after(meta, sent), 0, OURS)
    packed_3, send_2 = backward(after(meta, sent, keep_1), 1, THEIRS)

    one = Piece(keep_1, to_core(send_1), False)
    step = Step()
    step.swap(firsts=[one], seconds=[outs])
    step.along(both)
    sent, *z_both = step.run(after(meta, send_2), "step_2")
    moved = move(sent, links.x_or_y)
    for piece in (one, outs):
        piece.late.append((moved, piece.next))
    z_both = along(z_both)
    packed_4, keep_2 = backward(after(meta, sent), 1, OURS)

    two = Piece(keep_2, to_core(send_2), True)
    step = Step()
    step.swap(firsts=[two], seconds=[one])
    step.along(outs)
    sent, *z_outs = step.run(after(meta, keep_2, *z_both[1:]), "step_3")
    moved = move(sent, links.y_or_x)
    for piece in (two, one):
        piece.late.append((moved, piece.next))
    z_outs = along(z_outs)
    pieces = [packed_1, packed_2, packed_3, packed_4]
    grad_x, sums_one, sums_packed = input_grad(
        after(meta, sent), x, grad_attn, small, pieces, weights
    )

    step = Step()
    step.along(one, sums_of(sums_one, sums_packed))
    z_one = step.run(after(meta, grad_x, *z_outs[1:]), "step_4")
    step = Step()
    step.swap(seconds=[two])
    (sent,) = step.run(after(meta, z_one[0]), "step_5")
    two.late.append((move(sent, links.x_or_y), 0))
    step = Step()
    step.share([z_both, z_outs])
    (r_rest,) = step.run(after(meta, sent), "step_6")
    z_one = along(z_one)
    r_rest = share(after(r_rest, z_one[1]))

    step = Step()
    step.along(two)
    z_two = step.run(after(meta, z_one[1]), "step_7")
    step = Step()
    step.share([z_one])
    (r_one,) = step.run(after(meta, z_two[0]), "step_8")
    z_two = along(z_two)

    step = Step()
    step.share([z_two])
    (r_two,) = step.run(meta, "step_9")
    r_one = share(r_one, r_two)
    step = Step()
    step.small(r_one)
    other, smalls = step.run(after(meta, r_two), "step_10")
    rest = finish(
        after(meta, other),
        [r_rest],
        [lambda q, j: (2 - j // 2, q * 2 + j % 2)],
        [width] * 3,
        "finish_rest",
    )
    r_two = share(r_two, rest[0])
    smalls = smalls + move(other, links.x)
    (heads,) = finish(
        meta,
        [r_one, r_two],
        [lambda q, j: (0, j * HEADS + q), lambda q, j: (0, j * HEADS + GROUP + q)],
        [3 * width],
        "finish_heads",
    )
    return result(grad_x, [heads, *rest], smalls)


def solution(mesh):
    nb, nr = mesh.shape["batch"], mesh.shape["rep"]

    def body(*args):
        return per_device(*args, nb=nb, nr=nr)

    rows = P("batch", None)
    cols = P(None, "batch")
    data = P("rep", "batch", None, None)
    return jax.shard_map(
        body,
        mesh=mesh,
        in_specs=(data, rows, rows, rows, rows, cols, cols, P("batch"), data),
        out_specs=(data, data, rows, rows, rows, rows, cols, cols, P("batch")),
        check_vma=False,
    )
```
